128 devices in a mesh: sta: 16 (over x, y_hi, core), freq: 8 (over y_lo, z).
Axes of the slice: x: 4, y: 4 (y_hi: 2, y_lo: 2; y = y_hi * 2 + y_lo), z: 4, core: 2. Of those that a mesh axis runs over, the one named last changes fastest.
Arguments:
- records: bfloat16 [2048, 256, 512], P('sta', 'freq'), may hold values from -6 to 6
- available: int32 [2048, 256], P('sta', 'freq'), may hold values 0 or 1
Outputs:
- cross_gram: bfloat16 [2, 128, 2048, 2048], P(None, 'freq', 'sta')
The draws below stay inside these ranges and needn't reach their ends.
All inputs are finite; a program needn't handle non-finite values. No bound on the sum of `available` on one device may be relied on, other than what follows from the above.
Results may differ from the reference program's by a relative error of at most 0.0056.
Values may be sent and summed in bfloat16 or wider, within the bound.
No kernel may reach another device: no remote copies, remote signals or barrier semaphores. Data moves between devices by JAX's collectives and lax.ppermute only.
A program may use at most 192 MiB of HBM per device.

```python
import jax
import jax.numpy as jnp
from jax import lax

FFT_LEN = 512
BINS = 128
BAND_LO = 16
STATIONS = 2048
SEGS = 256


def plant(array, stream_key, smallest, high):
    longest = array.shape.index(max(array.shape))
    spots = []
    for shift in (0, 1):
        where = [jax.random.randint(jax.random.fold_in(stream_key, axis), (), 0, length) for axis, length in enumerate(array.shape)]
        where[longest] = (where[longest] + shift) % array.shape[longest]
        spots.append(tuple(where))
    return array.at[spots[0]].set(smallest).at[spots[1]].set(high)


def shard_levels(key, dims, cuts, smallest, largest):
    factor_of, own = 1.0, jax.random.fold_in(key, 6)
    for axis_at, blocks in cuts:
        steps = jnp.exp(jax.random.uniform(jax.random.fold_in(own, axis_at), (blocks,), jnp.float32, smallest / len(cuts), largest / len(cuts)))
        factor_of = factor_of * jnp.repeat(steps, dims[axis_at] // blocks).reshape([-1 if axis == axis_at else 1 for axis in range(len(dims))])
    return factor_of


def centred(key, extent, spread, bound, split=(), held_as=jnp.bfloat16):
    entries = jax.random.normal(key, extent, jnp.float32) * spread
    if len(split) > 0:
        entries = shard_levels(key, extent, split, -0.22, 0.18) * entries
    return jnp.clip(entries, min=-bound, max=bound).astype(held_as)


def setup_inputs(seed: int = 0) -> dict:
    streams_of = jax.random.split(jax.random.key(seed), 3)
    return {
        "records": centred(streams_of[0], (STATIONS, SEGS, FFT_LEN), 1.0, 6.0, ((0, 16), (1, 8))),
        "available": plant((jax.random.randint(streams_of[1], (STATIONS, SEGS), 0, 4) < 3).astype(jnp.int32), jax.random.fold_in(streams_of[1], 1), 0, 1),
    }


def whiten(records, available):
    sample_pos = jnp.arange(FFT_LEN, dtype=jnp.float32)
    window_taper = 0.5 - 0.5 * jnp.cos(2.0 * jnp.pi * sample_pos / FFT_LEN)
    tapered = records.astype(jnp.float32) * window_taper
    spectrum = jnp.fft.rfft(tapered, axis=-1)[..., BAND_LO:BAND_LO + BINS]
    real_part = jnp.real(spectrum)
    imag_part = jnp.imag(spectrum)
    power = lax.optimization_barrier(jnp.mean(real_part * real_part + imag_part * imag_part, axis=-1, keepdims=True))
    weight = available.astype(jnp.float32)[..., None] / jnp.sqrt(power + 1e-05)
    return ((real_part * weight).astype(jnp.bfloat16), (imag_part * weight).astype(jnp.bfloat16))

def reference(records, available):
    real_white, imag_white = whiten(records, available)
    real_bins = jnp.transpose(real_white, (2, 0, 1))
    imag_bins = jnp.transpose(imag_white, (2, 0, 1))
    highest = lax.Precision.HIGHEST

    def one_bin(pair):
        real_rows = pair[0].astype(jnp.float32)
        imag_rows = pair[1].astype(jnp.float32)
        both_real = jnp.dot(real_rows, real_rows.T, precision=highest, preferred_element_type=jnp.float32)
        both_imag = jnp.dot(imag_rows, imag_rows.T, precision=highest, preferred_element_type=jnp.float32)
        imag_real = jnp.dot(imag_rows, real_rows.T, precision=highest, preferred_element_type=jnp.float32)
        real_imag = jnp.dot(real_rows, imag_rows.T, precision=highest, preferred_element_type=jnp.float32)
        gram_real = ((both_real + both_imag) / SEGS).astype(jnp.bfloat16)
        gram_imag = ((imag_real - real_imag) / SEGS).astype(jnp.bfloat16)
        return (gram_real, gram_imag)
    gram_real, gram_imag = lax.map(one_bin, (real_bins, imag_bins))
    return jnp.stack([gram_real, gram_imag])
```

```python
import functools

import jax
import jax.numpy as jnp
import numpy as np
from jax import lax
from jax.experimental import pallas as pl
from jax.experimental.pallas import tpu as pltpu
from jax.sharding import Mesh, PartitionSpec as P

FFT_LEN = 512
BINS = 128
BAND_LO = 16
SUBS = 2


def spectra_table():
    sample = np.arange(FFT_LEN)
    phase = (sample[:, None] * (BAND_LO + np.arange(BINS))[None, :] % FFT_LEN) * (2.0 * np.pi / FFT_LEN)
    taper = 0.5 - 0.5 * np.cos(2.0 * np.pi * sample / FFT_LEN)
    table = np.concatenate([np.cos(phase), -np.sin(phase)], axis=1) * taper[:, None]
    high = table.astype(jnp.bfloat16)
    low = (table - high.astype(np.float64)).astype(jnp.bfloat16)
    return np.concatenate([high, low], axis=1)


def gram_kernel(scale, where, mine_ref, own_ref, other_ref, *outs):
    out_ref = outs[-1]
    panel = jnp.concatenate([own_ref[0], other_ref[0]], axis=1)
    gram = jnp.dot(mine_ref[0], panel, preferred_element_type=jnp.float32) * scale
    gram = gram.astype(jnp.bfloat16)
    rows = gram.shape[0] // 2
    cols = gram.shape[1] // 2
    own = pl.ds(pl.multiple_of(where[1] * cols, cols), cols)
    other = pl.ds(pl.multiple_of((1 - where[1]) * cols, cols), cols)
    out_ref[0, 0, :, own] = gram[:rows, :cols]
    out_ref[1, 0, :, own] = gram[rows:, :cols]
    out_ref[0, 0, :, other] = gram[:rows, cols:]
    out_ref[1, 0, :, other] = gram[rows:, cols:]


def gram(first, chip, core, mine, own, other, shape, out):
    bins, depth, cols = own.shape
    rows = mine.shape[1] // 2
    where = jnp.stack([chip, core]).astype(jnp.int32)
    held = [] if out is None else [out]
    return pl.pallas_call(
        functools.partial(gram_kernel, 2.0 / depth),
        grid_spec=pltpu.PrefetchScalarGridSpec(
            num_scalar_prefetch=1,
            grid=(bins,),
            in_specs=[
                pl.BlockSpec((1, 2 * rows, depth), lambda f, w: (first + f, 0, 0)),
                pl.BlockSpec((1, depth, cols), lambda f, w: (f, 0, 0)),
                pl.BlockSpec((1, depth, cols), lambda f, w: (f, 0, 0)),
            ] + [pl.BlockSpec(memory_space=pl.ANY)] * len(held),
            out_specs=pl.BlockSpec((2, 1, rows, 2 * cols), lambda f, w: (0, first + f, 0, w[0])),
        ),
        out_shape=jax.ShapeDtypeStruct(shape, jnp.bfloat16),
        input_output_aliases={4: 0} if held else {},
        cost_estimate=pl.CostEstimate(
            flops=8 * bins * rows * depth * cols,
            bytes_accessed=2 * bins * (2 * rows * depth + 2 * depth * cols + 4 * rows * cols),
            transcendentals=0,
        ),
        name="gram",
    )(where, mine, own, other, *held)


def ring(size, step):
    return [(i, (i + step) % size) for i in range(size)]


def shards(records, available):
    stations, segments, samples = records.shape
    x, yh, core = lax.axis_index("x"), lax.axis_index("yh"), lax.axis_index("core")
    spectra = jnp.dot(
        records.reshape(stations * segments, samples),
        jnp.asarray(spectra_table()),
        preferred_element_type=jnp.float32,
    )
    spectra = spectra[:, : 2 * BINS] + spectra[:, 2 * BINS :]
    spectra = spectra.reshape(stations, segments, 2 * BINS)
    power = jnp.sum(spectra * spectra, axis=-1, keepdims=True) / BINS
    weight = available.astype(jnp.float32)[..., None] / jnp.sqrt(power + 1e-05)
    whitened = (spectra * weight).astype(jnp.bfloat16).reshape(stations, segments, 2, BINS)
    whitened = jnp.transpose(whitened, (3, 2, 1, 0))
    panel = lax.all_to_all(whitened, ("yl", "z"), split_axis=0, concat_axis=2, tiled=True)
    bins, _, depth, _ = panel.shape
    turned = jnp.transpose(panel, (0, 1, 3, 2))
    real, imag = turned[:, 0], turned[:, 1]
    mine = jnp.concatenate(
        [jnp.concatenate([real, imag], axis=2), jnp.concatenate([imag, -real], axis=2)], axis=1
    )
    panel = panel.reshape(bins, 2 * depth, stations)

    out, shape = None, (2, bins, stations, 16 * stations)
    sub = bins // SUBS
    blocks = []
    for part in range(SUBS):
        step = 1 if part % 2 == 0 else -1
        along = lambda v, s: lax.ppermute(v, "x", ring(4, s))
        across = lambda v: lax.ppermute(v, "yh", ring(2, 1))
        own = panel[part * sub : (part + 1) * sub]
        near = along(own, step)
        back = along(own, -step)
        over = across(own)
        far = along(near, step)
        near_over = across(near)
        back_over = along(over, -step)
        far_over = along(near_over, step)
        got = [
            (0, 0, own), (step, 0, near), (-step, 0, back), (0, 1, over),
            (2 * step, 0, far), (step, 1, near_over), (-step, 1, back_over), (2 * step, 1, far_over),
        ]
        blocks.append([(dx, dy, v, lax.ppermute(v, "core", ring(2, 1))) for dx, dy, v in got])
    for group in zip(*blocks):
        for part, (dx, dy, own, other) in enumerate(group):
            chip = (x - dx) % 4 * 2 + (yh + dy) % 2
            out = gram(part * sub, chip, core, mine, own, other, shape, out)
    return out


def solution(mesh):
    fine = Mesh(mesh.devices.reshape(4, 2, 2, 2, 4), ("x", "yh", "core", "yl", "z"))
    sta, freq = ("x", "yh", "core"), ("yl", "z")
    return jax.shard_map(
        shards,
        mesh=fine,
        in_specs=(P(sta, freq, None), P(sta, freq)),
        out_specs=P(None, freq, sta, None),
        check_vma=False,
    )
```

```python
import functools

import jax
import jax.numpy as jnp
import numpy as np
from jax import lax
from jax.experimental import pallas as pl
from jax.experimental.pallas import tpu as pltpu
from jax.sharding import Mesh, PartitionSpec as P

FFT_LEN = 512
BINS = 128
BAND_LO = 16
OWNERS = 8
HALF = 8
SEG_STEP = 8
MIB = 1024 * 1024


def spectra_table():
    sample = np.arange(FFT_LEN)
    bins = (BAND_LO + np.arange(BINS)).reshape(OWNERS, 2, HALF).transpose(1, 0, 2).reshape(-1)
    phase = (sample[:, None] * bins[None, :] % FFT_LEN) * (2.0 * np.pi / FFT_LEN)
    taper = 0.5 - 0.5 * np.cos(2.0 * np.pi * sample / FFT_LEN)
    table = np.stack([np.cos(phase), -np.sin(phase)], axis=2).reshape(FFT_LEN, 2 * BINS) * taper[:, None]
    high = table.astype(jnp.bfloat16)
    low = (table - high.astype(np.float64)).astype(jnp.bfloat16)
    return high, low


def whiten_kernel(records_ref, available_ref, high_ref, low_ref, first_ref, second_ref, rows_ref, turned_ref):
    stations, segs, samples = records_ref.shape
    flat = records_ref[...].reshape(stations * segs, samples)
    spectra = jnp.dot(flat, high_ref[...], preferred_element_type=jnp.float32)
    spectra += jnp.dot(flat, low_ref[...], preferred_element_type=jnp.float32)
    wide = spectra.shape[1]
    for part in range(2):
        rows_ref[part] = spectra[:, part * BINS : (part + 1) * BINS]
    for seg in range(segs):
        turned = jnp.concatenate(
            [rows_ref[part, pl.ds(seg, stations, stride=segs), :].T for part in range(2)], axis=0
        )
        power = jnp.sum(turned * turned, axis=0, keepdims=True) / BINS
        weight = available_ref[seg : seg + 1, :].astype(jnp.float32) / jnp.sqrt(power + 1e-05)
        turned_ref[pl.ds(seg, wide, stride=segs), :] = turned * weight
    whitened = turned_ref[...].reshape(2, OWNERS, HALF, 2, segs, stations).astype(jnp.bfloat16)
    first_ref[...] = whitened[0]
    second_ref[...] = whitened[1]


def whiten(records, available):
    stations, segments, samples = records.shape
    high, low = spectra_table()
    half = jax.ShapeDtypeStruct((OWNERS, HALF, 2, segments, stations), jnp.bfloat16)
    half_spec = pl.BlockSpec((OWNERS, HALF, 2, SEG_STEP, stations), lambda i: (0, 0, 0, i, 0))
    return pl.pallas_call(
        whiten_kernel,
        grid=(segments // SEG_STEP,),
        in_specs=[
            pl.BlockSpec((stations, SEG_STEP, samples), lambda i: (0, i, 0)),
            pl.BlockSpec((SEG_STEP, stations), lambda i: (i, 0)),
            pl.BlockSpec((samples, 2 * BINS), lambda i: (0, 0)),
            pl.BlockSpec((samples, 2 * BINS), lambda i: (0, 0)),
        ],
        out_specs=[half_spec, half_spec],
        out_shape=[half, half],
        scratch_shapes=[
            pltpu.VMEM((2, stations * SEG_STEP, BINS), jnp.float32),
            pltpu.VMEM((2 * BINS * SEG_STEP, stations), jnp.float32),
        ],
        compiler_params=pltpu.CompilerParams(vmem_limit_bytes=32 * MIB),
        name="whiten",
    )(records, available.T, jnp.asarray(high), jnp.asarray(low))


def rows_kernel(panel_ref, mine_ref):
    bins, depth, rows = panel_ref.shape
    half = depth // 2
    for f in range(bins):
        real = panel_ref[f, :half, :].T
        imag = panel_ref[f, half:, :].T
        mine_ref[f, :rows, :half] = real
        mine_ref[f, :rows, half:] = imag
        mine_ref[f, rows:, :half] = imag
        mine_ref[f, rows:, half:] = -real


def rows_of(panel):
    bins, depth, rows = panel.shape
    step = 2
    return pl.pallas_call(
        rows_kernel,
        grid=(bins // step,),
        in_specs=[pl.BlockSpec((step, depth, rows), lambda f: (f, 0, 0))],
        out_specs=pl.BlockSpec((step, 2 * rows, depth), lambda f: (f, 0, 0)),
        out_shape=jax.ShapeDtypeStruct((bins, 2 * rows, depth), panel.dtype),
        compiler_params=pltpu.CompilerParams(vmem_limit_bytes=16 * MIB),
        name="rows",
    )(panel)


def gram_kernel(scale, first, count, where, mine_ref, *refs):
    panels, (out_ref, slots, sems) = refs[: 2 * count], refs[-3:]
    step, steps = pl.program_id(0), pl.num_programs(0)
    bins = mine_ref.shape[0]
    rows, cols = mine_ref.shape[1] // 2, panels[0].shape[2]
    slot = lax.rem(step, 2)

    def write(at, block, held):
        spot = pl.ds(pl.multiple_of(where[block] * 2 * cols, 2 * cols), 2 * cols)
        return pltpu.make_async_copy(
            slots.at[held, block],
            out_ref.at[:, pl.ds(first + at * bins, bins), :, spot],
            sems.at[held, block],
        )

    @pl.when(step >= 2)
    def _():
        for block in range(count):
            write(step - 2, block, slot).wait()

    own = pl.ds(pl.multiple_of(where[count] * cols, cols), cols)
    other = pl.ds(pl.multiple_of((1 - where[count]) * cols, cols), cols)
    for block in range(count):
        for f in range(bins):
            panel = jnp.concatenate([panels[2 * block][f], panels[2 * block + 1][f]], axis=1)
            gram = jnp.dot(mine_ref[f], panel, preferred_element_type=jnp.float32) * scale
            gram = gram.astype(jnp.bfloat16)
            slots[slot, block, 0, f, :, own] = gram[:rows, :cols]
            slots[slot, block, 1, f, :, own] = gram[rows:, :cols]
            slots[slot, block, 0, f, :, other] = gram[:rows, cols:]
            slots[slot, block, 1, f, :, other] = gram[rows:, cols:]
        write(step, block, slot).start()

    @pl.when(step == steps - 1)
    def _():
        for block in range(count):
            write(step - 1, block, 1 - slot).wait()
            write(step, block, slot).wait()


def gram(first, core, mine, blocks, shape, out):
    bins, depth, cols = blocks[0][1].shape
    rows = mine.shape[1] // 2
    count, step = len(blocks), 2
    where = jnp.stack([chip for chip, _, _ in blocks] + [core]).astype(jnp.int32)
    held = [] if out is None else [out]
    panels = [v for _, own, other in blocks for v in (own, other)]
    return pl.pallas_call(
        functools.partial(gram_kernel, 2.0 / depth, first, count),
        grid_spec=pltpu.PrefetchScalarGridSpec(
            num_scalar_prefetch=1,
            grid=(bins // step,),
            in_specs=[pl.BlockSpec((step, 2 * rows, depth), lambda f, w: (f, 0, 0))]
            + [pl.BlockSpec((step, depth, cols), lambda f, w: (f, 0, 0))] * (2 * count)
            + [pl.BlockSpec(memory_space=pl.ANY)] * len(held),
            out_specs=pl.BlockSpec(memory_space=pl.ANY),
            scratch_shapes=[
                pltpu.VMEM((2, count, 2, step, rows, 2 * cols), jnp.bfloat16),
                pltpu.SemaphoreType.DMA((2, count)),
            ],
        ),
        out_shape=jax.ShapeDtypeStruct(shape, jnp.bfloat16),
        input_output_aliases={2 + 2 * count: 0} if held else {},
        cost_estimate=pl.CostEstimate(
            flops=16 * count * bins * rows * depth * cols,
            bytes_accessed=2 * bins * (2 * rows * depth + count * (2 * depth * cols + 4 * rows * cols)),
            transcendentals=0,
        ),
        compiler_params=pltpu.CompilerParams(vmem_limit_bytes=16 * MIB),
        name="gram",
    )(where, mine, *panels, *held)


def after(value, *others):
    return lax.optimization_barrier((value, *others))[0]


def ring(size, step):
    return [(i, (i + step) % size) for i in range(size)]


def shards(records, available):
    stations = records.shape[0]
    x, yh, core = lax.axis_index("x"), lax.axis_index("yh"), lax.axis_index("core")
    right = lambda v: lax.ppermute(v, "x", ring(4, 1))
    left = lambda v: lax.ppermute(v, "x", ring(4, -1))
    over = lambda v: lax.ppermute(v, "yh", ring(2, 1))
    swap = lambda v: lax.ppermute(v, "core", ring(2, 1))

    def owned(half):
        got = lax.all_to_all(half, ("yl", "z"), split_axis=0, concat_axis=0, tiled=True)
        got = jnp.transpose(got, (1, 2, 0, 3, 4))
        return got.reshape(HALF, -1, stations)

    def entry(dx, dy, own):
        chip = (x - dx) % 4 * 2 + (yh + dy) % 2
        return chip, own, swap(own)

    first, second = whiten(records, available)
    shape = (2, 2 * HALF, stations, 16 * stations)
    p0 = owned(first)
    a0, b0, c0 = right(p0), left(p0), over(p0)
    m0 = rows_of(p0)
    p1 = owned(after(second, p0))
    e_p0 = entry(0, 0, p0)
    b1, a1, c1 = right(after(p1, a0)), left(after(p1, b0)), over(after(p1, c0))
    m1 = rows_of(p1)
    e_p1 = entry(0, 0, p1)
    out = gram(0, core, m0, [e_p0], shape, None)
    out = gram(HALF, core, m1, [e_p1], shape, out)
    e0 = [entry(1, 0, a0), entry(-1, 0, b0), entry(0, 1, c0)]
    d0, g0, f0 = right(after(a0, b1)), left(after(c0, a1)), over(after(a0, c1))
    out = gram(0, core, m0, e0, shape, out)
    e1 = [entry(-1, 0, a1), entry(1, 0, b1), entry(0, 1, c1)]
    g1, d1, f1 = right(after(c1, d0, out)), left(after(a1, g0, out)), over(after(a1, f0, out))
    out = gram(HALF, core, m1, e1, shape, out)
    e0 = [entry(2, 0, d0), entry(-1, 1, g0), entry(1, 1, f0)]
    h0, h1 = right(after(f0, g1, out)), left(after(f1, d1, out))
    out = gram(0, core, m0, e0, shape, out)
    e1 = [entry(-2, 0, d1), entry(1, 1, g1), entry(-1, 1, f1)]
    out = gram(HALF, core, m1, e1, shape, out)
    out = gram(0, core, m0, [entry(2, 1, after(h0, out))], shape, out)
    out = gram(HALF, core, m1, [entry(-2, 1, h1)], shape, out)
    return out


def solution(mesh):
    fine = Mesh(mesh.devices.reshape(4, 2, 2, 2, 4), ("x", "yh", "core", "yl", "z"))
    sta, freq = ("x", "yh", "core"), ("yl", "z")
    return jax.shard_map(
        shards,
        mesh=fine,
        in_specs=(P(sta, freq, None), P(sta, freq)),
        out_specs=P(None, freq, sta, None),
        check_vma=False,
    )
```

```python
import functools

import jax
import jax.numpy as jnp
import numpy as np
from jax import lax
from jax.experimental import pallas as pl
from jax.experimental.pallas import tpu as pltpu
from jax.sharding import Mesh, PartitionSpec as P

FFT_LEN = 512
BINS = 128
BAND_LO = 16
OWNERS = 8
HALF = 8
SEG_STEP = 8
MIB = 1024 * 1024


def spectra_table():
    sample = np.arange(FFT_LEN)
    bins = (BAND_LO + np.arange(BINS)).reshape(OWNERS, 2, HALF).transpose(1, 0, 2).reshape(-1)
    phase = (sample[:, None] * bins[None, :] % FFT_LEN) * (2.0 * np.pi / FFT_LEN)
    taper = 0.5 - 0.5 * np.cos(2.0 * np.pi * sample / FFT_LEN)
    table = np.stack([np.cos(phase), -np.sin(phase)], axis=2).reshape(FFT_LEN, 2 * BINS) * taper[:, None]
    high = table.astype(jnp.bfloat16)
    low = (table - high.astype(np.float64)).astype(jnp.bfloat16)
    return high, low


def whiten_kernel(records_ref, available_ref, high_ref, low_ref, first_ref, second_ref, rows_ref, turned_ref):
    stations, segs, samples = records_ref.shape
    flat = records_ref[...].reshape(stations * segs, samples)
    spectra = jnp.dot(flat, high_ref[...], preferred_element_type=jnp.float32)
    spectra += jnp.dot(flat, low_ref[...], preferred_element_type=jnp.float32)
    wide = spectra.shape[1]
    for part in range(2):
        rows_ref[part] = spectra[:, part * BINS : (part + 1) * BINS]
    for seg in range(segs):
        turned = jnp.concatenate(
            [rows_ref[part, pl.ds(seg, stations, stride=segs), :].T for part in range(2)], axis=0
        )
        power = jnp.sum(turned * turned, axis=0, keepdims=True) / BINS
        weight = available_ref[seg : seg + 1, :].astype(jnp.float32) / jnp.sqrt(power + 1e-05)
        turned_ref[pl.ds(seg, wide, stride=segs), :] = turned * weight
    whitened = turned_ref[...].reshape(2, OWNERS, HALF, 2, segs, stations).astype(jnp.bfloat16)
    first_ref[...] = whitened[0]
    second_ref[...] = whitened[1]


def whiten(records, available):
    stations, segments, samples = records.shape
    high, low = spectra_table()
    half = jax.ShapeDtypeStruct((OWNERS, HALF, 2, segments, stations), jnp.bfloat16)
    half_spec = pl.BlockSpec((OWNERS, HALF, 2, SEG_STEP, stations), lambda i: (0, 0, 0, i, 0))
    return pl.pallas_call(
        whiten_kernel,
        grid=(segments // SEG_STEP,),
        in_specs=[
            pl.BlockSpec((stations, SEG_STEP, samples), lambda i: (0, i, 0)),
            pl.BlockSpec((SEG_STEP, stations), lambda i: (i, 0)),
            pl.BlockSpec((samples, 2 * BINS), lambda i: (0, 0)),
            pl.BlockSpec((samples, 2 * BINS), lambda i: (0, 0)),
        ],
        out_specs=[half_spec, half_spec],
        out_shape=[half, half],
        scratch_shapes=[
            pltpu.VMEM((2, stations * SEG_STEP, BINS), jnp.float32),
            pltpu.VMEM((2 * BINS * SEG_STEP, stations), jnp.float32),
        ],
        compiler_params=pltpu.CompilerParams(vmem_limit_bytes=60 * MIB),
        name="whiten",
    )(records, available.T, jnp.asarray(high), jnp.asarray(low))


def rows_kernel(panel_ref, mine_ref):
    bins, depth, rows = panel_ref.shape
    half = depth // 2
    for f in range(bins):
        real = panel_ref[f, :half, :].T
        imag = panel_ref[f, half:, :].T
        mine_ref[f, :rows, :half] = real
        mine_ref[f, :rows, half:] = imag
        mine_ref[f, rows:, :half] = imag
        mine_ref[f, rows:, half:] = -real


def rows_of(panel):
    bins, depth, rows = panel.shape
    step = 2
    return pl.pallas_call(
        rows_kernel,
        grid=(bins // step,),
        in_specs=[pl.BlockSpec((step, depth, rows), lambda f: (f, 0, 0))],
        out_specs=pl.BlockSpec((step, 2 * rows, depth), lambda f: (f, 0, 0)),
        out_shape=jax.ShapeDtypeStruct((bins, 2 * rows, depth), panel.dtype),
        compiler_params=pltpu.CompilerParams(vmem_limit_bytes=60 * MIB),
        name="rows",
    )(panel)


def gram_kernel(scale, halves, where, mine0_ref, mine1_ref, *refs):
    count = len(halves)
    panels, (out_ref, slots, sems) = [v.at[0] if len(v.shape) == 4 else v for v in refs[: 2 * count]], refs[-3:]
    step, steps = pl.program_id(0), pl.num_programs(0)
    bins = mine0_ref.shape[0]
    rows, cols = mine0_ref.shape[1] // 2, panels[0].shape[2]
    slot = lax.rem(step, 2)

    def write(at, block, held):
        spot = pl.ds(pl.multiple_of(where[block] * 2 * cols, 2 * cols), 2 * cols)
        return pltpu.make_async_copy(
            slots.at[held, block],
            out_ref.at[:, pl.ds(halves[block] * HALF + at * bins, bins), :, spot],
            sems.at[held, block],
        )

    @pl.when(step >= 2)
    def _():
        for block in range(count):
            write(step - 2, block, slot).wait()

    own = pl.ds(pl.multiple_of(where[count] * cols, cols), cols)
    other = pl.ds(pl.multiple_of((1 - where[count]) * cols, cols), cols)
    for block in range(count):
        mine_ref = mine1_ref if halves[block] else mine0_ref
        for f in range(bins):
            panel = jnp.concatenate([panels[2 * block][f], panels[2 * block + 1][f]], axis=1)
            gram = jnp.dot(mine_ref[f], panel, preferred_element_type=jnp.float32) * scale
            gram = gram.astype(jnp.bfloat16)
            slots[slot, block, 0, f, :, own] = gram[:rows, :cols]
            slots[slot, block, 1, f, :, own] = gram[rows:, :cols]
            slots[slot, block, 0, f, :, other] = gram[:rows, cols:]
            slots[slot, block, 1, f, :, other] = gram[rows:, cols:]
        write(step, block, slot).start()

    @pl.when(step == steps - 1)
    def _():
        for block in range(count):
            write(step - 1, block, 1 - slot).wait()
            write(step, block, slot).wait()


def gram(core, mine, blocks, shape, out):
    bins, depth, cols = blocks[0][2].shape
    rows = shape[2]
    count, step = len(blocks), 2
    halves = [half for half, _, _, _ in blocks]
    where = jnp.stack([chip for _, chip, _, _ in blocks] + [core]).astype(jnp.int32)
    held = [] if out is None else [out]
    panels = [v for _, _, own, other in blocks for v in (own, other)]
    used = [
        pl.BlockSpec((step, 2 * rows, depth), (lambda f, w: (f, 0, 0)) if half in halves else (lambda f, w: (0, 0, 0)))
        for half in range(2)
    ]
    return pl.pallas_call(
        functools.partial(gram_kernel, 2.0 / depth, halves),
        grid_spec=pltpu.PrefetchScalarGridSpec(
            num_scalar_prefetch=1,
            grid=(bins // step,),
            in_specs=used
            + [
                pl.BlockSpec((step, depth, cols), lambda f, w: (f, 0, 0))
                if v.ndim == 3
                else pl.BlockSpec((1, step, depth, cols), lambda f, w: (1 - w[count], f, 0, 0))
                for v in panels
            ]
            + [pl.BlockSpec(memory_space=pl.ANY)] * len(held),
            out_specs=pl.BlockSpec(memory_space=pl.ANY),
            scratch_shapes=[
                pltpu.VMEM((2, count, 2, step, rows, 2 * cols), jnp.bfloat16),
                pltpu.SemaphoreType.DMA((2, count)),
            ],
        ),
        out_shape=jax.ShapeDtypeStruct(shape, jnp.bfloat16),
        input_output_aliases={3 + 2 * count: 0} if held else {},
        cost_estimate=pl.CostEstimate(
            flops=16 * count * bins * rows * depth * cols,
            bytes_accessed=2 * bins * (2 * rows * depth + count * (2 * depth * cols + 4 * rows * cols)),
            transcendentals=0,
        ),
        compiler_params=pltpu.CompilerParams(vmem_limit_bytes=60 * MIB),
        name="gram",
    )(where, *mine, *panels, *held)


def after(value, *others):
    return lax.optimization_barrier((value, *others))[0]


def ring(size, step):
    return [(i, (i + step) % size) for i in range(size)]


def shards(records, available):
    stations = records.shape[0]
    x, yh, core = lax.axis_index("x"), lax.axis_index("yh"), lax.axis_index("core")
    right = lambda v: lax.ppermute(v, "x", ring(4, 1))
    left = lambda v: lax.ppermute(v, "x", ring(4, -1))
    over = lambda v: lax.ppermute(v, "yh", ring(2, 1))
    swap = lambda v: lax.ppermute(v, "core", ring(2, 1))
    both = lambda v: lax.all_gather(v, "core")

    def owned(half):
        got = lax.all_to_all(half, ("yl", "z"), split_axis=0, concat_axis=0, tiled=True)
        got = jnp.transpose(got, (1, 2, 0, 3, 4))
        return got.reshape(HALF, -1, stations)

    def entry(half, dx, dy, own, other):
        return half, (x - dx) % 4 * 2 + (yh + dy) % 2, own, other

    gate = lambda *values: lax.optimization_barrier(values)
    shape = (2, 2 * HALF, stations, 16 * stations)
    first, second = whiten(records, available)
    p0 = owned(first)
    p0, second = gate(p0, second)

    a0, b0, p1, sp0, m0 = right(p0), left(p0), owned(second), swap(p0), rows_of(p0)
    p0, p1, a0, b0, sp0, m0 = gate(p0, p1, a0, b0, sp0, m0)

    b1, a1, c0, sa0, sb0, sp1 = right(p1), left(p1), over(p0), swap(a0), swap(b0), both(p1)
    m1 = rows_of(p1)
    out = gram(core, (m0, m0), [entry(0, 0, 0, p0, sp0)], shape, None)
    p1, a0, b0, a1, b1, c0, sa0, sb0, sp1, m1, out = gate(p1, a0, b0, a1, b1, c0, sa0, sb0, sp1, m1, out)
    mine = m0, m1

    d0, d1, c1, sa1, sb1, sc0 = right(a0), left(a1), over(p1), swap(a1), swap(b1), both(c0)
    blocks = [entry(1, 0, 0, p1, sp1), entry(0, 1, 0, a0, sa0), entry(0, -1, 0, b0, sb0)]
    out = gram(core, mine, blocks, shape, out)
    a0, a1, b1, c0, c1, d0, d1, sa1, sb1, sc0, out = gate(a0, a1, b1, c0, c1, d0, d1, sa1, sb1, sc0, out)

    g1, g0, f0, sd0, sd1, sc1 = right(c1), left(c0), over(a0), swap(d0), swap(d1), both(c1)
    blocks = [entry(1, -1, 0, a1, sa1), entry(1, 1, 0, b1, sb1), entry(0, 0, 1, c0, sc0)]
    out = gram(core, mine, blocks, shape, out)
    c1, d0, d1, g0, g1, f0, sd0, sd1, sc1, out = gate(c1, d0, d1, g0, g1, f0, sd0, sd1, sc1, out)

    h0, e1, f1, sg0, sg1, sf0 = right(f0), left(c1), over(d1), swap(g0), swap(g1), both(f0)
    blocks = [entry(0, 2, 0, d0, sd0), entry(1, -2, 0, d1, sd1), entry(1, 0, 1, c1, sc1)]
    out = gram(core, mine, blocks, shape, out)
    blocks = [entry(0, -1, 1, g0, sg0), entry(1, 1, 1, g1, sg1), entry(0, 1, 1, f0, sf0)]
    out = gram(core, mine, blocks, shape, out)
    h0, e1, f1, out = gate(h0, e1, f1, out)

    blocks = [entry(0, 2, 1, h0, swap(h0)), entry(1, -1, 1, e1, swap(e1)), entry(1, -2, 1, f1, swap(f1))]
    return gram(core, mine, blocks, shape, out)


def solution(mesh):
    fine = Mesh(mesh.devices.reshape(4, 2, 2, 2, 4), ("x", "yh", "core", "yl", "z"))
    sta, freq = ("x", "yh", "core"), ("yl", "z")
    return jax.shard_map(
        shards,
        mesh=fine,
        in_specs=(P(sta, freq, None), P(sta, freq)),
        out_specs=P(None, freq, sta, None),
        check_vma=False,
    )
```

```python
import functools

import jax
import jax.numpy as jnp
import numpy as np
from jax import lax
from jax.experimental import pallas as pl
from jax.experimental.pallas import tpu as pltpu
from jax.sharding import Mesh, PartitionSpec as P

FFT_LEN = 512
BINS = 128
BAND_LO = 16
OWNERS = 8
CHUNK = 4
SEG_STEP = 8
MIB = 1024 * 1024


def spectra_table():
    sample = np.arange(FFT_LEN)
    bins = (BAND_LO + np.arange(BINS)).reshape(OWNERS, 2, 2, CHUNK).transpose(2, 0, 1, 3).reshape(-1)
    phase = (sample[:, None] * bins[None, :] % FFT_LEN) * (2.0 * np.pi / FFT_LEN)
    taper = 0.5 - 0.5 * np.cos(2.0 * np.pi * sample / FFT_LEN)
    table = np.stack([np.cos(phase), -np.sin(phase)], axis=2).reshape(FFT_LEN, 2 * BINS) * taper[:, None]
    high = table.astype(jnp.bfloat16)
    low = (table - high.astype(np.float64)).astype(jnp.bfloat16)
    return high, low


def whiten_kernel(records_ref, available_ref, high_ref, low_ref, first_ref, second_ref, rows_ref, turned_ref):
    stations, segs, samples = records_ref.shape
    flat = records_ref[...].reshape(stations * segs, samples)
    spectra = jnp.dot(flat, high_ref[...], preferred_element_type=jnp.float32)
    spectra += jnp.dot(flat, low_ref[...], preferred_element_type=jnp.float32)
    wide = spectra.shape[1]
    for part in range(2):
        rows_ref[part] = spectra[:, part * BINS : (part + 1) * BINS]
    for seg in range(segs):
        turned = jnp.concatenate(
            [rows_ref[part, pl.ds(seg, stations, stride=segs), :].T for part in range(2)], axis=0
        )
        power = jnp.sum(turned * turned, axis=0, keepdims=True) / BINS
        weight = available_ref[seg : seg + 1, :].astype(jnp.float32) / jnp.sqrt(power + 1e-05)
        turned_ref[pl.ds(seg, wide, stride=segs), :] = turned * weight
    whitened = turned_ref[...].reshape(2, 2 * OWNERS, CHUNK, 2, segs, stations).astype(jnp.bfloat16)
    first_ref[...] = whitened[0]
    second_ref[...] = whitened[1]


def whiten(records, available):
    stations, segments, samples = records.shape
    high, low = spectra_table()
    half = jax.ShapeDtypeStruct((2 * OWNERS, CHUNK, 2, segments, stations), jnp.bfloat16)
    half_spec = pl.BlockSpec((2 * OWNERS, CHUNK, 2, SEG_STEP, stations), lambda i: (0, 0, 0, i, 0))
    return pl.pallas_call(
        whiten_kernel,
        grid=(segments // SEG_STEP,),
        in_specs=[
            pl.BlockSpec((stations, SEG_STEP, samples), lambda i: (0, i, 0)),
            pl.BlockSpec((SEG_STEP, stations), lambda i: (i, 0)),
            pl.BlockSpec((samples, 2 * BINS), lambda i: (0, 0)),
            pl.BlockSpec((samples, 2 * BINS), lambda i: (0, 0)),
        ],
        out_specs=[half_spec, half_spec],
        out_shape=[half, half],
        scratch_shapes=[
            pltpu.VMEM((2, stations * SEG_STEP, BINS), jnp.float32),
            pltpu.VMEM((2 * BINS * SEG_STEP, stations), jnp.float32),
        ],
        compiler_params=pltpu.CompilerParams(vmem_limit_bytes=60 * MIB),
        name="whiten",
    )(records, available.T, jnp.asarray(high), jnp.asarray(low))


def rows_kernel(panel_ref, mine_ref):
    bins, depth, width = panel_ref.shape
    half, rows = depth // 2, width // 2
    for f in range(bins):
        for core in range(2):
            real = panel_ref[f, :half, core * rows : (core + 1) * rows].T
            imag = panel_ref[f, half:, core * rows : (core + 1) * rows].T
            base = 2 * rows * core
            mine_ref[f, base : base + rows, :half] = real
            mine_ref[f, base : base + rows, half:] = imag
            mine_ref[f, base + rows : base + 2 * rows, :half] = imag
            mine_ref[f, base + rows : base + 2 * rows, half:] = -real


def rows_of(panel):
    bins, depth, width = panel.shape
    return pl.pallas_call(
        rows_kernel,
        grid=(bins,),
        in_specs=[pl.BlockSpec((1, depth, width), lambda f: (f, 0, 0))],
        out_specs=pl.BlockSpec((1, 2 * width, depth), lambda f: (f, 0, 0)),
        out_shape=jax.ShapeDtypeStruct((bins, 2 * width, depth), panel.dtype),
        compiler_params=pltpu.CompilerParams(vmem_limit_bytes=60 * MIB),
        name="rows",
    )(panel)


def placing(where, count, placed, sent_ref, out_ref, place_sem):
    core = where[count]
    for at, chunk in enumerate(placed):
        bins, cols = sent_ref.shape[2], sent_ref.shape[4]
        spot = pl.ds(pl.multiple_of(where[count + 1 + at] * cols, cols), cols)
        first = (1 - core) * 2 * CHUNK + chunk * CHUNK
        yield pltpu.make_async_copy(
            sent_ref.at[at], out_ref.at[:, pl.ds(first, bins), :, spot], place_sem.at[at]
        )


def gram_kernel(scale, chunks, placed, where, mine0_ref, mine1_ref, *refs):
    count = len(chunks)
    panels, rest = refs[:count], refs[count:]
    sent_ref = rest[0] if placed else None
    out_ref, send_ref, slots, sems, place_sem = rest[-5:]
    step, steps = pl.program_id(0), pl.num_programs(0)
    rows, cols = mine0_ref.shape[1] // 4, panels[0].shape[2]
    slot, core = lax.rem(step, 2), where[count]

    def writes(at, block, held):
        spot = pl.ds(pl.multiple_of(where[block] * cols, cols), cols)
        first = core * 2 * CHUNK + chunks[block] * CHUNK + at
        return (
            pltpu.make_async_copy(
                slots.at[held, block, core],
                out_ref.at[:, first, :, spot],
                sems.at[held, block, 0],
            ),
            pltpu.make_async_copy(
                slots.at[held, block, 1 - core],
                send_ref.at[block, :, at],
                sems.at[held, block, 1],
            ),
        )

    def place():
        return placing(where, count, placed, sent_ref, out_ref, place_sem)

    @pl.when(step == 0)
    def _():
        for copy in place():
            copy.start()

    @pl.when(step >= 2)
    def _():
        for block in range(count):
            for copy in writes(step - 2, block, slot):
                copy.wait()

    for block in range(count):
        mine_ref = mine1_ref if chunks[block] else mine0_ref
        gram = jnp.dot(mine_ref[0], panels[block][0], preferred_element_type=jnp.float32) * scale
        gram = gram.astype(jnp.bfloat16)
        for target in range(2):
            for part in range(2):
                base = (2 * target + part) * rows
                slots[slot, block, target, part] = gram[base : base + rows]
        for copy in writes(step, block, slot):
            copy.start()

    @pl.when(step == steps - 1)
    def _():
        for block in range(count):
            for copy in (*writes(step - 1, block, 1 - slot), *writes(step, block, slot)):
                copy.wait()
        for copy in place():
            copy.wait()


def gram(core, mine, blocks, shape, out, sent):
    bins, depth, cols = blocks[0][3].shape
    rows = shape[2]
    count = len(blocks)
    chunks = [block[0] for block in blocks]
    placed = [block[0] for block in sent[0]] if sent else []
    where = [block[1] for block in blocks] + [core] + ([block[2] for block in sent[0]] if sent else [])
    held = ([sent[1]] if sent else []) + ([] if out is None else [out])
    used = [
        pl.BlockSpec((1, 4 * rows, depth), (lambda f, w: (f, 0, 0)) if chunk in chunks else (lambda f, w: (0, 0, 0)))
        for chunk in range(2)
    ]
    send = jax.ShapeDtypeStruct((count, 2, bins, rows, cols), jnp.bfloat16)
    return pl.pallas_call(
        functools.partial(gram_kernel, 2.0 / depth, chunks, placed),
        grid_spec=pltpu.PrefetchScalarGridSpec(
            num_scalar_prefetch=1,
            grid=(bins,),
            in_specs=used
            + [pl.BlockSpec((1, depth, cols), lambda f, w: (f, 0, 0))] * count
            + [pl.BlockSpec(memory_space=pl.ANY)] * len(held),
            out_specs=[pl.BlockSpec(memory_space=pl.ANY)] * 2,
            scratch_shapes=[
                pltpu.VMEM((2, count, 2, 2, rows, cols), jnp.bfloat16),
                pltpu.SemaphoreType.DMA((2, count, 2)),
                pltpu.SemaphoreType.DMA((4,)),
            ],
        ),
        out_shape=[jax.ShapeDtypeStruct(shape, jnp.bfloat16), send],
        input_output_aliases={2 + count + len(held): 0} if out is not None else {},
        cost_estimate=pl.CostEstimate(
            flops=8 * count * bins * rows * depth * cols,
            bytes_accessed=2 * bins * (8 * rows * depth + count * (depth * cols + 4 * rows * cols)),
            transcendentals=0,
        ),
        compiler_params=pltpu.CompilerParams(vmem_limit_bytes=60 * MIB),
        name="gram",
    )(jnp.stack(where).astype(jnp.int32), *mine, *[block[3] for block in blocks], *held)


def place_kernel(placed, where, sent_ref, _, out_ref, place_sem):
    for copy in placing(where, 0, placed, sent_ref, out_ref, place_sem):
        copy.start()
    for copy in placing(where, 0, placed, sent_ref, out_ref, place_sem):
        copy.wait()


def place(core, sent, out):
    return pl.pallas_call(
        functools.partial(place_kernel, [block[0] for block in sent[0]]),
        grid_spec=pltpu.PrefetchScalarGridSpec(
            num_scalar_prefetch=1,
            grid=(1,),
            in_specs=[pl.BlockSpec(memory_space=pl.ANY)] * 2,
            out_specs=pl.BlockSpec(memory_space=pl.ANY),
            scratch_shapes=[pltpu.SemaphoreType.DMA((4,))],
        ),
        out_shape=jax.ShapeDtypeStruct(out.shape, out.dtype),
        input_output_aliases={2: 0},
        compiler_params=pltpu.CompilerParams(vmem_limit_bytes=60 * MIB),
        name="place",
    )(jnp.stack([core] + [block[2] for block in sent[0]]).astype(jnp.int32), sent[1], out)


def mirrored(step):
    return [
        (2 * x + core, (x + (1 - 2 * core) * step) % 4 * 2 + core) for x in range(4) for core in range(2)
    ]


def shards(records, available):
    stations = records.shape[0]
    x, yh, core = lax.axis_index("x"), lax.axis_index("yh"), lax.axis_index("core")
    fwd = lambda v: lax.ppermute(v, ("x", "core"), mirrored(1))
    bwd = lambda v: lax.ppermute(v, ("x", "core"), mirrored(-1))
    over = lambda v: lax.ppermute(v, "yh", [(0, 1), (1, 0)])
    swap = lambda v: lax.ppermute(v, "core", [(0, 1), (1, 0)])
    gate = lambda *values: lax.optimization_barrier(values)

    def owned(chunk):
        got = lax.all_to_all(chunk, ("yl", "z", "core"), split_axis=0, concat_axis=0, tiled=True)
        got = got.reshape(OWNERS, 2, *got.shape[1:])
        return jnp.transpose(got, (2, 3, 0, 4, 1, 5)).reshape(CHUNK, -1, 2 * stations)

    def entry(chunk, dx, dy, panel):
        sign = 1 - 2 * core
        chips = [(x - way * dx) % 4 * 2 + (yh + dy) % 2 for way in (sign, -sign)]
        return chunk, *chips, panel

    shape = (2, 4 * CHUNK, stations, 16 * stations)
    first, second = whiten(records, available)
    pa = owned(first)
    pa, second = gate(pa, second)

    na, ba, pb, ma = fwd(pa), bwd(pa), owned(second), rows_of(pa)
    pa, pb, na, ba, ma = gate(pa, pb, na, ba, ma)

    nb, bb, oa, mb = fwd(pb), bwd(pb), over(pa), rows_of(pb)
    blocks1 = [entry(0, 0, 0, pa), entry(0, 1, 0, na), entry(0, -1, 0, ba)]
    out, sent = gram(core, (ma, ma), blocks1, shape, None, None)
    na, nb, bb, oa, mb, pb, out, sent = gate(na, nb, bb, oa, mb, pb, out, sent)
    mine = ma, mb

    fa, fb, ob, sent1 = fwd(na), fwd(nb), over(pb), swap(sent)
    blocks2 = [entry(1, 0, 0, pb), entry(1, 1, 0, nb), entry(1, -1, 0, bb), entry(0, 0, 1, oa)]
    out, sent = gram(core, mine, blocks2, shape, out, None)
    na, oa, fa, fb, ob, sent1, out, sent = gate(na, oa, fa, fb, ob, sent1, out, sent)

    boa, bob, noa, sent2 = bwd(oa), bwd(ob), over(na), swap(sent)
    blocks3 = [entry(0, 2, 0, fa), entry(1, 2, 0, fb), entry(1, 0, 1, ob)]
    out, sent = gram(core, mine, blocks3, shape, out, (blocks1, sent1))
    ob, fb, boa, bob, noa, sent2, out, sent = gate(ob, fb, boa, bob, noa, sent2, out, sent)

    foa, nob, fob, sent3 = fwd(noa), fwd(ob), over(fb), swap(sent)
    blocks4 = [entry(0, -1, 1, boa), entry(1, -1, 1, bob), entry(0, 1, 1, noa)]
    out, sent = gram(core, mine, blocks4, shape, out, (blocks2, sent2))
    foa, nob, fob, sent3, out, sent = gate(foa, nob, fob, sent3, out, sent)

    sent4 = swap(sent)
    blocks5 = [entry(0, 2, 1, foa), entry(1, 1, 1, nob), entry(1, 2, 1, fob)]
    out, sent = gram(core, mine, blocks5, shape, out, (blocks3, sent3))
    sent5 = swap(sent)
    out = place(core, (blocks4, sent4), out)
    return place(core, (blocks5, sent5), out)


def solution(mesh):
    fine = Mesh(mesh.devices.reshape(4, 2, 2, 2, 4), ("x", "yh", "core", "yl", "z"))
    sta, freq = ("x", "yh", "core"), ("yl", "z")
    return jax.shard_map(
        shards,
        mesh=fine,
        in_specs=(P(sta, freq, None), P(sta, freq)),
        out_specs=P(None, freq, sta, None),
        check_vma=False,
    )
```

```python
import functools

import jax
import jax.numpy as jnp
import numpy as np
from jax import lax
from jax.experimental import pallas as pl
from jax.experimental.pallas import tpu as pltpu
from jax.sharding import Mesh, PartitionSpec as P

FFT_LEN = 512
BINS = 128
BAND_LO = 16
OWNERS = 8
CHUNK = 4
SEG_STEP = 8
MIB = 1024 * 1024


def spectra_table():
    sample = np.arange(FFT_LEN)
    bins = (BAND_LO + np.arange(BINS)).reshape(OWNERS, 2, 2, CHUNK).transpose(2, 0, 1, 3).reshape(-1)
    phase = (sample[:, None] * bins[None, :] % FFT_LEN) * (2.0 * np.pi / FFT_LEN)
    taper = 0.5 - 0.5 * np.cos(2.0 * np.pi * sample / FFT_LEN)
    table = np.stack([np.cos(phase), -np.sin(phase)], axis=2).reshape(FFT_LEN, 2 * BINS) * taper[:, None]
    high = table.astype(jnp.bfloat16)
    low = (table - high.astype(np.float64)).astype(jnp.bfloat16)
    return high, low


def whiten_kernel(records_ref, available_ref, high_ref, low_ref, first_ref, second_ref, rows_ref, turned_ref):
    stations, segs, samples = records_ref.shape
    flat = records_ref[...].reshape(stations * segs, samples)
    spectra = jnp.dot(flat, high_ref[...], preferred_element_type=jnp.float32)
    spectra += jnp.dot(flat, low_ref[...], preferred_element_type=jnp.float32)
    wide = spectra.shape[1]
    for part in range(2):
        rows_ref[part] = spectra[:, part * BINS : (part + 1) * BINS]
    for seg in range(segs):
        turned = jnp.concatenate(
            [rows_ref[part, pl.ds(seg, stations, stride=segs), :].T for part in range(2)], axis=0
        )
        power = jnp.sum(turned * turned, axis=0, keepdims=True) / BINS
        weight = available_ref[seg : seg + 1, :].astype(jnp.float32) / jnp.sqrt(power + 1e-05)
        turned_ref[pl.ds(seg, wide, stride=segs), :] = turned * weight
    whitened = turned_ref[...].reshape(2, 2 * OWNERS, CHUNK, 2, segs, stations).astype(jnp.bfloat16)
    first_ref[...] = whitened[0]
    second_ref[...] = whitened[1]


def whiten(records, available):
    stations, segments, samples = records.shape
    high, low = spectra_table()
    half = jax.ShapeDtypeStruct((2 * OWNERS, CHUNK, 2, segments, stations), jnp.bfloat16)
    half_spec = pl.BlockSpec((2 * OWNERS, CHUNK, 2, SEG_STEP, stations), lambda i: (0, 0, 0, i, 0))
    return pl.pallas_call(
        whiten_kernel,
        grid=(segments // SEG_STEP,),
        in_specs=[
            pl.BlockSpec((stations, SEG_STEP, samples), lambda i: (0, i, 0)),
            pl.BlockSpec((SEG_STEP, stations), lambda i: (i, 0)),
            pl.BlockSpec((samples, 2 * BINS), lambda i: (0, 0)),
            pl.BlockSpec((samples, 2 * BINS), lambda i: (0, 0)),
        ],
        out_specs=[half_spec, half_spec],
        out_shape=[half, half],
        scratch_shapes=[
            pltpu.VMEM((2, stations * SEG_STEP, BINS), jnp.float32),
            pltpu.VMEM((2 * BINS * SEG_STEP, stations), jnp.float32),
        ],
        compiler_params=pltpu.CompilerParams(vmem_limit_bytes=60 * MIB),
        name="whiten",
    )(records, available.T, jnp.asarray(high), jnp.asarray(low))


def rows_kernel(panel_ref, mine_ref):
    bins, depth, width = panel_ref.shape
    half, rows = depth // 2, width // 2
    for f in range(bins):
        for core in range(2):
            real = panel_ref[f, :half, core * rows : (core + 1) * rows].T
            imag = panel_ref[f, half:, core * rows : (core + 1) * rows].T
            base = 2 * rows * core
            mine_ref[f, base : base + rows, :half] = real
            mine_ref[f, base : base + rows, half:] = imag
            mine_ref[f, base + rows : base + 2 * rows, :half] = imag
            mine_ref[f, base + rows : base + 2 * rows, half:] = -real


def rows_of(panel):
    bins, depth, width = panel.shape
    return pl.pallas_call(
        rows_kernel,
        grid=(bins,),
        in_specs=[pl.BlockSpec((1, depth, width), lambda f: (f, 0, 0))],
        out_specs=pl.BlockSpec((1, 2 * width, depth), lambda f: (f, 0, 0)),
        out_shape=jax.ShapeDtypeStruct((bins, 2 * width, depth), panel.dtype),
        compiler_params=pltpu.CompilerParams(vmem_limit_bytes=60 * MIB),
        name="rows",
    )(panel)


def spot_of(where, at, cols):
    return pl.ds(pl.multiple_of(where[at] * cols, cols), cols)


def gram_kernel(scale, chunks, placed, where, mine0_ref, mine1_ref, *refs):
    count, sets = len(chunks), len(placed)
    panels, sent, rest = refs[:count], refs[count : count + sets], refs[count + sets :]
    out_ref, send_ref, slots, place_slots, sems, place_sems = rest[-6:]
    step, steps = pl.program_id(0), pl.num_programs(0)
    bins = mine0_ref.shape[0]
    rows, cols = mine0_ref.shape[1] // 4, panels[0].shape[2]
    slot, core = lax.rem(step, 2), where[count]
    received = [(which, at, chunk) for which, some in enumerate(placed) for at, chunk in enumerate(some)]

    def first_bin(owner, chunk, at):
        return owner * 2 * CHUNK + chunk * CHUNK + at * bins

    def writes(at, held):
        for block, chunk in enumerate(chunks):
            spot = out_ref.at[:, pl.ds(first_bin(core, chunk, at), bins), :, spot_of(where, block, cols)]
            yield pltpu.make_async_copy(slots.at[held, block, core], spot, sems.at[held, block, 0])
            spot = send_ref.at[block, :, pl.ds(at * bins, bins)]
            yield pltpu.make_async_copy(slots.at[held, block, 1 - core], spot, sems.at[held, block, 1])

    def places(at, held):
        for k, (_, _, chunk) in enumerate(received):
            spot = spot_of(where, count + 1 + k, cols)
            spot = out_ref.at[:, pl.ds(first_bin(1 - core, chunk, at), bins), :, spot]
            yield pltpu.make_async_copy(place_slots.at[held, k], spot, place_sems.at[held, k])

    @pl.when(step >= 2)
    def _():
        for copy in (*writes(step - 2, slot), *places(step - 2, slot)):
            copy.wait()

    for k, (which, at, _) in enumerate(received):
        place_slots[slot, k] = sent[which][at]
    for copy in places(step, slot):
        copy.start()
    for block, chunk in enumerate(chunks):
        mine_ref = mine1_ref if chunk else mine0_ref
        for f in range(bins):
            gram = jnp.dot(mine_ref[f], panels[block][f], preferred_element_type=jnp.float32) * scale
            gram = gram.astype(jnp.bfloat16)
            for target in range(2):
                for part in range(2):
                    base = (2 * target + part) * rows
                    slots[slot, block, target, part, f] = gram[base : base + rows]
    for copy in writes(step, slot):
        copy.start()

    @pl.when(step == steps - 1)
    def _():
        for copy in (*writes(step - 1, 1 - slot), *places(step - 1, 1 - slot)):
            copy.wait()
        for copy in (*writes(step, slot), *places(step, slot)):
            copy.wait()


def sent_spec(results, step):
    block = (results.shape[0], 2, step, *results.shape[3:])
    return pl.BlockSpec(block, lambda f, w: (0, 0, f, 0, 0))


def gram(core, mine, blocks, shape, out, *sent):
    bins, depth, cols = blocks[0][3].shape
    rows, step = shape[2], 2
    count = len(blocks)
    chunks = [block[0] for block in blocks]
    received = [block for some, _ in sent for block in some]
    where = [block[1] for block in blocks] + [core] + [block[2] for block in received]
    held = [] if out is None else [out]
    used = [
        pl.BlockSpec((step, 4 * rows, depth), (lambda f, w: (f, 0, 0)) if chunk in chunks else (lambda f, w: (0, 0, 0)))
        for chunk in range(2)
    ]
    send = jax.ShapeDtypeStruct((count, 2, bins, rows, cols), jnp.bfloat16)
    spots = max(len(received), 1)
    return pl.pallas_call(
        functools.partial(gram_kernel, 2.0 / depth, chunks, [[block[0] for block in some] for some, _ in sent]),
        grid_spec=pltpu.PrefetchScalarGridSpec(
            num_scalar_prefetch=1,
            grid=(bins // step,),
            in_specs=used
            + [pl.BlockSpec((step, depth, cols), lambda f, w: (f, 0, 0))] * count
            + [sent_spec(results, step) for _, results in sent]
            + [pl.BlockSpec(memory_space=pl.ANY)] * len(held),
            out_specs=[pl.BlockSpec(memory_space=pl.ANY)] * 2,
            scratch_shapes=[
                pltpu.VMEM((2, count, 2, 2, step, rows, cols), jnp.bfloat16),
                pltpu.VMEM((2, spots, 2, step, rows, cols), jnp.bfloat16),
                pltpu.SemaphoreType.DMA((2, count, 2)),
                pltpu.SemaphoreType.DMA((2, spots)),
            ],
        ),
        out_shape=[jax.ShapeDtypeStruct(shape, jnp.bfloat16), send],
        input_output_aliases={3 + count + len(sent): 0} if held else {},
        cost_estimate=pl.CostEstimate(
            flops=8 * count * bins * rows * depth * cols,
            bytes_accessed=2 * bins * (8 * rows * depth + count * (depth * cols + 4 * rows * cols)),
            transcendentals=0,
        ),
        compiler_params=pltpu.CompilerParams(vmem_limit_bytes=60 * MIB),
        name="gram",
    )(jnp.stack(where).astype(jnp.int32), *mine, *[block[3] for block in blocks], *[r for _, r in sent], *held)


def place_kernel(chunks, where, sent_ref, _, out_ref, sems):
    bins, cols = sent_ref.shape[2], sent_ref.shape[4]
    step, core = pl.program_id(0), where[len(chunks)]
    copies = []
    for k, chunk in enumerate(chunks):
        first = (1 - core) * 2 * CHUNK + chunk * CHUNK + step * bins
        spot = out_ref.at[:, pl.ds(first, bins), :, spot_of(where, k, cols)]
        copies.append(pltpu.make_async_copy(sent_ref.at[k], spot, sems.at[k]))
    for copy in copies:
        copy.start()
    for copy in copies:
        copy.wait()


def place(core, sent, out):
    blocks, results = sent
    return pl.pallas_call(
        functools.partial(place_kernel, [block[0] for block in blocks]),
        grid_spec=pltpu.PrefetchScalarGridSpec(
            num_scalar_prefetch=1,
            grid=(results.shape[2] // 2,),
            in_specs=[sent_spec(results, 2), pl.BlockSpec(memory_space=pl.ANY)],
            out_specs=pl.BlockSpec(memory_space=pl.ANY),
            scratch_shapes=[pltpu.SemaphoreType.DMA((len(blocks),))],
        ),
        out_shape=jax.ShapeDtypeStruct(out.shape, out.dtype),
        input_output_aliases={2: 0},
        compiler_params=pltpu.CompilerParams(vmem_limit_bytes=60 * MIB),
        name="place",
    )(jnp.stack([block[2] for block in blocks] + [core]).astype(jnp.int32), results, out)


def mirrored(step):
    return [
        (2 * x + core, (x + (1 - 2 * core) * step) % 4 * 2 + core) for x in range(4) for core in range(2)
    ]


def shards(records, available):
    stations = records.shape[0]
    x, yh, core = lax.axis_index("x"), lax.axis_index("yh"), lax.axis_index("core")
    fwd = lambda v: lax.ppermute(v, ("x", "core"), mirrored(1))
    bwd = lambda v: lax.ppermute(v, ("x", "core"), mirrored(-1))
    over = lambda v: lax.ppermute(v, "yh", [(0, 1), (1, 0)])
    swap = lambda v: lax.ppermute(v, "core", [(0, 1), (1, 0)])
    after = lambda value, *others: lax.optimization_barrier((value, *others))[0]

    def owned(chunk):
        got = lax.all_to_all(chunk, ("yl", "z", "core"), split_axis=0, concat_axis=0, tiled=True)
        got = got.reshape(OWNERS, 2, *got.shape[1:])
        return jnp.transpose(got, (2, 3, 0, 4, 1, 5)).reshape(CHUNK, -1, 2 * stations)

    def entry(chunk, dx, dy, panel):
        sign = 1 - 2 * core
        chips = [(x - way * dx) % 4 * 2 + (yh + dy) % 2 for way in (sign, -sign)]
        return chunk, *chips, panel

    shape = (2, 4 * CHUNK, stations, 16 * stations)
    first, second = whiten(records, available)
    pa = owned(first)
    na, ba = fwd(pa), bwd(pa)
    pb = owned(after(second, pa))
    ma = rows_of(pa)

    nb, bb, oa = fwd(after(pb, na)), bwd(after(pb, ba)), over(after(pa, pb))
    blocks1 = [entry(0, 0, 0, pa), entry(0, 1, 0, na), entry(0, -1, 0, ba)]
    out, sent = gram(core, (ma, ma), blocks1, shape, None)
    mine = ma, rows_of(pb)

    fa, fb, ob = fwd(after(na, nb, out)), fwd(after(nb, bb)), over(after(pb, oa))
    sent1 = blocks1, swap(sent)
    blocks2 = [entry(1, 0, 0, pb), entry(1, 1, 0, nb), entry(1, -1, 0, bb), entry(0, 0, 1, oa)]
    out, sent = gram(core, mine, blocks2, shape, out)

    boa, bob, noa = bwd(after(oa, fa, out)), bwd(after(ob, fb)), over(after(na, ob))
    sent2 = blocks2, swap(sent)
    blocks3 = [entry(0, 2, 0, fa), entry(1, 2, 0, fb), entry(1, 0, 1, ob)]
    out, sent = gram(core, mine, blocks3, shape, out, sent1)

    foa, nob, fob = fwd(after(noa, boa, out)), fwd(after(ob, bob)), over(after(fb, noa))
    sent3 = blocks3, swap(sent)
    blocks4 = [entry(0, -1, 1, boa), entry(1, -1, 1, bob), entry(0, 1, 1, noa)]
    out, sent = gram(core, mine, blocks4, shape, out, sent2)

    sent4 = blocks4, swap(sent)
    blocks5 = [entry(0, 2, 1, foa), entry(1, 1, 1, nob), entry(1, 2, 1, fob)]
    out, sent = gram(core, mine, blocks5, shape, out, sent3)
    out = place(core, sent4, out)
    return place(core, (blocks5, swap(sent)), out)


def solution(mesh):
    fine = Mesh(mesh.devices.reshape(4, 2, 2, 2, 4), ("x", "yh", "core", "yl", "z"))
    sta, freq = ("x", "yh", "core"), ("yl", "z")
    return jax.shard_map(
        shards,
        mesh=fine,
        in_specs=(P(sta, freq, None), P(sta, freq)),
        out_specs=P(None, freq, sta, None),
        check_vma=False,
    )
```

```python
import functools

import jax
import jax.numpy as jnp
import numpy as np
from jax import lax
from jax.experimental import pallas as pl
from jax.experimental.pallas import tpu as pltpu
from jax.sharding import Mesh, PartitionSpec as P

FFT_LEN = 512
BINS = 128
BAND_LO = 16
OWNERS = 8
CHUNK = 4
SEG_STEP = 8
MIB = 1024 * 1024


def spectra_table():
    sample = np.arange(FFT_LEN)
    bins = (BAND_LO + np.arange(BINS)).reshape(OWNERS, 2, 2, CHUNK).transpose(2, 0, 1, 3).reshape(-1)
    phase = (sample[:, None] * bins[None, :] % FFT_LEN) * (2.0 * np.pi / FFT_LEN)
    taper = 0.5 - 0.5 * np.cos(2.0 * np.pi * sample / FFT_LEN)
    table = np.stack([np.cos(phase), -np.sin(phase)], axis=2).reshape(FFT_LEN, 2 * BINS) * taper[:, None]
    high = table.astype(jnp.bfloat16)
    low = (table - high.astype(np.float64)).astype(jnp.bfloat16)
    return high, low


def whiten_kernel(records_ref, available_ref, high_ref, low_ref, first_ref, second_ref, rows_ref, turned_ref):
    stations, segs, samples = records_ref.shape
    flat = records_ref[...].reshape(stations * segs, samples)
    spectra = jnp.dot(flat, high_ref[...], preferred_element_type=jnp.float32)
    spectra += jnp.dot(flat, low_ref[...], preferred_element_type=jnp.float32)
    wide = spectra.shape[1]
    for part in range(2):
        rows_ref[part] = spectra[:, part * BINS : (part + 1) * BINS]
    for seg in range(segs):
        turned = jnp.concatenate(
            [rows_ref[part, pl.ds(seg, stations, stride=segs), :].T for part in range(2)], axis=0
        )
        power = jnp.sum(turned * turned, axis=0, keepdims=True) / BINS
        weight = available_ref[seg : seg + 1, :].astype(jnp.float32) / jnp.sqrt(power + 1e-05)
        turned_ref[pl.ds(seg, wide, stride=segs), :] = turned * weight
    whitened = turned_ref[...].reshape(2, 2 * OWNERS, CHUNK, 2, segs, stations).astype(jnp.bfloat16)
    first_ref[...] = whitened[0]
    second_ref[...] = whitened[1]


def whiten(records, available):
    stations, segments, samples = records.shape
    high, low = spectra_table()
    half = jax.ShapeDtypeStruct((2 * OWNERS, CHUNK, 2, segments, stations), jnp.bfloat16)
    half_spec = pl.BlockSpec((2 * OWNERS, CHUNK, 2, SEG_STEP, stations), lambda i: (0, 0, 0, i, 0))
    return pl.pallas_call(
        whiten_kernel,
        grid=(segments // SEG_STEP,),
        in_specs=[
            pl.BlockSpec((stations, SEG_STEP, samples), lambda i: (0, i, 0)),
            pl.BlockSpec((SEG_STEP, stations), lambda i: (i, 0)),
            pl.BlockSpec((samples, 2 * BINS), lambda i: (0, 0)),
            pl.BlockSpec((samples, 2 * BINS), lambda i: (0, 0)),
        ],
        out_specs=[half_spec, half_spec],
        out_shape=[half, half],
        scratch_shapes=[
            pltpu.VMEM((2, stations * SEG_STEP, BINS), jnp.float32),
            pltpu.VMEM((2 * BINS * SEG_STEP, stations), jnp.float32),
        ],
        compiler_params=pltpu.CompilerParams(vmem_limit_bytes=60 * MIB),
        name="whiten",
    )(records, available.T, jnp.asarray(high), jnp.asarray(low))


def rows_kernel(panel_ref, mine_ref):
    bins, depth, width = panel_ref.shape
    half, rows = depth // 2, width // 2
    for f in range(bins):
        for core in range(2):
            real = panel_ref[f, :half, core * rows : (core + 1) * rows].T
            imag = panel_ref[f, half:, core * rows : (core + 1) * rows].T
            base = 2 * rows * core
            mine_ref[f, base : base + rows, :half] = real
            mine_ref[f, base : base + rows, half:] = imag
            mine_ref[f, base + rows : base + 2 * rows, :half] = imag
            mine_ref[f, base + rows : base + 2 * rows, half:] = -real


def rows_of(panel):
    bins, depth, width = panel.shape
    return pl.pallas_call(
        rows_kernel,
        grid=(bins,),
        in_specs=[pl.BlockSpec((1, depth, width), lambda f: (f, 0, 0))],
        out_specs=pl.BlockSpec((1, 2 * width, depth), lambda f: (f, 0, 0)),
        out_shape=jax.ShapeDtypeStruct((bins, 2 * width, depth), panel.dtype),
        compiler_params=pltpu.CompilerParams(vmem_limit_bytes=24 * MIB),
        name="rows",
    )(panel)


def spot_of(where, at, cols):
    return pl.ds(pl.multiple_of(where[at] * cols, cols), cols)


def gram_kernel(scale, chunks, placed, own, other, where, mine0_ref, mine1_ref, *refs):
    count, sets = len(chunks), len(placed)
    panels, sent, rest = refs[:count], refs[count : count + sets], refs[count + sets :]
    slots, place_slots, sems, place_sems = rest[-4:]
    out_ref, send_ref = rest[-5 - (own and other)], rest[-5]
    step, steps = pl.program_id(0), pl.num_programs(0)
    bins = mine0_ref.shape[0]
    rows, cols = mine0_ref.shape[1] // 4, panels[0].shape[2]
    slot, core = lax.rem(step, 2), where[count]
    received = [(which, at, chunk) for which, some in enumerate(placed) for at, chunk in enumerate(some)]

    def first_bin(owner, chunk, at):
        return owner * 2 * CHUNK + chunk * CHUNK + at * bins

    def writes(at, held):
        for block, chunk in enumerate(chunks):
            if own:
                spot = out_ref.at[:, pl.ds(first_bin(core, chunk, at), bins), :, spot_of(where, block, cols)]
                source = slots.at[held, block, core if other else 0]
                yield pltpu.make_async_copy(source, spot, sems.at[held, block, 0])
            if other:
                spot = send_ref.at[block, :, pl.ds(at * bins, bins)]
                source = slots.at[held, block, 1 - core if own else 0]
                yield pltpu.make_async_copy(source, spot, sems.at[held, block, 1])

    def places(at, held):
        for k, (_, _, chunk) in enumerate(received):
            spot = spot_of(where, count + 1 + k, cols)
            spot = out_ref.at[:, pl.ds(first_bin(1 - core, chunk, at), bins), :, spot]
            yield pltpu.make_async_copy(place_slots.at[held, k], spot, place_sems.at[held, k])

    @pl.when(step >= 2)
    def _():
        for copy in (*writes(step - 2, slot), *places(step - 2, slot)):
            copy.wait()

    for k, (which, at, _) in enumerate(received):
        place_slots[slot, k] = sent[which][at]
    for copy in places(step, slot):
        copy.start()
    for block, chunk in enumerate(chunks):
        mine_ref = mine1_ref if chunk else mine0_ref
        for f in range(bins):
            if own and other:
                mine = mine_ref[f]
            else:
                target = core if own else 1 - core
                mine = mine_ref[f, pl.ds(pl.multiple_of(target * 2 * rows, 2 * rows), 2 * rows), :]
            gram = jnp.dot(mine, panels[block][f], preferred_element_type=jnp.float32) * scale
            gram = gram.astype(jnp.bfloat16)
            for target in range(own + other):
                for part in range(2):
                    base = (2 * target + part) * rows
                    slots[slot, block, target, part, f] = gram[base : base + rows]
    for copy in writes(step, slot):
        copy.start()

    @pl.when(step == steps - 1)
    def _():
        for copy in (*writes(step - 1, 1 - slot), *places(step - 1, 1 - slot)):
            copy.wait()
        for copy in (*writes(step, slot), *places(step, slot)):
            copy.wait()


def sent_spec(results, step):
    block = (results.shape[0], 2, step, *results.shape[3:])
    return pl.BlockSpec(block, lambda f, w: (0, 0, f, 0, 0))


def gram(core, mine, blocks, shape, out, *sent, own=True, other=True):
    bins, depth, cols = blocks[0][3].shape
    rows, step = shape[2], 2
    count = len(blocks)
    chunks = [block[0] for block in blocks]
    received = [block for some, _ in sent for block in some]
    where = [block[1] for block in blocks] + [core] + [block[2] for block in received]
    held = [] if out is None else [out]
    used = [
        pl.BlockSpec((step, 4 * rows, depth), (lambda f, w: (f, 0, 0)) if chunk in chunks else (lambda f, w: (0, 0, 0)))
        for chunk in range(2)
    ]
    send = jax.ShapeDtypeStruct((count, 2, bins, rows, cols), jnp.bfloat16)
    spots = max(len(received), 1)
    return pl.pallas_call(
        functools.partial(
            gram_kernel, 2.0 / depth, chunks, [[block[0] for block in some] for some, _ in sent], own, other
        ),
        grid_spec=pltpu.PrefetchScalarGridSpec(
            num_scalar_prefetch=1,
            grid=(bins // step,),
            in_specs=used
            + [pl.BlockSpec((step, depth, cols), lambda f, w: (f, 0, 0))] * count
            + [sent_spec(results, step) for _, results in sent]
            + [pl.BlockSpec(memory_space=pl.ANY)] * len(held),
            out_specs=[pl.BlockSpec(memory_space=pl.ANY)] * (own + other),
            scratch_shapes=[
                pltpu.VMEM((2, count, own + other, 2, step, rows, cols), jnp.bfloat16),
                pltpu.VMEM((2, spots, 2, step, rows, cols), jnp.bfloat16),
                pltpu.SemaphoreType.DMA((2, count, 2)),
                pltpu.SemaphoreType.DMA((2, spots)),
            ],
        ),
        out_shape=[jax.ShapeDtypeStruct(shape, jnp.bfloat16)] * own + [send] * other,
        input_output_aliases={3 + count + len(sent): 0} if held else {},
        cost_estimate=pl.CostEstimate(
            flops=8 * count * bins * rows * depth * cols,
            bytes_accessed=2 * bins * (8 * rows * depth + count * (depth * cols + 4 * rows * cols)),
            transcendentals=0,
        ),
        compiler_params=pltpu.CompilerParams(vmem_limit_bytes=24 * MIB),
        name="gram",
    )(jnp.stack(where).astype(jnp.int32), *mine, *[block[3] for block in blocks], *[r for _, r in sent], *held)


def place_kernel(chunks, where, sent_ref, _, out_ref, sems):
    bins, cols = sent_ref.shape[2], sent_ref.shape[4]
    step, core = pl.program_id(0), where[len(chunks)]
    copies = []
    for k, chunk in enumerate(chunks):
        first = (1 - core) * 2 * CHUNK + chunk * CHUNK + step * bins
        spot = out_ref.at[:, pl.ds(first, bins), :, spot_of(where, k, cols)]
        copies.append(pltpu.make_async_copy(sent_ref.at[k], spot, sems.at[k]))
    for copy in copies:
        copy.start()
    for copy in copies:
        copy.wait()


def place(core, sent, out):
    blocks, results = sent
    return pl.pallas_call(
        functools.partial(place_kernel, [block[0] for block in blocks]),
        grid_spec=pltpu.PrefetchScalarGridSpec(
            num_scalar_prefetch=1,
            grid=(results.shape[2] // 2,),
            in_specs=[sent_spec(results, 2), pl.BlockSpec(memory_space=pl.ANY)],
            out_specs=pl.BlockSpec(memory_space=pl.ANY),
            scratch_shapes=[pltpu.SemaphoreType.DMA((len(blocks),))],
        ),
        out_shape=jax.ShapeDtypeStruct(out.shape, out.dtype),
        input_output_aliases={2: 0},
        compiler_params=pltpu.CompilerParams(vmem_limit_bytes=24 * MIB),
        name="place",
    )(jnp.stack([block[2] for block in blocks] + [core]).astype(jnp.int32), results, out)


def mirrored(step):
    return [
        (2 * x + core, (x + (1 - 2 * core) * step) % 4 * 2 + core) for x in range(4) for core in range(2)
    ]


def shards(records, available):
    stations = records.shape[0]
    x, yh, core = lax.axis_index("x"), lax.axis_index("yh"), lax.axis_index("core")
    fwd = lambda v: lax.ppermute(v, ("x", "core"), mirrored(1))
    bwd = lambda v: lax.ppermute(v, ("x", "core"), mirrored(-1))
    over = lambda v: lax.ppermute(v, "yh", [(0, 1), (1, 0)])
    swap = lambda v: lax.ppermute(v, "core", [(0, 1), (1, 0)])
    after = lambda value, *others: lax.optimization_barrier((value, *others))[0]

    def owned(chunk):
        got = lax.all_to_all(chunk, ("yl", "z", "core"), split_axis=0, concat_axis=0, tiled=True)
        got = got.reshape(OWNERS, 2, *got.shape[1:])
        return jnp.transpose(got, (2, 3, 0, 4, 1, 5)).reshape(CHUNK, -1, 2 * stations)

    def entry(chunk, dx, dy, panel):
        sign = 1 - 2 * core
        chips = [(x - way * dx) % 4 * 2 + (yh + dy) % 2 for way in (sign, -sign)]
        return chunk, *chips, panel

    shape = (2, 4 * CHUNK, stations, 16 * stations)
    first, second = whiten(records, available)
    pa = owned(first)
    na, ba = fwd(pa), bwd(pa)
    pb = owned(after(second, pa))
    ma = rows_of(pa)

    nb, bb, oa = fwd(after(pb, na)), bwd(after(pb, ba)), over(after(pa, pb))
    blocks1 = [entry(0, 0, 0, pa), entry(0, 1, 0, na), entry(0, -1, 0, ba)]
    out, sent = gram(core, (ma, ma), blocks1, shape, None)
    mine = ma, rows_of(pb)

    fa, fb, ob = fwd(after(na, nb, out)), fwd(after(nb, bb)), over(after(pb, oa))
    sent1 = blocks1, swap(sent)
    blocks2 = [entry(1, 0, 0, pb), entry(1, 1, 0, nb), entry(1, -1, 0, bb), entry(0, 0, 1, oa)]
    out, sent = gram(core, mine, blocks2, shape, out)

    boa, bob, noa = bwd(after(oa, fa, out)), bwd(after(ob, fb)), over(after(na, ob))
    sent2 = blocks2, swap(sent)
    blocks3 = [entry(0, 2, 0, fa), entry(1, 2, 0, fb), entry(1, 0, 1, ob)]
    out, sent = gram(core, mine, blocks3, shape, out, sent1)

    foa, nob, fob = fwd(after(noa, boa, out)), fwd(after(ob, bob)), over(after(fb, noa))
    sent3 = blocks3, swap(sent)
    blocks4 = [entry(0, -1, 1, boa), entry(1, -1, 1, bob), entry(0, 1, 1, noa)]
    out, sent = gram(core, mine, blocks4, shape, out, sent2)

    sent4 = blocks4, swap(sent)
    blocks5 = [entry(0, 2, 1, foa), entry(1, 1, 1, nob), entry(1, 2, 1, fob)]
    (sent,) = gram(core, mine, blocks5, shape, None, own=False)
    (out,) = gram(core, mine, blocks5, shape, out, sent3, sent4, other=False)
    return place(core, (blocks5, swap(sent)), out)


def solution(mesh):
    fine = Mesh(mesh.devices.reshape(4, 2, 2, 2, 4), ("x", "yh", "core", "yl", "z"))
    sta, freq = ("x", "yh", "core"), ("yl", "z")
    return jax.shard_map(
        shards,
        mesh=fine,
        in_specs=(P(sta, freq, None), P(sta, freq)),
        out_specs=P(None, freq, sta, None),
        check_vma=False,
    )
```

```python
import functools

import jax
import jax.numpy as jnp
import numpy as np
from jax import lax
from jax.experimental import pallas as pl
from jax.experimental.pallas import tpu as pltpu
from jax.sharding import Mesh, PartitionSpec as P

FFT_LEN = 512
BINS = 128
BAND_LO = 16
OWNERS = 8
CHUNK = 4
SEG_STEP = 8
MIB = 1024 * 1024


def spectra_table():
    sample = np.arange(FFT_LEN)
    bins = (BAND_LO + np.arange(BINS)).reshape(OWNERS, 2, 2, CHUNK).transpose(2, 0, 1, 3).reshape(-1)
    phase = (sample[:, None] * bins[None, :] % FFT_LEN) * (2.0 * np.pi / FFT_LEN)
    taper = 0.5 - 0.5 * np.cos(2.0 * np.pi * sample / FFT_LEN)
    table = np.stack([np.cos(phase), -np.sin(phase)], axis=2).reshape(FFT_LEN, 2 * BINS) * taper[:, None]
    high = table.astype(jnp.bfloat16)
    low = (table - high.astype(np.float64)).astype(jnp.bfloat16)
    return high, low


def whiten_kernel(records_ref, available_ref, high_ref, low_ref, first_ref, second_ref, rows_ref, turned_ref):
    stations, segs, samples = records_ref.shape
    flat = records_ref[...].reshape(stations * segs, samples)
    spectra = jnp.dot(flat, high_ref[...], preferred_element_type=jnp.float32)
    spectra += jnp.dot(flat, low_ref[...], preferred_element_type=jnp.float32)
    wide = spectra.shape[1]
    for part in range(2):
        rows_ref[part] = spectra[:, part * BINS : (part + 1) * BINS]
    for seg in range(segs):
        turned = jnp.concatenate(
            [rows_ref[part, pl.ds(seg, stations, stride=segs), :].T for part in range(2)], axis=0
        )
        power = jnp.sum(turned * turned, axis=0, keepdims=True) / BINS
        weight = available_ref[seg : seg + 1, :].astype(jnp.float32) / jnp.sqrt(power + 1e-05)
        turned_ref[pl.ds(seg, wide, stride=segs), :] = turned * weight
    whitened = turned_ref[...].reshape(2, 2 * OWNERS, CHUNK, 2, segs, stations).astype(jnp.bfloat16)
    first_ref[...] = whitened[0]
    second_ref[...] = whitened[1]


def whiten(records, available):
    stations, segments, samples = records.shape
    high, low = spectra_table()
    half = jax.ShapeDtypeStruct((2 * OWNERS, CHUNK, 2, segments, stations), jnp.bfloat16)
    half_spec = pl.BlockSpec((2 * OWNERS, CHUNK, 2, SEG_STEP, stations), lambda i: (0, 0, 0, i, 0))
    return pl.pallas_call(
        whiten_kernel,
        grid=(segments // SEG_STEP,),
        in_specs=[
            pl.BlockSpec((stations, SEG_STEP, samples), lambda i: (0, i, 0)),
            pl.BlockSpec((SEG_STEP, stations), lambda i: (i, 0)),
            pl.BlockSpec((samples, 2 * BINS), lambda i: (0, 0)),
            pl.BlockSpec((samples, 2 * BINS), lambda i: (0, 0)),
        ],
        out_specs=[half_spec, half_spec],
        out_shape=[half, half],
        scratch_shapes=[
            pltpu.VMEM((2, stations * SEG_STEP, BINS), jnp.float32),
            pltpu.VMEM((2 * BINS * SEG_STEP, stations), jnp.float32),
        ],
        compiler_params=pltpu.CompilerParams(vmem_limit_bytes=60 * MIB),
        name="whiten",
    )(records, available.T, jnp.asarray(high), jnp.asarray(low))


def rows_kernel(panel_ref, mine_ref):
    sources, _, depth, rows = panel_ref.shape
    panel = panel_ref[:, 0].reshape(sources // 2, 2, 2, depth // 2, rows)
    for core in range(2):
        part = panel[:, core]
        turned = jnp.stack([part[:, 1], -part[:, 0]], axis=1)
        base = 2 * rows * core
        mine_ref[0, base : base + rows] = part.reshape(-1, rows).T
        mine_ref[0, base + rows : base + 2 * rows] = turned.reshape(-1, rows).T


def rows_of(panel):
    sources, bins, depth, rows = panel.shape
    block = (1, 4 * rows, sources // 2 * depth)
    return pl.pallas_call(
        rows_kernel,
        grid=(bins,),
        in_specs=[pl.BlockSpec((sources, 1, depth, rows), lambda f: (0, f, 0, 0))],
        out_specs=pl.BlockSpec(block, lambda f: (f, 0, 0)),
        out_shape=jax.ShapeDtypeStruct((bins, *block[1:]), panel.dtype),
        compiler_params=pltpu.CompilerParams(vmem_limit_bytes=24 * MIB),
        name="rows",
    )(panel)


def spot_of(where, at, cols):
    return pl.ds(pl.multiple_of(where[at] * cols, cols), cols)


def gram_kernel(scale, chunks, placed, own, other, where, mine0_ref, mine1_ref, *refs):
    count, sets = len(chunks), len(placed)
    panels, sent, rest = refs[:count], refs[count : count + sets], refs[count + sets :]
    slots, place_slots, sems, place_sems = rest[-4:]
    out_ref, send_ref = rest[-5 - (own and other)], rest[-5]
    step, steps = pl.program_id(0), pl.num_programs(0)
    bins = mine0_ref.shape[0]
    rows, cols = mine0_ref.shape[1] // 4, 2 * panels[0].shape[3]
    slot, core = lax.rem(step, 2), where[count]
    received = [(which, at, chunk) for which, some in enumerate(placed) for at, chunk in enumerate(some)]

    def first_bin(owner, chunk, at):
        return owner * 2 * CHUNK + chunk * CHUNK + at * bins

    def writes(at, held):
        for block, chunk in enumerate(chunks):
            if own:
                spot = out_ref.at[:, pl.ds(first_bin(core, chunk, at), bins), :, spot_of(where, block, cols)]
                source = slots.at[held, block, core if other else 0]
                yield pltpu.make_async_copy(source, spot, sems.at[held, block, 0])
            if other:
                spot = send_ref.at[block, :, pl.ds(at * bins, bins)]
                source = slots.at[held, block, 1 - core if own else 0]
                yield pltpu.make_async_copy(source, spot, sems.at[held, block, 1])

    def places(at, held):
        for k, (_, _, chunk) in enumerate(received):
            spot = spot_of(where, count + 1 + k, cols)
            spot = out_ref.at[:, pl.ds(first_bin(1 - core, chunk, at), bins), :, spot]
            yield pltpu.make_async_copy(place_slots.at[held, k], spot, place_sems.at[held, k])

    @pl.when(step >= 2)
    def _():
        for copy in (*writes(step - 2, slot), *places(step - 2, slot)):
            copy.wait()

    for k, (which, at, _) in enumerate(received):
        place_slots[slot, k] = sent[which][at]
    for copy in places(step, slot):
        copy.start()
    for block, chunk in enumerate(chunks):
        mine_ref = mine1_ref if chunk else mine0_ref
        for f in range(bins):
            if own and other:
                mine = mine_ref[f]
            else:
                target = core if own else 1 - core
                mine = mine_ref[f, pl.ds(pl.multiple_of(target * 2 * rows, 2 * rows), 2 * rows), :]
            panel = panels[block][:, f].reshape(-1, 2, *panels[block].shape[2:])
            panel = jnp.concatenate([panel[:, side].reshape(-1, rows) for side in range(2)], axis=1)
            gram = jnp.dot(mine, panel, preferred_element_type=jnp.float32) * scale
            gram = gram.astype(jnp.bfloat16)
            for target in range(own + other):
                for part in range(2):
                    base = (2 * target + part) * rows
                    slots[slot, block, target, part, f] = gram[base : base + rows]
    for copy in writes(step, slot):
        copy.start()

    @pl.when(step == steps - 1)
    def _():
        for copy in (*writes(step - 1, 1 - slot), *places(step - 1, 1 - slot)):
            copy.wait()
        for copy in (*writes(step, slot), *places(step, slot)):
            copy.wait()


def sent_spec(results, step):
    block = (results.shape[0], 2, step, *results.shape[3:])
    return pl.BlockSpec(block, lambda f, w: (0, 0, f, 0, 0))


def gram(core, mine, blocks, shape, out, *sent, own=True, other=True):
    sources, bins, part, rows = blocks[0][3].shape
    depth, cols, step = sources // 2 * part, 2 * rows, 2
    count = len(blocks)
    chunks = [block[0] for block in blocks]
    received = [block for some, _ in sent for block in some]
    where = [block[1] for block in blocks] + [core] + [block[2] for block in received]
    held = [] if out is None else [out]
    used = [
        pl.BlockSpec((step, 4 * rows, depth), (lambda f, w: (f, 0, 0)) if chunk in chunks else (lambda f, w: (0, 0, 0)))
        for chunk in range(2)
    ]
    send = jax.ShapeDtypeStruct((count, 2, bins, rows, cols), jnp.bfloat16)
    spots = max(len(received), 1)
    return pl.pallas_call(
        functools.partial(
            gram_kernel, 2.0 / depth, chunks, [[block[0] for block in some] for some, _ in sent], own, other
        ),
        grid_spec=pltpu.PrefetchScalarGridSpec(
            num_scalar_prefetch=1,
            grid=(bins // step,),
            in_specs=used
            + [pl.BlockSpec((sources, step, part, rows), lambda f, w: (0, f, 0, 0))] * count
            + [sent_spec(results, step) for _, results in sent]
            + [pl.BlockSpec(memory_space=pl.ANY)] * len(held),
            out_specs=[pl.BlockSpec(memory_space=pl.ANY)] * (own + other),
            scratch_shapes=[
                pltpu.VMEM((2, count, own + other, 2, step, rows, cols), jnp.bfloat16),
                pltpu.VMEM((2, spots, 2, step, rows, cols), jnp.bfloat16),
                pltpu.SemaphoreType.DMA((2, count, 2)),
                pltpu.SemaphoreType.DMA((2, spots)),
            ],
        ),
        out_shape=[jax.ShapeDtypeStruct(shape, jnp.bfloat16)] * own + [send] * other,
        input_output_aliases={3 + count + len(sent): 0} if held else {},
        cost_estimate=pl.CostEstimate(
            flops=8 * count * bins * rows * depth * cols,
            bytes_accessed=2 * bins * (8 * rows * depth + count * (depth * cols + 4 * rows * cols)),
            transcendentals=0,
        ),
        compiler_params=pltpu.CompilerParams(vmem_limit_bytes=24 * MIB),
        name="gram",
    )(jnp.stack(where).astype(jnp.int32), *mine, *[block[3] for block in blocks], *[r for _, r in sent], *held)


def place_kernel(chunks, where, sent_ref, _, out_ref, sems):
    bins, cols = sent_ref.shape[2], sent_ref.shape[4]
    step, core = pl.program_id(0), where[len(chunks)]
    copies = []
    for k, chunk in enumerate(chunks):
        first = (1 - core) * 2 * CHUNK + chunk * CHUNK + step * bins
        spot = out_ref.at[:, pl.ds(first, bins), :, spot_of(where, k, cols)]
        copies.append(pltpu.make_async_copy(sent_ref.at[k], spot, sems.at[k]))
    for copy in copies:
        copy.start()
    for copy in copies:
        copy.wait()


def place(core, sent, out):
    blocks, results = sent
    return pl.pallas_call(
        functools.partial(place_kernel, [block[0] for block in blocks]),
        grid_spec=pltpu.PrefetchScalarGridSpec(
            num_scalar_prefetch=1,
            grid=(results.shape[2] // 2,),
            in_specs=[sent_spec(results, 2), pl.BlockSpec(memory_space=pl.ANY)],
            out_specs=pl.BlockSpec(memory_space=pl.ANY),
            scratch_shapes=[pltpu.SemaphoreType.DMA((len(blocks),))],
        ),
        out_shape=jax.ShapeDtypeStruct(out.shape, out.dtype),
        input_output_aliases={2: 0},
        compiler_params=pltpu.CompilerParams(vmem_limit_bytes=24 * MIB),
        name="place",
    )(jnp.stack([block[2] for block in blocks] + [core]).astype(jnp.int32), results, out)


def mirrored(step):
    return [
        (2 * x + core, (x + (1 - 2 * core) * step) % 4 * 2 + core) for x in range(4) for core in range(2)
    ]


def shards(records, available):
    stations = records.shape[0]
    x, yh, core = lax.axis_index("x"), lax.axis_index("yh"), lax.axis_index("core")
    fwd = lambda v: lax.ppermute(v, ("x", "core"), mirrored(1))
    bwd = lambda v: lax.ppermute(v, ("x", "core"), mirrored(-1))
    over = lambda v: lax.ppermute(v, "yh", [(0, 1), (1, 0)])
    swap = lambda v: lax.ppermute(v, "core", [(0, 1), (1, 0)])
    after = lambda value, *others: lax.optimization_barrier((value, *others))[0]

    def owned(chunk):
        got = lax.all_to_all(chunk, ("yl", "z", "core"), split_axis=0, concat_axis=0, tiled=True)
        return got.reshape(2 * OWNERS, CHUNK, -1, stations)

    def entry(chunk, dx, dy, panel):
        sign = 1 - 2 * core
        chips = [(x - way * dx) % 4 * 2 + (yh + dy) % 2 for way in (sign, -sign)]
        return chunk, *chips, panel

    shape = (2, 4 * CHUNK, stations, 16 * stations)
    first, second = whiten(records, available)
    pa = owned(first)
    na, ba = fwd(pa), bwd(pa)
    pb = owned(after(second, pa))
    ma = rows_of(pa)

    nb, bb, oa = fwd(after(pb, na)), bwd(after(pb, ba)), over(after(pa, pb))
    blocks1 = [entry(0, 0, 0, pa), entry(0, 1, 0, na), entry(0, -1, 0, ba)]
    out, sent = gram(core, (ma, ma), blocks1, shape, None)
    mine = ma, rows_of(pb)

    fa, fb, ob = fwd(after(na, nb, out)), fwd(after(nb, bb)), over(after(pb, oa))
    sent1 = blocks1, swap(sent)
    blocks2 = [entry(1, 0, 0, pb), entry(1, 1, 0, nb), entry(1, -1, 0, bb), entry(0, 0, 1, oa)]
    out, sent = gram(core, mine, blocks2, shape, out)

    boa, bob, noa = bwd(after(oa, fa, out)), bwd(after(ob, fb)), over(after(na, ob))
    sent2 = blocks2, swap(sent)
    blocks3 = [entry(0, 2, 0, fa), entry(1, 2, 0, fb), entry(1, 0, 1, ob)]
    out, sent = gram(core, mine, blocks3, shape, out, sent1)

    foa, nob, fob = fwd(after(noa, boa, out)), fwd(after(ob, bob)), over(after(fb, noa))
    sent3 = blocks3, swap(sent)
    blocks4 = [entry(0, -1, 1, boa), entry(1, -1, 1, bob), entry(0, 1, 1, noa)]
    out, sent = gram(core, mine, blocks4, shape, out, sent2)

    sent4 = blocks4, swap(sent)
    blocks5 = [entry(0, 2, 1, foa)]
    out, sent = gram(core, mine, blocks5, shape, out, sent3)

    sent5 = blocks5, swap(sent)
    blocks6 = [entry(1, 1, 1, after(nob, out)), entry(1, 2, 1, fob)]
    (sent,) = gram(core, mine, blocks6, shape, None, own=False)
    (out,) = gram(core, mine, blocks6, shape, out, sent4, sent5, other=False)
    return place(core, (blocks6, swap(sent)), out)


def solution(mesh):
    fine = Mesh(mesh.devices.reshape(4, 2, 2, 2, 4), ("x", "yh", "core", "yl", "z"))
    sta, freq = ("x", "yh", "core"), ("yl", "z")
    return jax.shard_map(
        shards,
        mesh=fine,
        in_specs=(P(sta, freq, None), P(sta, freq)),
        out_specs=P(None, freq, sta, None),
        check_vma=False,
    )
```

```python
import functools

import jax
import jax.numpy as jnp
import numpy as np
from jax import lax
from jax.experimental import pallas as pl
from jax.experimental.pallas import tpu as pltpu
from jax.sharding import Mesh, PartitionSpec as P

FFT_LEN = 512
BINS = 128
BAND_LO = 16
OWNERS = 8
CHUNK = 4
SEG_STEP = 8
MIB = 1024 * 1024


def spectra_table():
    sample = np.arange(FFT_LEN)
    bins = (BAND_LO + np.arange(BINS)).reshape(OWNERS, 2, 2, CHUNK).transpose(2, 0, 1, 3).reshape(-1)
    phase = (sample[:, None] * bins[None, :] % FFT_LEN) * (2.0 * np.pi / FFT_LEN)
    taper = 0.5 - 0.5 * np.cos(2.0 * np.pi * sample / FFT_LEN)
    table = np.stack([np.cos(phase), -np.sin(phase)], axis=2).reshape(FFT_LEN, 2 * BINS) * taper[:, None]
    high = table.astype(jnp.bfloat16)
    low = (table - high.astype(np.float64)).astype(jnp.bfloat16)
    return high, low


def whiten_kernel(records_ref, available_ref, high_ref, low_ref, first_ref, second_ref, rows_ref, turned_ref):
    stations, segs, samples = records_ref.shape
    flat = records_ref[...].reshape(stations * segs, samples)
    spectra = jnp.dot(flat, high_ref[...], preferred_element_type=jnp.float32)
    spectra += jnp.dot(flat, low_ref[...], preferred_element_type=jnp.float32)
    wide = spectra.shape[1]
    for part in range(2):
        rows_ref[part] = spectra[:, part * BINS : (part + 1) * BINS]
    for seg in range(segs):
        turned = jnp.concatenate(
            [rows_ref[part, pl.ds(seg, stations, stride=segs), :].T for part in range(2)], axis=0
        )
        power = jnp.sum(turned * turned, axis=0, keepdims=True) / BINS
        weight = available_ref[seg : seg + 1, :].astype(jnp.float32) / jnp.sqrt(power + 1e-05)
        turned_ref[pl.ds(seg, wide, stride=segs), :] = turned * weight
    whitened = turned_ref[...].reshape(2, 2 * OWNERS, CHUNK, 2, segs, stations).astype(jnp.bfloat16)
    first_ref[...] = whitened[0]
    second_ref[...] = whitened[1]


def whiten(records, available):
    stations, segments, samples = records.shape
    high, low = spectra_table()
    half = jax.ShapeDtypeStruct((2 * OWNERS, CHUNK, 2, segments, stations), jnp.bfloat16)
    half_spec = pl.BlockSpec((2 * OWNERS, CHUNK, 2, SEG_STEP, stations), lambda i: (0, 0, 0, i, 0))
    return pl.pallas_call(
        whiten_kernel,
        grid=(segments // SEG_STEP,),
        in_specs=[
            pl.BlockSpec((stations, SEG_STEP, samples), lambda i: (0, i, 0)),
            pl.BlockSpec((SEG_STEP, stations), lambda i: (i, 0)),
            pl.BlockSpec((samples, 2 * BINS), lambda i: (0, 0)),
            pl.BlockSpec((samples, 2 * BINS), lambda i: (0, 0)),
        ],
        out_specs=[half_spec, half_spec],
        out_shape=[half, half],
        scratch_shapes=[
            pltpu.VMEM((2, stations * SEG_STEP, BINS), jnp.float32),
            pltpu.VMEM((2 * BINS * SEG_STEP, stations), jnp.float32),
        ],
        compiler_params=pltpu.CompilerParams(vmem_limit_bytes=60 * MIB),
        name="whiten",
    )(records, available.T, jnp.asarray(high), jnp.asarray(low))


def rows_kernel(panel_ref, mine_ref):
    sources, _, depth, rows = panel_ref.shape
    panel = panel_ref[:, 0].reshape(sources // 2, 2, 2, depth // 2, rows)
    for core in range(2):
        part = panel[:, core]
        turned = jnp.stack([part[:, 1], -part[:, 0]], axis=1)
        base = 2 * rows * core
        mine_ref[0, base : base + rows] = part.reshape(-1, rows).T
        mine_ref[0, base + rows : base + 2 * rows] = turned.reshape(-1, rows).T


def rows_of(panel):
    sources, bins, depth, rows = panel.shape
    block = (1, 4 * rows, sources // 2 * depth)
    return pl.pallas_call(
        rows_kernel,
        grid=(bins,),
        in_specs=[pl.BlockSpec((sources, 1, depth, rows), lambda f: (0, f, 0, 0))],
        out_specs=pl.BlockSpec(block, lambda f: (f, 0, 0)),
        out_shape=pltpu.HBM((bins, *block[1:]), panel.dtype),
        compiler_params=pltpu.CompilerParams(vmem_limit_bytes=24 * MIB),
        name="rows",
    )(panel)


def spot_of(where, at, cols):
    return pl.ds(pl.multiple_of(where[at] * cols, cols), cols)


def gram_kernel(scale, chunks, placed, own, other, where, mine0_ref, mine1_ref, *refs):
    count, sets = len(chunks), len(placed)
    panels, sent, rest = refs[:count], refs[count : count + sets], refs[count + sets :]
    slots, place_slots, sems, place_sems = rest[-4:]
    out_ref, send_ref = rest[-5 - (own and other)], rest[-5]
    step, steps = pl.program_id(0), pl.num_programs(0)
    bins = mine0_ref.shape[0]
    rows, cols = mine0_ref.shape[1] // 4, 2 * panels[0].shape[3]
    slot, core = lax.rem(step, 2), where[count]
    received = [(which, at, chunk) for which, some in enumerate(placed) for at, chunk in enumerate(some)]

    def first_bin(owner, chunk, at):
        return owner * 2 * CHUNK + chunk * CHUNK + at * bins

    def writes(at, held):
        for block, chunk in enumerate(chunks):
            if own:
                spot = out_ref.at[:, pl.ds(first_bin(core, chunk, at), bins), :, spot_of(where, block, cols)]
                source = slots.at[held, block, core if other else 0]
                yield pltpu.make_async_copy(source, spot, sems.at[held, block, 0])
            if other:
                spot = send_ref.at[block, :, pl.ds(at * bins, bins)]
                source = slots.at[held, block, 1 - core if own else 0]
                yield pltpu.make_async_copy(source, spot, sems.at[held, block, 1])

    def places(at, held):
        for k, (_, _, chunk) in enumerate(received):
            spot = spot_of(where, count + 1 + k, cols)
            spot = out_ref.at[:, pl.ds(first_bin(1 - core, chunk, at), bins), :, spot]
            yield pltpu.make_async_copy(place_slots.at[held, k], spot, place_sems.at[held, k])

    @pl.when(step >= 2)
    def _():
        for copy in (*writes(step - 2, slot), *places(step - 2, slot)):
            copy.wait()

    for k, (which, at, _) in enumerate(received):
        place_slots[slot, k] = sent[which][at]
    for copy in places(step, slot):
        copy.start()
    for block, chunk in enumerate(chunks):
        mine_ref = mine1_ref if chunk else mine0_ref
        for f in range(bins):
            if own and other:
                mine = mine_ref[f]
            else:
                target = core if own else 1 - core
                mine = mine_ref[f, pl.ds(pl.multiple_of(target * 2 * rows, 2 * rows), 2 * rows), :]
            panel = panels[block][:, f].reshape(-1, 2, *panels[block].shape[2:])
            panel = jnp.concatenate([panel[:, side].reshape(-1, rows) for side in range(2)], axis=1)
            gram = jnp.dot(mine, panel, preferred_element_type=jnp.float32) * scale
            gram = gram.astype(jnp.bfloat16)
            for target in range(own + other):
                for part in range(2):
                    base = (2 * target + part) * rows
                    slots[slot, block, target, part, f] = gram[base : base + rows]
    for copy in writes(step, slot):
        copy.start()

    @pl.when(step == steps - 1)
    def _():
        for copy in (*writes(step - 1, 1 - slot), *places(step - 1, 1 - slot)):
            copy.wait()
        for copy in (*writes(step, slot), *places(step, slot)):
            copy.wait()


def far(value):
    return pltpu.with_memory_space_constraint(value, pltpu.HBM)


def sent_spec(results, step):
    block = (results.shape[0], 2, step, *results.shape[3:])
    return pl.BlockSpec(block, lambda f, w: (0, 0, f, 0, 0))


def gram(core, mine, blocks, shape, out, *sent, own=True, other=True):
    sources, bins, part, rows = blocks[0][3].shape
    depth, cols, step = sources // 2 * part, 2 * rows, 2
    count = len(blocks)
    chunks = [block[0] for block in blocks]
    received = [block for some, _ in sent for block in some]
    where = [block[1] for block in blocks] + [core] + [block[2] for block in received]
    held = [] if out is None else [out]
    used = [
        pl.BlockSpec((step, 4 * rows, depth), (lambda f, w: (f, 0, 0)) if chunk in chunks else (lambda f, w: (0, 0, 0)))
        for chunk in range(2)
    ]
    send = jax.ShapeDtypeStruct((count, 2, bins, rows, cols), jnp.bfloat16)
    spots = max(len(received), 1)
    return pl.pallas_call(
        functools.partial(
            gram_kernel, 2.0 / depth, chunks, [[block[0] for block in some] for some, _ in sent], own, other
        ),
        grid_spec=pltpu.PrefetchScalarGridSpec(
            num_scalar_prefetch=1,
            grid=(bins // step,),
            in_specs=used
            + [pl.BlockSpec((sources, step, part, rows), lambda f, w: (0, f, 0, 0))] * count
            + [sent_spec(results, step) for _, results in sent]
            + [pl.BlockSpec(memory_space=pl.ANY)] * len(held),
            out_specs=[pl.BlockSpec(memory_space=pl.ANY)] * (own + other),
            scratch_shapes=[
                pltpu.VMEM((2, count, own + other, 2, step, rows, cols), jnp.bfloat16),
                pltpu.VMEM((2, spots, 2, step, rows, cols), jnp.bfloat16),
                pltpu.SemaphoreType.DMA((2, count, 2)),
                pltpu.SemaphoreType.DMA((2, spots)),
            ],
        ),
        out_shape=[jax.ShapeDtypeStruct(shape, jnp.bfloat16)] * own + [send] * other,
        input_output_aliases={3 + count + len(sent): 0} if held else {},
        cost_estimate=pl.CostEstimate(
            flops=8 * count * bins * rows * depth * cols,
            bytes_accessed=2 * bins * (8 * rows * depth + count * (depth * cols + 4 * rows * cols)),
            transcendentals=0,
        ),
        compiler_params=pltpu.CompilerParams(vmem_limit_bytes=24 * MIB),
        name="gram",
    )(jnp.stack(where).astype(jnp.int32), *map(far, mine), *[block[3] for block in blocks], *[r for _, r in sent], *held)


def place_kernel(placed, where, *refs):
    sent, (out_ref, sems) = refs[: len(placed)], refs[-2:]
    step, count = pl.program_id(0), sum(map(len, placed))
    core, copies = where[count], []
    for which, chunks in enumerate(placed):
        bins, cols = sent[which].shape[2], sent[which].shape[4]
        for at, chunk in enumerate(chunks):
            first = (1 - core) * 2 * CHUNK + chunk * CHUNK + step * bins
            spot = out_ref.at[:, pl.ds(first, bins), :, spot_of(where, len(copies), cols)]
            copies.append(pltpu.make_async_copy(sent[which].at[at], spot, sems.at[len(copies)]))
    for copy in copies:
        copy.start()
    for copy in copies:
        copy.wait()


def place(core, out, *sent):
    received = [block for blocks, _ in sent for block in blocks]
    return pl.pallas_call(
        functools.partial(place_kernel, [[block[0] for block in blocks] for blocks, _ in sent]),
        grid_spec=pltpu.PrefetchScalarGridSpec(
            num_scalar_prefetch=1,
            grid=(CHUNK // 2,),
            in_specs=[sent_spec(results, 2) for _, results in sent] + [pl.BlockSpec(memory_space=pl.ANY)],
            out_specs=pl.BlockSpec(memory_space=pl.ANY),
            scratch_shapes=[pltpu.SemaphoreType.DMA((len(received),))],
        ),
        out_shape=jax.ShapeDtypeStruct(out.shape, out.dtype),
        input_output_aliases={1 + len(sent): 0},
        compiler_params=pltpu.CompilerParams(vmem_limit_bytes=24 * MIB),
        name="place",
    )(jnp.stack([block[2] for block in received] + [core]).astype(jnp.int32), *[r for _, r in sent], out)


def mirrored(step):
    return [
        (2 * x + core, (x + (1 - 2 * core) * step) % 4 * 2 + core) for x in range(4) for core in range(2)
    ]


def shards(records, available):
    stations = records.shape[0]
    x, yh, core = lax.axis_index("x"), lax.axis_index("yh"), lax.axis_index("core")
    fwd = lambda v: lax.ppermute(v, ("x", "core"), mirrored(1))
    bwd = lambda v: lax.ppermute(v, ("x", "core"), mirrored(-1))
    over = lambda v: lax.ppermute(v, "yh", [(0, 1), (1, 0)])
    swap = lambda v: lax.ppermute(v, "core", [(0, 1), (1, 0)])
    after = lambda value, *others: lax.optimization_barrier((value, *others))[0]

    def owned(chunk):
        got = lax.all_to_all(chunk, ("yl", "z", "core"), split_axis=0, concat_axis=0, tiled=True)
        return got.reshape(2 * OWNERS, CHUNK, -1, stations)

    def entry(chunk, dx, dy, panel):
        sign = 1 - 2 * core
        chips = [(x - way * dx) % 4 * 2 + (yh + dy) % 2 for way in (sign, -sign)]
        return chunk, *chips, panel

    shape = (2, 4 * CHUNK, stations, 16 * stations)
    first, second = whiten(records, available)
    pa = owned(first)
    na, ba = fwd(pa), bwd(pa)
    pb = owned(after(second, pa))
    ma = rows_of(pa)

    fa, nb, oa = fwd(after(na, pb)), fwd(after(pb, na)), over(after(pa, pb))
    blocks1 = [entry(0, 0, 0, pa), entry(0, 1, 0, na), entry(0, -1, 0, ba)]
    out, sent = gram(core, (ma, ma), blocks1, shape, None)
    mine = ma, rows_of(pb)

    bb, fb, ob = bwd(after(pb, fa, out)), fwd(after(nb, out)), over(after(pb, oa, fa))
    sent1 = blocks1, swap(sent)
    blocks2 = [entry(1, 0, 0, pb), entry(0, 2, 0, fa), entry(1, 1, 0, nb), entry(0, 0, 1, oa)]
    out, sent = gram(core, mine, blocks2, shape, out)

    boa, bob, noa = bwd(after(oa, bb, out)), bwd(after(ob, fb)), over(after(na, ob, bb))
    sent2 = blocks2, swap(sent)
    blocks3 = [entry(1, -1, 0, bb), entry(1, 2, 0, fb), entry(1, 0, 1, ob)]
    out, sent = gram(core, mine, blocks3, shape, out, sent1)

    nob, foa, fob = fwd(after(ob, boa, out)), fwd(after(noa, bob)), over(after(fb, noa, boa))
    sent3 = blocks3, swap(sent)
    blocks4 = [entry(0, -1, 1, boa), entry(1, -1, 1, bob), entry(0, 1, 1, noa)]
    out, sent = gram(core, mine, blocks4, shape, out, sent2)

    sent4 = blocks4, swap(sent)
    blocks5 = [entry(1, 1, 1, nob)]
    out, sent = gram(core, mine, blocks5, shape, out, sent3)

    sent5 = blocks5, swap(sent)
    blocks6 = [entry(0, 2, 1, after(foa, out)), entry(1, 2, 1, fob)]
    (sent,) = gram(core, mine, blocks6, shape, None, own=False)
    (out,) = gram(core, mine, blocks6, shape, out, sent4, other=False)
    return place(core, out, sent5, (blocks6, swap(sent)))


def solution(mesh):
    fine = Mesh(mesh.devices.reshape(4, 2, 2, 2, 4), ("x", "yh", "core", "yl", "z"))
    sta, freq = ("x", "yh", "core"), ("yl", "z")
    return jax.shard_map(
        shards,
        mesh=fine,
        in_specs=(P(sta, freq, None), P(sta, freq)),
        out_specs=P(None, freq, sta, None),
        check_vma=False,
    )
```

```python
import functools

import jax
import jax.numpy as jnp
import numpy as np
from jax import lax
from jax.experimental import pallas as pl
from jax.experimental.pallas import tpu as pltpu
from jax.sharding import Mesh, PartitionSpec as P

FFT_LEN = 512
BINS = 128
BAND_LO = 16
OWNERS = 8
CHUNK = 4
SEG_STEP = 8
MIB = 1024 * 1024


def spectra_table():
    sample = np.arange(FFT_LEN)
    bins = (BAND_LO + np.arange(BINS)).reshape(OWNERS, 2, 2, CHUNK).transpose(2, 0, 1, 3).reshape(-1)
    phase = (sample[:, None] * bins[None, :] % FFT_LEN) * (2.0 * np.pi / FFT_LEN)
    taper = 0.5 - 0.5 * np.cos(2.0 * np.pi * sample / FFT_LEN)
    table = np.stack([np.cos(phase), -np.sin(phase)], axis=2).reshape(FFT_LEN, 2 * BINS) * taper[:, None]
    high = table.astype(jnp.bfloat16)
    low = (table - high.astype(np.float64)).astype(jnp.bfloat16)
    return high, low


def whiten_kernel(records_ref, available_ref, high_ref, low_ref, first_ref, second_ref, rows_ref, turned_ref):
    stations, segs, samples = records_ref.shape
    flat = records_ref[...].reshape(stations * segs, samples)
    spectra = jnp.dot(flat, high_ref[...], preferred_element_type=jnp.float32)
    spectra += jnp.dot(flat, low_ref[...], preferred_element_type=jnp.float32)
    wide = spectra.shape[1]
    for part in range(2):
        rows_ref[part] = spectra[:, part * BINS : (part + 1) * BINS]
    for seg in range(segs):
        turned = jnp.concatenate(
            [rows_ref[part, pl.ds(seg, stations, stride=segs), :].T for part in range(2)], axis=0
        )
        power = jnp.sum(turned * turned, axis=0, keepdims=True) / BINS
        weight = available_ref[seg : seg + 1, :].astype(jnp.float32) / jnp.sqrt(power + 1e-05)
        turned_ref[pl.ds(seg, wide, stride=segs), :] = turned * weight
    whitened = turned_ref[...].reshape(2, 2 * OWNERS, CHUNK, 2, segs, stations).astype(jnp.bfloat16)
    first_ref[...] = whitened[0]
    second_ref[...] = whitened[1]


def whiten(records, available):
    stations, segments, samples = records.shape
    high, low = spectra_table()
    half = jax.ShapeDtypeStruct((2 * OWNERS, CHUNK, 2, segments, stations), jnp.bfloat16)
    half_spec = pl.BlockSpec((2 * OWNERS, CHUNK, 2, SEG_STEP, stations), lambda i: (0, 0, 0, i, 0))
    return pl.pallas_call(
        whiten_kernel,
        grid=(segments // SEG_STEP,),
        in_specs=[
            pl.BlockSpec((stations, SEG_STEP, samples), lambda i: (0, i, 0)),
            pl.BlockSpec((SEG_STEP, stations), lambda i: (i, 0)),
            pl.BlockSpec((samples, 2 * BINS), lambda i: (0, 0)),
            pl.BlockSpec((samples, 2 * BINS), lambda i: (0, 0)),
        ],
        out_specs=[half_spec, half_spec],
        out_shape=[half, half],
        scratch_shapes=[
            pltpu.VMEM((2, stations * SEG_STEP, BINS), jnp.float32),
            pltpu.VMEM((2 * BINS * SEG_STEP, stations), jnp.float32),
        ],
        compiler_params=pltpu.CompilerParams(vmem_limit_bytes=60 * MIB),
        name="whiten",
    )(records, available.T, jnp.asarray(high), jnp.asarray(low))


def rows_kernel(panel_ref, mine_ref):
    sources, _, depth, rows = panel_ref.shape
    panel = panel_ref[:, 0].reshape(sources // 2, 2, 2, depth // 2, rows)
    for core in range(2):
        part = panel[:, core]
        turned = jnp.stack([part[:, 1], -part[:, 0]], axis=1)
        base = 2 * rows * core
        mine_ref[0, base : base + rows] = part.reshape(-1, rows).T
        mine_ref[0, base + rows : base + 2 * rows] = turned.reshape(-1, rows).T


def rows_of(panel):
    sources, bins, depth, rows = panel.shape
    block = (1, 4 * rows, sources // 2 * depth)
    return pl.pallas_call(
        rows_kernel,
        grid=(bins,),
        in_specs=[pl.BlockSpec((sources, 1, depth, rows), lambda f: (0, f, 0, 0))],
        out_specs=pl.BlockSpec(block, lambda f: (f, 0, 0)),
        out_shape=pltpu.HBM((bins, *block[1:]), panel.dtype),
        compiler_params=pltpu.CompilerParams(vmem_limit_bytes=24 * MIB),
        name="rows",
    )(panel)


def spot_of(where, at, cols):
    return pl.ds(pl.multiple_of(where[at] * cols, cols), cols)


def gram_kernel(scale, chunks, placed, own, other, where, mine0_ref, mine1_ref, *refs):
    count, sets = len(chunks), len(placed)
    panels, sent, rest = refs[:count], refs[count : count + sets], refs[count + sets :]
    slots, place_slots, sems, place_sems = rest[-4:]
    out_ref, send_ref = rest[-5 - (own and other)], rest[-5]
    step, steps = pl.program_id(0), pl.num_programs(0)
    bins = mine0_ref.shape[0]
    rows, cols = mine0_ref.shape[1] // 4, 2 * panels[0].shape[3]
    slot, core = lax.rem(step, 2), where[count]
    received = [(which, at, chunk) for which, some in enumerate(placed) for at, chunk in enumerate(some)]

    def first_bin(owner, chunk, at):
        return owner * 2 * CHUNK + chunk * CHUNK + at * bins

    def writes(at, held):
        for block, chunk in enumerate(chunks):
            if own:
                spot = out_ref.at[:, pl.ds(first_bin(core, chunk, at), bins), :, spot_of(where, block, cols)]
                source = slots.at[held, block, core if other else 0]
                yield pltpu.make_async_copy(source, spot, sems.at[held, block, 0])
            if other:
                spot = send_ref.at[block, :, pl.ds(at * bins, bins)]
                source = slots.at[held, block, 1 - core if own else 0]
                yield pltpu.make_async_copy(source, spot, sems.at[held, block, 1])

    def places(at, held):
        for k, (_, _, chunk) in enumerate(received):
            spot = spot_of(where, count + 1 + k, cols)
            spot = out_ref.at[:, pl.ds(first_bin(1 - core, chunk, at), bins), :, spot]
            yield pltpu.make_async_copy(place_slots.at[held, k], spot, place_sems.at[held, k])

    @pl.when(step >= 2)
    def _():
        for copy in (*writes(step - 2, slot), *places(step - 2, slot)):
            copy.wait()

    for k, (which, at, _) in enumerate(received):
        place_slots[slot, k] = sent[which][at]
    for copy in places(step, slot):
        copy.start()
    for block, chunk in enumerate(chunks):
        mine_ref = mine1_ref if chunk else mine0_ref
        for f in range(bins):
            if own and other:
                mine = mine_ref[f]
            else:
                target = core if own else 1 - core
                mine = mine_ref[f, pl.ds(pl.multiple_of(target * 2 * rows, 2 * rows), 2 * rows), :]
            panel = panels[block][:, f].reshape(-1, 2, *panels[block].shape[2:])
            panel = jnp.concatenate([panel[:, side].reshape(-1, rows) for side in range(2)], axis=1)
            gram = jnp.dot(mine, panel, preferred_element_type=jnp.float32) * scale
            gram = gram.astype(jnp.bfloat16)
            for target in range(own + other):
                for part in range(2):
                    base = (2 * target + part) * rows
                    slots[slot, block, target, part, f] = gram[base : base + rows]
    for copy in writes(step, slot):
        copy.start()

    @pl.when(step == steps - 1)
    def _():
        for copy in (*writes(step - 1, 1 - slot), *places(step - 1, 1 - slot)):
            copy.wait()
        for copy in (*writes(step, slot), *places(step, slot)):
            copy.wait()


def far(value):
    return pltpu.with_memory_space_constraint(value, pltpu.HBM)


def sent_spec(results, step):
    block = (results.shape[0], 2, step, *results.shape[3:])
    return pl.BlockSpec(block, lambda f, w: (0, 0, f, 0, 0))


def gram(core, mine, blocks, shape, out, *sent, own=True, other=True):
    sources, bins, part, rows = blocks[0][3].shape
    depth, cols, step = sources // 2 * part, 2 * rows, 2
    count = len(blocks)
    chunks = [block[0] for block in blocks]
    received = [block for some, _ in sent for block in some]
    where = [block[1] for block in blocks] + [core] + [block[2] for block in received]
    held = [] if out is None else [out]
    used = [
        pl.BlockSpec((step, 4 * rows, depth), (lambda f, w: (f, 0, 0)) if chunk in chunks else (lambda f, w: (0, 0, 0)))
        for chunk in range(2)
    ]
    send = jax.ShapeDtypeStruct((count, 2, bins, rows, cols), jnp.bfloat16)
    spots = max(len(received), 1)
    return pl.pallas_call(
        functools.partial(
            gram_kernel, 2.0 / depth, chunks, [[block[0] for block in some] for some, _ in sent], own, other
        ),
        grid_spec=pltpu.PrefetchScalarGridSpec(
            num_scalar_prefetch=1,
            grid=(bins // step,),
            in_specs=used
            + [pl.BlockSpec((sources, step, part, rows), lambda f, w: (0, f, 0, 0))] * count
            + [sent_spec(results, step) for _, results in sent]
            + [pl.BlockSpec(memory_space=pl.ANY)] * len(held),
            out_specs=[pl.BlockSpec(memory_space=pl.ANY)] * (own + other),
            scratch_shapes=[
                pltpu.VMEM((2, count, own + other, 2, step, rows, cols), jnp.bfloat16),
                pltpu.VMEM((2, spots, 2, step, rows, cols), jnp.bfloat16),
                pltpu.SemaphoreType.DMA((2, count, 2)),
                pltpu.SemaphoreType.DMA((2, spots)),
            ],
        ),
        out_shape=[jax.ShapeDtypeStruct(shape, jnp.bfloat16)] * own + [send] * other,
        input_output_aliases={3 + count + len(sent): 0} if held else {},
        cost_estimate=pl.CostEstimate(
            flops=8 * count * bins * rows * depth * cols,
            bytes_accessed=2 * bins * (8 * rows * depth + count * (depth * cols + 4 * rows * cols)),
            transcendentals=0,
        ),
        compiler_params=pltpu.CompilerParams(vmem_limit_bytes=24 * MIB),
        name="gram",
    )(jnp.stack(where).astype(jnp.int32), *map(far, mine), *[block[3] for block in blocks], *[r for _, r in sent], *held)


def place_kernel(placed, where, *refs):
    sent, (out_ref, sems) = refs[: len(placed)], refs[-2:]
    step, count = pl.program_id(0), sum(map(len, placed))
    core, copies = where[count], []
    for which, chunks in enumerate(placed):
        bins, cols = sent[which].shape[2], sent[which].shape[4]
        for at, chunk in enumerate(chunks):
            first = (1 - core) * 2 * CHUNK + chunk * CHUNK + step * bins
            spot = out_ref.at[:, pl.ds(first, bins), :, spot_of(where, len(copies), cols)]
            copies.append(pltpu.make_async_copy(sent[which].at[at], spot, sems.at[len(copies)]))
    for copy in copies:
        copy.start()
    for copy in copies:
        copy.wait()


def place(core, out, *sent):
    received = [block for blocks, _ in sent for block in blocks]
    return pl.pallas_call(
        functools.partial(place_kernel, [[block[0] for block in blocks] for blocks, _ in sent]),
        grid_spec=pltpu.PrefetchScalarGridSpec(
            num_scalar_prefetch=1,
            grid=(CHUNK // 2,),
            in_specs=[sent_spec(results, 2) for _, results in sent] + [pl.BlockSpec(memory_space=pl.ANY)],
            out_specs=pl.BlockSpec(memory_space=pl.ANY),
            scratch_shapes=[pltpu.SemaphoreType.DMA((len(received),))],
        ),
        out_shape=jax.ShapeDtypeStruct(out.shape, out.dtype),
        input_output_aliases={1 + len(sent): 0},
        compiler_params=pltpu.CompilerParams(vmem_limit_bytes=24 * MIB),
        name="place",
    )(jnp.stack([block[2] for block in received] + [core]).astype(jnp.int32), *[r for _, r in sent], out)


def mirrored(step):
    return [
        (2 * x + core, (x + (1 - 2 * core) * step) % 4 * 2 + core) for x in range(4) for core in range(2)
    ]


def shards(records, available):
    stations = records.shape[0]
    x, yh, core = lax.axis_index("x"), lax.axis_index("yh"), lax.axis_index("core")
    fwd = lambda v: lax.ppermute(v, ("x", "core"), mirrored(1))
    bwd = lambda v: lax.ppermute(v, ("x", "core"), mirrored(-1))
    over = lambda v: lax.ppermute(v, "yh", [(0, 1), (1, 0)])
    swap = lambda v: lax.ppermute(v, "core", [(0, 1), (1, 0)])
    after = lambda value, *others: lax.optimization_barrier((value, *others))[0]

    def owned(chunk):
        got = lax.all_to_all(chunk, ("yl", "z", "core"), split_axis=0, concat_axis=0, tiled=True)
        return got.reshape(2 * OWNERS, CHUNK, -1, stations)

    def entry(chunk, dx, dy, panel):
        sign = 1 - 2 * core
        chips = [(x - way * dx) % 4 * 2 + (yh + dy) % 2 for way in (sign, -sign)]
        return chunk, *chips, panel

    shape = (2, 4 * CHUNK, stations, 16 * stations)
    first, second = whiten(records, available)
    pa = owned(first)
    na, ba = fwd(pa), bwd(pa)
    pb = owned(after(second, pa))
    ma = rows_of(pa)

    fa, nb, oa = fwd(after(na, pb)), fwd(after(pb, na)), over(pa)
    blocks1 = [entry(0, 0, 0, pa), entry(0, 1, 0, na), entry(0, -1, 0, ba)]
    out, sent = gram(core, (ma, ma), blocks1, shape, None)
    mine = ma, rows_of(pb)

    bb, fb, ob = bwd(after(pb, fa, out)), fwd(after(nb, out)), over(after(pb, oa))
    sent1 = blocks1, swap(sent)
    blocks2 = [entry(1, 0, 0, pb), entry(0, 2, 0, fa), entry(1, 1, 0, nb), entry(0, 0, 1, oa)]
    out, sent = gram(core, mine, blocks2, shape, out)

    boa, bob, noa = bwd(after(oa, bb, out)), bwd(after(ob, fb)), over(after(na, ob))
    sent2 = blocks2, swap(sent)
    blocks3 = [entry(1, -1, 0, bb), entry(1, 2, 0, fb), entry(1, 0, 1, ob)]
    out, sent = gram(core, mine, blocks3, shape, out, sent1)

    nob, foa, fob = fwd(after(ob, boa, out)), fwd(after(noa, bob)), over(after(fb, noa))
    sent3 = blocks3, swap(sent)
    blocks4 = [entry(0, -1, 1, boa), entry(1, -1, 1, bob), entry(0, 1, 1, noa)]
    out, sent = gram(core, mine, blocks4, shape, out, sent2)

    sent4 = blocks4, swap(sent)
    blocks5 = [entry(1, 2, 1, fob)]
    out, sent = gram(core, mine, blocks5, shape, out)

    sent5 = blocks5, swap(sent)
    out = place(core, out, sent3)
    blocks6 = [entry(0, 2, 1, after(foa, sent5[1], out)), entry(1, 1, 1, nob)]
    (sent,) = gram(core, mine, blocks6, shape, None, own=False)
    (out,) = gram(core, mine, blocks6, shape, out, sent4, sent5, other=False)
    return place(core, out, (blocks6, swap(sent)))


def solution(mesh):
    fine = Mesh(mesh.devices.reshape(4, 2, 2, 2, 4), ("x", "yh", "core", "yl", "z"))
    sta, freq = ("x", "yh", "core"), ("yl", "z")
    return jax.shard_map(
        shards,
        mesh=fine,
        in_specs=(P(sta, freq, None), P(sta, freq)),
        out_specs=P(None, freq, sta, None),
        check_vma=False,
    )
```

```python
import functools

import jax
import jax.numpy as jnp
import numpy as np
from jax import lax
from jax.experimental import pallas as pl
from jax.experimental.pallas import tpu as pltpu
from jax.sharding import Mesh, PartitionSpec as P

FFT_LEN = 512
BINS = 128
BAND_LO = 16
OWNERS = 8
CHUNK = 4
SEG_STEP = 8
MIB = 1024 * 1024


def spectra_table():
    sample = np.arange(FFT_LEN)
    bins = (BAND_LO + np.arange(BINS)).reshape(OWNERS, 2, 2, CHUNK).transpose(2, 0, 1, 3).reshape(-1)
    phase = (sample[:, None] * bins[None, :] % FFT_LEN) * (2.0 * np.pi / FFT_LEN)
    taper = 0.5 - 0.5 * np.cos(2.0 * np.pi * sample / FFT_LEN)
    table = np.stack([np.cos(phase), -np.sin(phase)], axis=2).reshape(FFT_LEN, 2 * BINS) * taper[:, None]
    high = table.astype(jnp.bfloat16)
    low = (table - high.astype(np.float64)).astype(jnp.bfloat16)
    return high, low


def whiten_kernel(records_ref, available_ref, high_ref, low_ref, first_ref, second_ref, rows_ref, turned_ref):
    stations, segs, samples = records_ref.shape
    flat = records_ref[...].reshape(stations * segs, samples)
    spectra = jnp.dot(flat, high_ref[...], preferred_element_type=jnp.float32)
    spectra += jnp.dot(flat, low_ref[...], preferred_element_type=jnp.float32)
    wide = spectra.shape[1]
    for part in range(2):
        rows_ref[part] = spectra[:, part * BINS : (part + 1) * BINS]
    for seg in range(segs):
        turned = jnp.concatenate(
            [rows_ref[part, pl.ds(seg, stations, stride=segs), :].T for part in range(2)], axis=0
        )
        power = jnp.sum(turned * turned, axis=0, keepdims=True) / BINS
        weight = available_ref[seg : seg + 1, :].astype(jnp.float32) / jnp.sqrt(power + 1e-05)
        turned_ref[pl.ds(seg, wide, stride=segs), :] = turned * weight
    whitened = turned_ref[...].reshape(2, 2 * OWNERS, CHUNK, 2, segs, stations).astype(jnp.bfloat16)
    first_ref[...] = whitened[0]
    second_ref[...] = whitened[1]


def whiten(records, available):
    stations, segments, samples = records.shape
    high, low = spectra_table()
    half = jax.ShapeDtypeStruct((2 * OWNERS, CHUNK, 2, segments, stations), jnp.bfloat16)
    half_spec = pl.BlockSpec((2 * OWNERS, CHUNK, 2, SEG_STEP, stations), lambda i: (0, 0, 0, i, 0))
    return pl.pallas_call(
        whiten_kernel,
        grid=(segments // SEG_STEP,),
        in_specs=[
            pl.BlockSpec((stations, SEG_STEP, samples), lambda i: (0, i, 0)),
            pl.BlockSpec((SEG_STEP, stations), lambda i: (i, 0)),
            pl.BlockSpec((samples, 2 * BINS), lambda i: (0, 0)),
            pl.BlockSpec((samples, 2 * BINS), lambda i: (0, 0)),
        ],
        out_specs=[half_spec, half_spec],
        out_shape=[half, half],
        scratch_shapes=[
            pltpu.VMEM((2, stations * SEG_STEP, BINS), jnp.float32),
            pltpu.VMEM((2 * BINS * SEG_STEP, stations), jnp.float32),
        ],
        compiler_params=pltpu.CompilerParams(vmem_limit_bytes=60 * MIB),
        name="whiten",
    )(records, available.T, jnp.asarray(high), jnp.asarray(low))


def rows_kernel(panel_ref, mine_ref):
    sources, _, depth, rows = panel_ref.shape
    panel = panel_ref[:, 0].reshape(sources // 2, 2, 2, depth // 2, rows)
    for core in range(2):
        part = panel[:, core]
        turned = jnp.stack([part[:, 1], -part[:, 0]], axis=1)
        base = 2 * rows * core
        mine_ref[0, base : base + rows] = part.reshape(-1, rows).T
        mine_ref[0, base + rows : base + 2 * rows] = turned.reshape(-1, rows).T


def rows_of(panel):
    sources, bins, depth, rows = panel.shape
    block = (1, 4 * rows, sources // 2 * depth)
    return pl.pallas_call(
        rows_kernel,
        grid=(bins,),
        in_specs=[pl.BlockSpec((sources, 1, depth, rows), lambda f: (0, f, 0, 0))],
        out_specs=pl.BlockSpec(block, lambda f: (f, 0, 0)),
        out_shape=pltpu.HBM((bins, *block[1:]), panel.dtype),
        compiler_params=pltpu.CompilerParams(vmem_limit_bytes=24 * MIB),
        name="rows",
    )(panel)


def spot_of(where, at, cols):
    return pl.ds(pl.multiple_of(where[at] * cols, cols), cols)


def gram_kernel(scale, chunks, placed, own, other, where, mine0_ref, mine1_ref, *refs):
    count, sets = len(chunks), len(placed)
    panels, sent, rest = refs[:count], refs[count : count + sets], refs[count + sets :]
    slots, place_slots, sems, place_sems = rest[-4:]
    out_ref, send_ref = rest[-5 - (own and other)], rest[-5]
    step, steps = pl.program_id(0), pl.num_programs(0)
    bins = mine0_ref.shape[0]
    rows, cols = mine0_ref.shape[1] // 4, 2 * panels[0].shape[3]
    slot, core = lax.rem(step, 2), where[count]
    received = [(which, at, chunk) for which, some in enumerate(placed) for at, chunk in enumerate(some)]

    def first_bin(owner, chunk, at):
        return owner * 2 * CHUNK + chunk * CHUNK + at * bins

    def writes(at, held):
        for block, chunk in enumerate(chunks):
            if own:
                spot = out_ref.at[:, pl.ds(first_bin(core, chunk, at), bins), :, spot_of(where, block, cols)]
                source = slots.at[held, block, core if other else 0]
                yield pltpu.make_async_copy(source, spot, sems.at[held, block, 0])
            if other:
                spot = send_ref.at[block, :, pl.ds(at * bins, bins)]
                source = slots.at[held, block, 1 - core if own else 0]
                yield pltpu.make_async_copy(source, spot, sems.at[held, block, 1])

    def places(at, held):
        for k, (_, _, chunk) in enumerate(received):
            spot = spot_of(where, count + 1 + k, cols)
            spot = out_ref.at[:, pl.ds(first_bin(1 - core, chunk, at), bins), :, spot]
            yield pltpu.make_async_copy(place_slots.at[held, k], spot, place_sems.at[held, k])

    @pl.when(step >= 2)
    def _():
        for copy in (*writes(step - 2, slot), *places(step - 2, slot)):
            copy.wait()

    for k, (which, at, _) in enumerate(received):
        place_slots[slot, k] = sent[which][at]
    for copy in places(step, slot):
        copy.start()
    for block, chunk in enumerate(chunks):
        mine_ref = mine1_ref if chunk else mine0_ref
        for f in range(bins):
            if own and other:
                mine = mine_ref[f]
            else:
                target = core if own else 1 - core
                mine = mine_ref[f, pl.ds(pl.multiple_of(target * 2 * rows, 2 * rows), 2 * rows), :]
            panel = panels[block][:, f].reshape(-1, 2, *panels[block].shape[2:])
            panel = jnp.concatenate([panel[:, side].reshape(-1, rows) for side in range(2)], axis=1)
            gram = jnp.dot(mine, panel, preferred_element_type=jnp.float32) * scale
            gram = gram.astype(jnp.bfloat16)
            for target in range(own + other):
                for part in range(2):
                    base = (2 * target + part) * rows
                    slots[slot, block, target, part, f] = gram[base : base + rows]
    for copy in writes(step, slot):
        copy.start()

    @pl.when(step == steps - 1)
    def _():
        for copy in (*writes(step - 1, 1 - slot), *places(step - 1, 1 - slot)):
            copy.wait()
        for copy in (*writes(step, slot), *places(step, slot)):
            copy.wait()


def far(value):
    return pltpu.with_memory_space_constraint(value, pltpu.HBM)


def sent_spec(results, step):
    block = (results.shape[0], 2, step, *results.shape[3:])
    return pl.BlockSpec(block, lambda f, w: (0, 0, f, 0, 0))


def gram(core, mine, blocks, shape, out, *sent, own=True, other=True):
    sources, bins, part, rows = blocks[0][3].shape
    depth, cols, step = sources // 2 * part, 2 * rows, 2
    count = len(blocks)
    chunks = [block[0] for block in blocks]
    received = [block for some, _ in sent for block in some]
    where = [block[1] for block in blocks] + [core] + [block[2] for block in received]
    held = [] if out is None else [out]
    used = [
        pl.BlockSpec((step, 4 * rows, depth), (lambda f, w: (f, 0, 0)) if chunk in chunks else (lambda f, w: (0, 0, 0)))
        for chunk in range(2)
    ]
    send = jax.ShapeDtypeStruct((count, 2, bins, rows, cols), jnp.bfloat16)
    spots = max(len(received), 1)
    return pl.pallas_call(
        functools.partial(
            gram_kernel, 2.0 / depth, chunks, [[block[0] for block in some] for some, _ in sent], own, other
        ),
        grid_spec=pltpu.PrefetchScalarGridSpec(
            num_scalar_prefetch=1,
            grid=(bins // step,),
            in_specs=used
            + [pl.BlockSpec((sources, step, part, rows), lambda f, w: (0, f, 0, 0))] * count
            + [sent_spec(results, step) for _, results in sent]
            + [pl.BlockSpec(memory_space=pl.ANY)] * len(held),
            out_specs=[pl.BlockSpec(memory_space=pl.ANY)] * (own + other),
            scratch_shapes=[
                pltpu.VMEM((2, count, own + other, 2, step, rows, cols), jnp.bfloat16),
                pltpu.VMEM((2, spots, 2, step, rows, cols), jnp.bfloat16),
                pltpu.SemaphoreType.DMA((2, count, 2)),
                pltpu.SemaphoreType.DMA((2, spots)),
            ],
        ),
        out_shape=[jax.ShapeDtypeStruct(shape, jnp.bfloat16)] * own + [send] * other,
        input_output_aliases={3 + count + len(sent): 0} if held else {},
        cost_estimate=pl.CostEstimate(
            flops=8 * count * bins * rows * depth * cols,
            bytes_accessed=2 * bins * (8 * rows * depth + count * (depth * cols + 4 * rows * cols)),
            transcendentals=0,
        ),
        compiler_params=pltpu.CompilerParams(vmem_limit_bytes=24 * MIB),
        name="gram",
    )(jnp.stack(where).astype(jnp.int32), *map(far, mine), *[block[3] for block in blocks], *[r for _, r in sent], *held)


def place_kernel(placed, where, *refs):
    sent, (out_ref, sems) = refs[: len(placed)], refs[-2:]
    step, count = pl.program_id(0), sum(map(len, placed))
    core, copies = where[count], []
    for which, chunks in enumerate(placed):
        bins, cols = sent[which].shape[2], sent[which].shape[4]
        for at, chunk in enumerate(chunks):
            first = (1 - core) * 2 * CHUNK + chunk * CHUNK + step * bins
            spot = out_ref.at[:, pl.ds(first, bins), :, spot_of(where, len(copies), cols)]
            copies.append(pltpu.make_async_copy(sent[which].at[at], spot, sems.at[len(copies)]))
    for copy in copies:
        copy.start()
    for copy in copies:
        copy.wait()


def place(core, out, *sent):
    received = [block for blocks, _ in sent for block in blocks]
    return pl.pallas_call(
        functools.partial(place_kernel, [[block[0] for block in blocks] for blocks, _ in sent]),
        grid_spec=pltpu.PrefetchScalarGridSpec(
            num_scalar_prefetch=1,
            grid=(CHUNK // 2,),
            in_specs=[sent_spec(results, 2) for _, results in sent] + [pl.BlockSpec(memory_space=pl.ANY)],
            out_specs=pl.BlockSpec(memory_space=pl.ANY),
            scratch_shapes=[pltpu.SemaphoreType.DMA((len(received),))],
        ),
        out_shape=jax.ShapeDtypeStruct(out.shape, out.dtype),
        input_output_aliases={1 + len(sent): 0},
        compiler_params=pltpu.CompilerParams(vmem_limit_bytes=24 * MIB),
        name="place",
    )(jnp.stack([block[2] for block in received] + [core]).astype(jnp.int32), *[r for _, r in sent], out)


def mirrored(step):
    return [
        (2 * x + core, (x + (1 - 2 * core) * step) % 4 * 2 + core) for x in range(4) for core in range(2)
    ]


def shards(records, available):
    stations = records.shape[0]
    x, yh, core = lax.axis_index("x"), lax.axis_index("yh"), lax.axis_index("core")
    fwd = lambda v: lax.ppermute(v, ("x", "core"), mirrored(1))
    bwd = lambda v: lax.ppermute(v, ("x", "core"), mirrored(-1))
    over = lambda v: lax.ppermute(v, "yh", [(0, 1), (1, 0)])
    swap = lambda v: lax.ppermute(v, "core", [(0, 1), (1, 0)])
    after = lambda value, *others: lax.optimization_barrier((value, *others))[0]

    def owned(chunk):
        got = lax.all_to_all(chunk, ("yl", "z", "core"), split_axis=0, concat_axis=0, tiled=True)
        return got.reshape(2 * OWNERS, CHUNK, -1, stations)

    def entry(chunk, dx, dy, panel):
        sign = 1 - 2 * core
        chips = [(x - way * dx) % 4 * 2 + (yh + dy) % 2 for way in (sign, -sign)]
        return chunk, *chips, panel

    shape = (2, 4 * CHUNK, stations, 16 * stations)
    first, second = whiten(records, available)
    pa = owned(first)
    na, ba = fwd(pa), bwd(pa)
    pb = owned(after(second, pa))
    ma = rows_of(pa)

    fa, nb, oa = fwd(after(na, pb)), fwd(after(pb, na)), over(after(pa, pb))
    blocks1 = [entry(0, 0, 0, pa), entry(0, 1, 0, na), entry(0, -1, 0, ba)]
    out, sent = gram(core, (ma, ma), blocks1, shape, None)
    mine = ma, rows_of(pb)

    bb, fb, ob = bwd(after(pb, fa, out)), fwd(after(nb, out)), over(after(pb, oa, fa))
    sent1 = blocks1, swap(sent)
    blocks2 = [entry(1, 0, 0, pb), entry(0, 2, 0, fa), entry(1, 1, 0, nb), entry(0, 0, 1, oa)]
    out, sent = gram(core, mine, blocks2, shape, out)

    boa, nob, noa = bwd(after(oa, bb, out)), fwd(after(ob, fb)), over(after(na, ob, bb))
    sent2 = blocks2, swap(sent)
    blocks3 = [entry(1, -1, 0, bb), entry(1, 2, 0, fb), entry(1, 0, 1, ob)]
    out, sent = gram(core, mine, blocks3, shape, out, sent1)

    half = CHUNK // 2
    foa, bob = fwd(after(noa, boa, out)), bwd(after(ob, nob))
    fob = over(after(fb[:, :half], noa)), fwd(nob[:, half:])
    sent3 = blocks3, swap(sent)
    blocks4 = [entry(0, -1, 1, boa), entry(1, 1, 1, nob), entry(0, 1, 1, noa)]
    out, sent = gram(core, mine, blocks4, shape, out, sent2)

    sent4 = blocks4, swap(sent)
    blocks5 = [entry(0, 2, 1, foa)]
    out, sent = gram(core, mine, blocks5, shape, out, sent3)

    sent5 = blocks5, swap(sent)
    blocks6 = [entry(1, -1, 1, after(bob, out)), entry(1, 2, 1, jnp.concatenate([after(fob[0], out), after(fob[1], out)], axis=1))]
    (sent,) = gram(core, mine, blocks6, shape, None, own=False)
    (out,) = gram(core, mine, blocks6, shape, out, sent4, other=False)
    return place(core, out, sent5, (blocks6, swap(sent)))


def solution(mesh):
    fine = Mesh(mesh.devices.reshape(4, 2, 2, 2, 4), ("x", "yh", "core", "yl", "z"))
    sta, freq = ("x", "yh", "core"), ("yl", "z")
    return jax.shard_map(
        shards,
        mesh=fine,
        in_specs=(P(sta, freq, None), P(sta, freq)),
        out_specs=P(None, freq, sta, None),
        check_vma=False,
    )
```

```python
import functools

import jax
import jax.numpy as jnp
import numpy as np
from jax import lax
from jax.experimental import pallas as pl
from jax.experimental.pallas import tpu as pltpu
from jax.sharding import Mesh, PartitionSpec as P

FFT_LEN = 512
BINS = 128
BAND_LO = 16
OWNERS = 8
CHUNK = 4
SEG_STEP = 8
MIB = 1024 * 1024


def spectra_table():
    sample = np.arange(FFT_LEN)
    bins = (BAND_LO + np.arange(BINS)).reshape(OWNERS, 2, 2, CHUNK).transpose(2, 0, 1, 3).reshape(-1)
    phase = (sample[:, None] * bins[None, :] % FFT_LEN) * (2.0 * np.pi / FFT_LEN)
    taper = 0.5 - 0.5 * np.cos(2.0 * np.pi * sample / FFT_LEN)
    table = np.stack([np.cos(phase), -np.sin(phase)], axis=2).reshape(FFT_LEN, 2 * BINS) * taper[:, None]
    high = table.astype(jnp.bfloat16)
    low = (table - high.astype(np.float64)).astype(jnp.bfloat16)
    return high, low


def whiten_kernel(records_ref, available_ref, high_ref, low_ref, first_ref, second_ref, rows_ref, turned_ref):
    stations, segs, samples = records_ref.shape
    flat = records_ref[...].reshape(stations * segs, samples)
    spectra = jnp.dot(flat, high_ref[...], preferred_element_type=jnp.float32)
    spectra += jnp.dot(flat, low_ref[...], preferred_element_type=jnp.float32)
    wide = spectra.shape[1]
    for part in range(2):
        rows_ref[part] = spectra[:, part * BINS : (part + 1) * BINS]
    for seg in range(segs):
        turned = jnp.concatenate(
            [rows_ref[part, pl.ds(seg, stations, stride=segs), :].T for part in range(2)], axis=0
        )
        power = jnp.sum(turned * turned, axis=0, keepdims=True) / BINS
        weight = available_ref[seg : seg + 1, :].astype(jnp.float32) / jnp.sqrt(power + 1e-05)
        turned_ref[pl.ds(seg, wide, stride=segs), :] = turned * weight
    whitened = turned_ref[...].reshape(2, 2 * OWNERS, CHUNK, 2, segs, stations).astype(jnp.bfloat16)
    first_ref[...] = whitened[0]
    second_ref[...] = whitened[1]


def whiten(records, available):
    stations, segments, samples = records.shape
    high, low = spectra_table()
    half = jax.ShapeDtypeStruct((2 * OWNERS, CHUNK, 2, segments, stations), jnp.bfloat16)
    half_spec = pl.BlockSpec((2 * OWNERS, CHUNK, 2, SEG_STEP, stations), lambda i: (0, 0, 0, i, 0))
    return pl.pallas_call(
        whiten_kernel,
        grid=(segments // SEG_STEP,),
        in_specs=[
            pl.BlockSpec((stations, SEG_STEP, samples), lambda i: (0, i, 0)),
            pl.BlockSpec((SEG_STEP, stations), lambda i: (i, 0)),
            pl.BlockSpec((samples, 2 * BINS), lambda i: (0, 0)),
            pl.BlockSpec((samples, 2 * BINS), lambda i: (0, 0)),
        ],
        out_specs=[half_spec, half_spec],
        out_shape=[half, half],
        scratch_shapes=[
            pltpu.VMEM((2, stations * SEG_STEP, BINS), jnp.float32),
            pltpu.VMEM((2 * BINS * SEG_STEP, stations), jnp.float32),
        ],
        compiler_params=pltpu.CompilerParams(vmem_limit_bytes=60 * MIB),
        name="whiten",
    )(records, available.T, jnp.asarray(high), jnp.asarray(low))


def rows_kernel(panel_ref, mine_ref):
    sources, _, depth, rows = panel_ref.shape
    panel = panel_ref[:, 0].reshape(sources // 2, 2, 2, depth // 2, rows)
    for core in range(2):
        part = panel[:, core]
        turned = jnp.stack([part[:, 1], -part[:, 0]], axis=1)
        base = 2 * rows * core
        mine_ref[0, base : base + rows] = part.reshape(-1, rows).T
        mine_ref[0, base + rows : base + 2 * rows] = turned.reshape(-1, rows).T


def rows_of(panel):
    sources, bins, depth, rows = panel.shape
    block = (1, 4 * rows, sources // 2 * depth)
    return pl.pallas_call(
        rows_kernel,
        grid=(bins,),
        in_specs=[pl.BlockSpec((sources, 1, depth, rows), lambda f: (0, f, 0, 0))],
        out_specs=pl.BlockSpec(block, lambda f: (f, 0, 0)),
        out_shape=pltpu.HBM((bins, *block[1:]), panel.dtype),
        compiler_params=pltpu.CompilerParams(vmem_limit_bytes=24 * MIB),
        name="rows",
    )(panel)


def spot_of(where, at, cols):
    return pl.ds(pl.multiple_of(where[at] * cols, cols), cols)


def gram_kernel(scale, chunks, placed, own, other, where, mine0_ref, mine1_ref, *refs):
    count, sets = len(chunks), len(placed)
    panels, sent, rest = refs[:count], refs[count : count + sets], refs[count + sets :]
    slots, place_slots, sems, place_sems = rest[-4:]
    out_ref, send_ref = rest[-5 - (own and other)], rest[-5]
    step, steps = pl.program_id(0), pl.num_programs(0)
    bins = mine0_ref.shape[0]
    rows, cols = mine0_ref.shape[1] // 4, 2 * panels[0].shape[3]
    slot, core = lax.rem(step, 2), where[count]
    received = [(which, at, chunk) for which, some in enumerate(placed) for at, chunk in enumerate(some)]

    def first_bin(owner, chunk, at):
        return owner * 2 * CHUNK + chunk * CHUNK + at * bins

    def writes(at, held):
        for block, chunk in enumerate(chunks):
            if own:
                spot = out_ref.at[:, pl.ds(first_bin(core, chunk, at), bins), :, spot_of(where, block, cols)]
                source = slots.at[held, block, core if other else 0]
                yield pltpu.make_async_copy(source, spot, sems.at[held, block, 0])
            if other:
                spot = send_ref.at[block, :, pl.ds(at * bins, bins)]
                source = slots.at[held, block, 1 - core if own else 0]
                yield pltpu.make_async_copy(source, spot, sems.at[held, block, 1])

    def places(at, held):
        for k, (_, _, chunk) in enumerate(received):
            spot = spot_of(where, count + 1 + k, cols)
            spot = out_ref.at[:, pl.ds(first_bin(1 - core, chunk, at), bins), :, spot]
            yield pltpu.make_async_copy(place_slots.at[held, k], spot, place_sems.at[held, k])

    @pl.when(step >= 2)
    def _():
        for copy in (*writes(step - 2, slot), *places(step - 2, slot)):
            copy.wait()

    for k, (which, at, _) in enumerate(received):
        place_slots[slot, k] = sent[which][at]
    for copy in places(step, slot):
        copy.start()
    for block, chunk in enumerate(chunks):
        mine_ref = mine1_ref if chunk else mine0_ref
        for f in range(bins):
            if own and other:
                mine = mine_ref[f]
            else:
                target = core if own else 1 - core
                mine = mine_ref[f, pl.ds(pl.multiple_of(target * 2 * rows, 2 * rows), 2 * rows), :]
            panel = panels[block][:, f].reshape(-1, 2, *panels[block].shape[2:])
            panel = jnp.concatenate([panel[:, side].reshape(-1, rows) for side in range(2)], axis=1)
            gram = jnp.dot(mine, panel, preferred_element_type=jnp.float32) * scale
            gram = gram.astype(jnp.bfloat16)
            for target in range(own + other):
                for part in range(2):
                    base = (2 * target + part) * rows
                    slots[slot, block, target, part, f] = gram[base : base + rows]
    for copy in writes(step, slot):
        copy.start()

    @pl.when(step == steps - 1)
    def _():
        for copy in (*writes(step - 1, 1 - slot), *places(step - 1, 1 - slot)):
            copy.wait()
        for copy in (*writes(step, slot), *places(step, slot)):
            copy.wait()


def far(value):
    return pltpu.with_memory_space_constraint(value, pltpu.HBM)


def sent_spec(results, step):
    block = (results.shape[0], 2, step, *results.shape[3:])
    return pl.BlockSpec(block, lambda f, w: (0, 0, f, 0, 0))


def gram(core, mine, blocks, shape, out, *sent, own=True, other=True):
    sources, bins, part, rows = blocks[0][3].shape
    depth, cols, step = sources // 2 * part, 2 * rows, 2
    count = len(blocks)
    chunks = [block[0] for block in blocks]
    received = [block for some, _ in sent for block in some]
    where = [block[1] for block in blocks] + [core] + [block[2] for block in received]
    held = [] if out is None else [out]
    used = [
        pl.BlockSpec((step, 4 * rows, depth), (lambda f, w: (f, 0, 0)) if chunk in chunks else (lambda f, w: (0, 0, 0)))
        for chunk in range(2)
    ]
    send = jax.ShapeDtypeStruct((count, 2, bins, rows, cols), jnp.bfloat16)
    spots = max(len(received), 1)
    return pl.pallas_call(
        functools.partial(
            gram_kernel, 2.0 / depth, chunks, [[block[0] for block in some] for some, _ in sent], own, other
        ),
        grid_spec=pltpu.PrefetchScalarGridSpec(
            num_scalar_prefetch=1,
            grid=(bins // step,),
            in_specs=used
            + [pl.BlockSpec((sources, step, part, rows), lambda f, w: (0, f, 0, 0))] * count
            + [sent_spec(results, step) for _, results in sent]
            + [pl.BlockSpec(memory_space=pl.ANY)] * len(held),
            out_specs=[pl.BlockSpec(memory_space=pl.ANY)] * (own + other),
            scratch_shapes=[
                pltpu.VMEM((2, count, own + other, 2, step, rows, cols), jnp.bfloat16),
                pltpu.VMEM((2, spots, 2, step, rows, cols), jnp.bfloat16),
                pltpu.SemaphoreType.DMA((2, count, 2)),
                pltpu.SemaphoreType.DMA((2, spots)),
            ],
        ),
        out_shape=[jax.ShapeDtypeStruct(shape, jnp.bfloat16)] * own + [send] * other,
        input_output_aliases={3 + count + len(sent): 0} if held else {},
        cost_estimate=pl.CostEstimate(
            flops=8 * count * bins * rows * depth * cols,
            bytes_accessed=2 * bins * (8 * rows * depth + count * (depth * cols + 4 * rows * cols)),
            transcendentals=0,
        ),
        compiler_params=pltpu.CompilerParams(vmem_limit_bytes=24 * MIB),
        name="gram",
    )(jnp.stack(where).astype(jnp.int32), *map(far, mine), *[block[3] for block in blocks], *[r for _, r in sent], *held)


def place_kernel(placed, where, *refs):
    sent, (out_ref, sems) = refs[: len(placed)], refs[-2:]
    step, count = pl.program_id(0), sum(map(len, placed))
    core, copies = where[count], []
    for which, chunks in enumerate(placed):
        bins, cols = sent[which].shape[2], sent[which].shape[4]
        for at, chunk in enumerate(chunks):
            first = (1 - core) * 2 * CHUNK + chunk * CHUNK + step * bins
            spot = out_ref.at[:, pl.ds(first, bins), :, spot_of(where, len(copies), cols)]
            copies.append(pltpu.make_async_copy(sent[which].at[at], spot, sems.at[len(copies)]))
    for copy in copies:
        copy.start()
    for copy in copies:
        copy.wait()


def place(core, out, *sent):
    received = [block for blocks, _ in sent for block in blocks]
    return pl.pallas_call(
        functools.partial(place_kernel, [[block[0] for block in blocks] for blocks, _ in sent]),
        grid_spec=pltpu.PrefetchScalarGridSpec(
            num_scalar_prefetch=1,
            grid=(CHUNK // 2,),
            in_specs=[sent_spec(results, 2) for _, results in sent] + [pl.BlockSpec(memory_space=pl.ANY)],
            out_specs=pl.BlockSpec(memory_space=pl.ANY),
            scratch_shapes=[pltpu.SemaphoreType.DMA((len(received),))],
        ),
        out_shape=jax.ShapeDtypeStruct(out.shape, out.dtype),
        input_output_aliases={1 + len(sent): 0},
        compiler_params=pltpu.CompilerParams(vmem_limit_bytes=24 * MIB),
        name="place",
    )(jnp.stack([block[2] for block in received] + [core]).astype(jnp.int32), *[r for _, r in sent], out)


def mirrored(step):
    return [
        (2 * x + core, (x + (1 - 2 * core) * step) % 4 * 2 + core) for x in range(4) for core in range(2)
    ]


def shards(records, available):
    stations = records.shape[0]
    x, yh, core = lax.axis_index("x"), lax.axis_index("yh"), lax.axis_index("core")
    fwd = lambda v: lax.ppermute(v, ("x", "core"), mirrored(1))
    bwd = lambda v: lax.ppermute(v, ("x", "core"), mirrored(-1))
    over = lambda v: lax.ppermute(v, "yh", [(0, 1), (1, 0)])
    swap = lambda v: lax.ppermute(v, "core", [(0, 1), (1, 0)])
    after = lambda value, *others: lax.optimization_barrier((value, *others))[0]

    def owned(chunk):
        got = lax.all_to_all(chunk, ("yl", "z", "core"), split_axis=0, concat_axis=0, tiled=True)
        return got.reshape(2 * OWNERS, CHUNK, -1, stations)

    def entry(chunk, dx, dy, panel):
        sign = 1 - 2 * core
        chips = [(x - way * dx) % 4 * 2 + (yh + dy) % 2 for way in (sign, -sign)]
        return chunk, *chips, panel

    shape = (2, 4 * CHUNK, stations, 16 * stations)
    first, second = whiten(records, available)
    pa = owned(first)
    na, ba = fwd(pa), bwd(pa)
    pb = owned(after(second, pa))
    ma = rows_of(pa)

    fa, nb, oa = fwd(after(na, pb)), fwd(after(pb, na)), over(after(pa, pb))
    blocks1 = [entry(0, 0, 0, pa), entry(0, 1, 0, na), entry(0, -1, 0, ba)]
    out, sent = gram(core, (ma, ma), blocks1, shape, None)
    mine = ma, rows_of(pb)

    bb, fb, ob = bwd(after(pb, fa, out)), fwd(after(nb, out)), over(after(pb, oa, fa))
    sent1 = blocks1, swap(sent)
    blocks2 = [entry(1, 0, 0, after(pb, bb)), entry(0, 2, 0, fa), entry(1, 1, 0, nb), entry(0, 0, 1, oa)]
    out, sent = gram(core, mine, blocks2, shape, out)

    boa, nob, noa = bwd(after(oa, bb)), fwd(after(ob, fb)), over(after(na, ob, bb))
    sent2 = blocks2, swap(sent)
    blocks3 = [entry(1, -1, 0, bb), entry(1, 2, 0, fb), entry(1, 0, 1, ob)]
    out, sent = gram(core, mine, blocks3, shape, out, sent1)

    half = CHUNK // 2
    bob, foa = bwd(after(ob, boa, out)), fwd(after(noa, nob))
    fob = over(after(fb[:, :half], noa)), fwd(nob[:, half:])
    sent3 = blocks3, swap(sent)
    blocks4 = [entry(0, -1, 1, boa), entry(1, 1, 1, nob), entry(0, 1, 1, noa)]
    out, sent = gram(core, mine, blocks4, shape, out)

    sent4 = blocks4, swap(sent)
    blocks5 = [entry(1, -1, 1, bob)]
    out, sent = gram(core, mine, blocks5, shape, out, sent2)

    sent5 = blocks5, swap(sent)
    blocks6 = [entry(0, 2, 1, after(foa, out)), entry(1, 2, 1, jnp.concatenate([after(fob[0], out), after(fob[1], out)], axis=1))]
    (sent,) = gram(core, mine, blocks6, shape, None, own=False)
    (out,) = gram(core, mine, blocks6, shape, out, sent3, sent4, other=False)
    return place(core, out, sent5, (blocks6, swap(sent)))


def solution(mesh):
    fine = Mesh(mesh.devices.reshape(4, 2, 2, 2, 4), ("x", "yh", "core", "yl", "z"))
    sta, freq = ("x", "yh", "core"), ("yl", "z")
    return jax.shard_map(
        shards,
        mesh=fine,
        in_specs=(P(sta, freq, None), P(sta, freq)),
        out_specs=P(None, freq, sta, None),
        check_vma=False,
    )
```

```python
import functools

import jax
import jax.numpy as jnp
import numpy as np
from jax import lax
from jax.experimental import pallas as pl
from jax.experimental.pallas import tpu as pltpu
from jax.sharding import Mesh, PartitionSpec as P

FFT_LEN = 512
BINS = 128
BAND_LO = 16
OWNERS = 8
CHUNK = 4
SEG_STEP = 8
MIB = 1024 * 1024


def spectra_table():
    sample = np.arange(FFT_LEN)
    bins = (BAND_LO + np.arange(BINS)).reshape(OWNERS, 2, 2, CHUNK).transpose(2, 0, 1, 3).reshape(-1)
    phase = (sample[:, None] * bins[None, :] % FFT_LEN) * (2.0 * np.pi / FFT_LEN)
    taper = 0.5 - 0.5 * np.cos(2.0 * np.pi * sample / FFT_LEN)
    table = np.stack([np.cos(phase), -np.sin(phase)], axis=2).reshape(FFT_LEN, 2 * BINS) * taper[:, None]
    high = table.astype(jnp.bfloat16)
    low = (table - high.astype(np.float64)).astype(jnp.bfloat16)
    return high, low


def whiten_kernel(records_ref, available_ref, high_ref, low_ref, first_ref, second_ref, rows_ref, turned_ref):
    stations, segs, samples = records_ref.shape
    flat = records_ref[...].reshape(stations * segs, samples)
    spectra = jnp.dot(flat, high_ref[...], preferred_element_type=jnp.float32)
    spectra += jnp.dot(flat, low_ref[...], preferred_element_type=jnp.float32)
    wide = spectra.shape[1]
    for part in range(2):
        rows_ref[part] = spectra[:, part * BINS : (part + 1) * BINS]
    for seg in range(segs):
        turned = jnp.concatenate(
            [rows_ref[part, pl.ds(seg, stations, stride=segs), :].T for part in range(2)], axis=0
        )
        power = jnp.sum(turned * turned, axis=0, keepdims=True) / BINS
        weight = available_ref[seg : seg + 1, :].astype(jnp.float32) / jnp.sqrt(power + 1e-05)
        turned_ref[pl.ds(seg, wide, stride=segs), :] = turned * weight
    whitened = turned_ref[...].reshape(2, 2 * OWNERS, CHUNK, 2, segs, stations).astype(jnp.bfloat16)
    first_ref[...] = whitened[0]
    second_ref[...] = whitened[1]


def whiten(records, available):
    stations, segments, samples = records.shape
    high, low = spectra_table()
    half = jax.ShapeDtypeStruct((2 * OWNERS, CHUNK, 2, segments, stations), jnp.bfloat16)
    half_spec = pl.BlockSpec((2 * OWNERS, CHUNK, 2, SEG_STEP, stations), lambda i: (0, 0, 0, i, 0))
    return pl.pallas_call(
        whiten_kernel,
        grid=(segments // SEG_STEP,),
        in_specs=[
            pl.BlockSpec((stations, SEG_STEP, samples), lambda i: (0, i, 0)),
            pl.BlockSpec((SEG_STEP, stations), lambda i: (i, 0)),
            pl.BlockSpec((samples, 2 * BINS), lambda i: (0, 0)),
            pl.BlockSpec((samples, 2 * BINS), lambda i: (0, 0)),
        ],
        out_specs=[half_spec, half_spec],
        out_shape=[half, half],
        scratch_shapes=[
            pltpu.VMEM((2, stations * SEG_STEP, BINS), jnp.float32),
            pltpu.VMEM((2 * BINS * SEG_STEP, stations), jnp.float32),
        ],
        compiler_params=pltpu.CompilerParams(vmem_limit_bytes=60 * MIB),
        name="whiten",
    )(records, available.T, jnp.asarray(high), jnp.asarray(low))


def rows_kernel(panel_ref, mine_ref):
    sources, _, depth, rows = panel_ref.shape
    panel = panel_ref[:, 0].reshape(sources // 2, 2, 2, depth // 2, rows)
    for core in range(2):
        part = panel[:, core]
        turned = jnp.stack([part[:, 1], -part[:, 0]], axis=1)
        base = 2 * rows * core
        mine_ref[0, base : base + rows] = part.reshape(-1, rows).T
        mine_ref[0, base + rows : base + 2 * rows] = turned.reshape(-1, rows).T


def rows_of(panel):
    sources, bins, depth, rows = panel.shape
    block = (1, 4 * rows, sources // 2 * depth)
    return pl.pallas_call(
        rows_kernel,
        grid=(bins,),
        in_specs=[pl.BlockSpec((sources, 1, depth, rows), lambda f: (0, f, 0, 0))],
        out_specs=pl.BlockSpec(block, lambda f: (f, 0, 0)),
        out_shape=pltpu.HBM((bins, *block[1:]), panel.dtype),
        compiler_params=pltpu.CompilerParams(vmem_limit_bytes=24 * MIB),
        name="rows",
    )(panel)


def spot_of(where, at, cols):
    return pl.ds(pl.multiple_of(where[at] * cols, cols), cols)


def gram_kernel(scale, chunks, placed, own, other, where, mine0_ref, mine1_ref, *refs):
    count, sets = len(chunks), len(placed)
    panels, sent, rest = refs[:count], refs[count : count + sets], refs[count + sets :]
    slots, place_slots, sems, place_sems = rest[-4:]
    out_ref, send_ref = rest[-5 - (own and other)], rest[-5]
    step, steps = pl.program_id(0), pl.num_programs(0)
    bins = mine0_ref.shape[0]
    rows, cols = mine0_ref.shape[1] // 4, 2 * panels[0].shape[3]
    slot, core = lax.rem(step, 2), where[count]
    received = [(which, at, chunk) for which, some in enumerate(placed) for at, chunk in enumerate(some)]

    def first_bin(owner, chunk, at):
        return owner * 2 * CHUNK + chunk * CHUNK + at * bins

    def writes(at, held):
        for block, chunk in enumerate(chunks):
            if own:
                spot = out_ref.at[:, pl.ds(first_bin(core, chunk, at), bins), :, spot_of(where, block, cols)]
                source = slots.at[held, block, core if other else 0]
                yield pltpu.make_async_copy(source, spot, sems.at[held, block, 0])
            if other:
                spot = send_ref.at[block, :, pl.ds(at * bins, bins)]
                source = slots.at[held, block, 1 - core if own else 0]
                yield pltpu.make_async_copy(source, spot, sems.at[held, block, 1])

    def places(at, held):
        for k, (_, _, chunk) in enumerate(received):
            spot = spot_of(where, count + 1 + k, cols)
            spot = out_ref.at[:, pl.ds(first_bin(1 - core, chunk, at), bins), :, spot]
            yield pltpu.make_async_copy(place_slots.at[held, k], spot, place_sems.at[held, k])

    @pl.when(step >= 2)
    def _():
        for copy in (*writes(step - 2, slot), *places(step - 2, slot)):
            copy.wait()

    for k, (which, at, _) in enumerate(received):
        place_slots[slot, k] = sent[which][at]
    for copy in places(step, slot):
        copy.start()
    for block, chunk in enumerate(chunks):
        mine_ref = mine1_ref if chunk else mine0_ref
        for f in range(bins):
            if own and other:
                mine = mine_ref[f]
            else:
                target = core if own else 1 - core
                mine = mine_ref[f, pl.ds(pl.multiple_of(target * 2 * rows, 2 * rows), 2 * rows), :]
            panel = panels[block][:, f].reshape(-1, 2, *panels[block].shape[2:])
            panel = jnp.concatenate([panel[:, side].reshape(-1, rows) for side in range(2)], axis=1)
            gram = jnp.dot(mine, panel, preferred_element_type=jnp.float32) * scale
            gram = gram.astype(jnp.bfloat16)
            for target in range(own + other):
                for part in range(2):
                    base = (2 * target + part) * rows
                    slots[slot, block, target, part, f] = gram[base : base + rows]
    for copy in writes(step, slot):
        copy.start()

    @pl.when(step == steps - 1)
    def _():
        for copy in (*writes(step - 1, 1 - slot), *places(step - 1, 1 - slot)):
            copy.wait()
        for copy in (*writes(step, slot), *places(step, slot)):
            copy.wait()


def far(value):
    return pltpu.with_memory_space_constraint(value, pltpu.HBM)


def sent_spec(results, step):
    block = (results.shape[0], 2, step, *results.shape[3:])
    return pl.BlockSpec(block, lambda f, w: (0, 0, f, 0, 0))


def gram(core, mine, blocks, shape, out, *sent, own=True, other=True):
    sources, bins, part, rows = blocks[0][3].shape
    depth, cols, step = sources // 2 * part, 2 * rows, 2
    count = len(blocks)
    chunks = [block[0] for block in blocks]
    received = [block for some, _ in sent for block in some]
    where = [block[1] for block in blocks] + [core] + [block[2] for block in received]
    held = [] if out is None else [out]
    used = [
        pl.BlockSpec((step, 4 * rows, depth), (lambda f, w: (f, 0, 0)) if chunk in chunks else (lambda f, w: (0, 0, 0)))
        for chunk in range(2)
    ]
    send = jax.ShapeDtypeStruct((count, 2, bins, rows, cols), jnp.bfloat16)
    spots = max(len(received), 1)
    return pl.pallas_call(
        functools.partial(
            gram_kernel, 2.0 / depth, chunks, [[block[0] for block in some] for some, _ in sent], own, other
        ),
        grid_spec=pltpu.PrefetchScalarGridSpec(
            num_scalar_prefetch=1,
            grid=(bins // step,),
            in_specs=used
            + [pl.BlockSpec((sources, step, part, rows), lambda f, w: (0, f, 0, 0))] * count
            + [sent_spec(results, step) for _, results in sent]
            + [pl.BlockSpec(memory_space=pl.ANY)] * len(held),
            out_specs=[pl.BlockSpec(memory_space=pl.ANY)] * (own + other),
            scratch_shapes=[
                pltpu.VMEM((2, count, own + other, 2, step, rows, cols), jnp.bfloat16),
                pltpu.VMEM((2, spots, 2, step, rows, cols), jnp.bfloat16),
                pltpu.SemaphoreType.DMA((2, count, 2)),
                pltpu.SemaphoreType.DMA((2, spots)),
            ],
        ),
        out_shape=[jax.ShapeDtypeStruct(shape, jnp.bfloat16)] * own + [send] * other,
        input_output_aliases={3 + count + len(sent): 0} if held else {},
        cost_estimate=pl.CostEstimate(
            flops=8 * count * bins * rows * depth * cols,
            bytes_accessed=2 * bins * (8 * rows * depth + count * (depth * cols + 4 * rows * cols)),
            transcendentals=0,
        ),
        compiler_params=pltpu.CompilerParams(vmem_limit_bytes=24 * MIB),
        name="gram",
    )(jnp.stack(where).astype(jnp.int32), *map(far, mine), *[block[3] for block in blocks], *[r for _, r in sent], *held)


def place_kernel(placed, where, *refs):
    sent, (out_ref, sems) = refs[: len(placed)], refs[-2:]
    step, count = pl.program_id(0), sum(map(len, placed))
    core, copies = where[count], []
    for which, chunks in enumerate(placed):
        bins, cols = sent[which].shape[2], sent[which].shape[4]
        for at, chunk in enumerate(chunks):
            first = (1 - core) * 2 * CHUNK + chunk * CHUNK + step * bins
            spot = out_ref.at[:, pl.ds(first, bins), :, spot_of(where, len(copies), cols)]
            copies.append(pltpu.make_async_copy(sent[which].at[at], spot, sems.at[len(copies)]))
    for copy in copies:
        copy.start()
    for copy in copies:
        copy.wait()


def place(core, out, *sent):
    received = [block for blocks, _ in sent for block in blocks]
    return pl.pallas_call(
        functools.partial(place_kernel, [[block[0] for block in blocks] for blocks, _ in sent]),
        grid_spec=pltpu.PrefetchScalarGridSpec(
            num_scalar_prefetch=1,
            grid=(CHUNK // 2,),
            in_specs=[sent_spec(results, 2) for _, results in sent] + [pl.BlockSpec(memory_space=pl.ANY)],
            out_specs=pl.BlockSpec(memory_space=pl.ANY),
            scratch_shapes=[pltpu.SemaphoreType.DMA((len(received),))],
        ),
        out_shape=jax.ShapeDtypeStruct(out.shape, out.dtype),
        input_output_aliases={1 + len(sent): 0},
        compiler_params=pltpu.CompilerParams(vmem_limit_bytes=24 * MIB),
        name="place",
    )(jnp.stack([block[2] for block in received] + [core]).astype(jnp.int32), *[r for _, r in sent], out)


def mirrored(step):
    return [
        (2 * x + core, (x + (1 - 2 * core) * step) % 4 * 2 + core) for x in range(4) for core in range(2)
    ]


def shards(records, available):
    stations = records.shape[0]
    x, yh, core = lax.axis_index("x"), lax.axis_index("yh"), lax.axis_index("core")
    fwd = lambda v: lax.ppermute(v, ("x", "core"), mirrored(1))
    bwd = lambda v: lax.ppermute(v, ("x", "core"), mirrored(-1))
    over = lambda v: lax.ppermute(v, "yh", [(0, 1), (1, 0)])
    swap = lambda v: lax.ppermute(v, "core", [(0, 1), (1, 0)])
    after = lambda value, *others: lax.optimization_barrier((value, *others))[0]

    def owned(chunk):
        got = lax.all_to_all(chunk, ("yl", "z", "core"), split_axis=0, concat_axis=0, tiled=True)
        return got.reshape(2 * OWNERS, CHUNK, -1, stations)

    def entry(chunk, dx, dy, panel):
        sign = 1 - 2 * core
        chips = [(x - way * dx) % 4 * 2 + (yh + dy) % 2 for way in (sign, -sign)]
        return chunk, *chips, panel

    shape = (2, 4 * CHUNK, stations, 16 * stations)
    first, second = whiten(records, available)
    pa = owned(first)
    na, ba = fwd(pa), bwd(pa)
    pb = owned(after(second, pa))
    ma = rows_of(pa)

    fa, nb, oa = fwd(after(na, pb)), fwd(after(pb, na)), over(after(pa, pb))
    blocks1 = [entry(0, 0, 0, pa), entry(0, 1, 0, na), entry(0, -1, 0, ba)]
    out, sent = gram(core, (ma, ma), blocks1, shape, None)
    mine = ma, rows_of(pb)

    bb, fb, ob = bwd(after(pb, fa, out)), fwd(after(nb, oa, out)), over(after(pb, oa))
    sent1 = blocks1, swap(sent)
    blocks2 = [entry(1, 0, 0, after(pb, bb)), entry(0, 2, 0, fa), entry(1, 1, 0, nb), entry(0, 0, 1, oa)]
    out, sent = gram(core, mine, blocks2, shape, out)

    boa, nob, noa = bwd(after(oa, bb)), fwd(after(ob, fb)), over(after(na, ob))
    sent2 = blocks2, swap(sent)
    blocks3 = [entry(1, -1, 0, bb), entry(1, 2, 0, fb), entry(1, 0, 1, ob)]
    out, sent = gram(core, mine, blocks3, shape, out, sent1)

    half = CHUNK // 2
    bob, foa = bwd(after(ob, boa, out)), fwd(after(noa, nob))
    fob = over(after(fb[:, :half], noa)), fwd(nob[:, half:])
    sent3 = blocks3, swap(sent)
    blocks4 = [entry(0, -1, 1, boa), entry(1, 1, 1, nob), entry(0, 1, 1, noa)]
    out, sent = gram(core, mine, blocks4, shape, out)

    sent4 = blocks4, swap(sent)
    blocks5 = [entry(1, -1, 1, bob)]
    out, sent = gram(core, mine, blocks5, shape, out, sent2)

    sent5 = blocks5, swap(sent)
    blocks6 = [entry(0, 2, 1, after(foa, out)), entry(1, 2, 1, jnp.concatenate([after(fob[0], out), after(fob[1], out)], axis=1))]
    (sent,) = gram(core, mine, blocks6, shape, None, own=False)
    (out,) = gram(core, mine, blocks6, shape, out, sent3, sent4, other=False)
    return place(core, out, sent5, (blocks6, swap(sent)))


def solution(mesh):
    fine = Mesh(mesh.devices.reshape(4, 2, 2, 2, 4), ("x", "yh", "core", "yl", "z"))
    sta, freq = ("x", "yh", "core"), ("yl", "z")
    return jax.shard_map(
        shards,
        mesh=fine,
        in_specs=(P(sta, freq, None), P(sta, freq)),
        out_specs=P(None, freq, sta, None),
        check_vma=False,
    )
```

```python
import functools

import jax
import jax.numpy as jnp
import numpy as np
from jax import lax
from jax.experimental import pallas as pl
from jax.experimental.pallas import tpu as pltpu
from jax.sharding import Mesh, PartitionSpec as P

FFT_LEN = 512
BINS = 128
BAND_LO = 16
OWNERS = 8
CHUNK = 4
SEG_STEP = 8
MIB = 1024 * 1024


def spectra_table():
    sample = np.arange(FFT_LEN)
    bins = (BAND_LO + np.arange(BINS)).reshape(OWNERS, 2, 2, CHUNK).transpose(2, 0, 1, 3).reshape(-1)
    phase = (sample[:, None] * bins[None, :] % FFT_LEN) * (2.0 * np.pi / FFT_LEN)
    taper = 0.5 - 0.5 * np.cos(2.0 * np.pi * sample / FFT_LEN)
    table = np.stack([np.cos(phase), -np.sin(phase)], axis=2).reshape(FFT_LEN, 2 * BINS) * taper[:, None]
    return table.astype(jnp.bfloat16)


def whiten_kernel(records_ref, available_ref, table_ref, first_ref, second_ref, rows_ref, turned_ref):
    stations, segs, samples = records_ref.shape
    flat = records_ref[...].reshape(stations * segs, samples)
    spectra = jnp.dot(flat, table_ref[...], preferred_element_type=jnp.float32)
    wide = spectra.shape[1]
    for part in range(2):
        rows_ref[part] = spectra[:, part * BINS : (part + 1) * BINS]
    for seg in range(segs):
        turned = jnp.concatenate(
            [rows_ref[part, pl.ds(seg, stations, stride=segs), :].T for part in range(2)], axis=0
        )
        power = jnp.sum(turned * turned, axis=0, keepdims=True) / BINS
        weight = available_ref[seg : seg + 1, :].astype(jnp.float32) / jnp.sqrt(power + 1e-05)
        turned_ref[pl.ds(seg, wide, stride=segs), :] = turned * weight
    whitened = turned_ref[...].reshape(2, 2 * OWNERS, CHUNK, 2, segs, stations).astype(jnp.bfloat16)
    first_ref[...] = whitened[0]
    second_ref[...] = whitened[1]


def whiten(records, available):
    stations, segments, samples = records.shape
    half = jax.ShapeDtypeStruct((2 * OWNERS, CHUNK, 2, segments, stations), jnp.bfloat16)
    half_spec = pl.BlockSpec((2 * OWNERS, CHUNK, 2, SEG_STEP, stations), lambda i: (0, 0, 0, i, 0))
    return pl.pallas_call(
        whiten_kernel,
        grid=(segments // SEG_STEP,),
        in_specs=[
            pl.BlockSpec((stations, SEG_STEP, samples), lambda i: (0, i, 0)),
            pl.BlockSpec((SEG_STEP, stations), lambda i: (i, 0)),
            pl.BlockSpec((samples, 2 * BINS), lambda i: (0, 0)),
        ],
        out_specs=[half_spec, half_spec],
        out_shape=[half, half],
        scratch_shapes=[
            pltpu.VMEM((2, stations * SEG_STEP, BINS), jnp.float32),
            pltpu.VMEM((2 * BINS * SEG_STEP, stations), jnp.float32),
        ],
        compiler_params=pltpu.CompilerParams(vmem_limit_bytes=60 * MIB),
        name="whiten",
    )(records, available.T, jnp.asarray(spectra_table()))


def rows_kernel(panel_ref, mine_ref):
    sources, _, depth, rows = panel_ref.shape
    panel = panel_ref[:, 0].reshape(sources // 2, 2, 2, depth // 2, rows)
    for core in range(2):
        part = panel[:, core]
        turned = jnp.stack([part[:, 1], -part[:, 0]], axis=1)
        base = 2 * rows * core
        mine_ref[0, base : base + rows] = part.reshape(-1, rows).T
        mine_ref[0, base + rows : base + 2 * rows] = turned.reshape(-1, rows).T


def rows_of(panel):
    sources, bins, depth, rows = panel.shape
    block = (1, 4 * rows, sources // 2 * depth)
    return pl.pallas_call(
        rows_kernel,
        grid=(bins,),
        in_specs=[pl.BlockSpec((sources, 1, depth, rows), lambda f: (0, f, 0, 0))],
        out_specs=pl.BlockSpec(block, lambda f: (f, 0, 0)),
        out_shape=pltpu.HBM((bins, *block[1:]), panel.dtype),
        compiler_params=pltpu.CompilerParams(vmem_limit_bytes=24 * MIB),
        name="rows",
    )(panel)


def spot_of(where, at, cols):
    return pl.ds(pl.multiple_of(where[at] * cols, cols), cols)


def gram_kernel(scale, chunks, placed, own, other, where, mine0_ref, mine1_ref, *refs):
    count, sets = len(chunks), len(placed)
    panels, sent, rest = refs[:count], refs[count : count + sets], refs[count + sets :]
    slots, place_slots, sems, place_sems = rest[-4:]
    out_ref, send_ref = rest[-5 - (own and other)], rest[-5]
    step, steps = pl.program_id(0), pl.num_programs(0)
    bins = mine0_ref.shape[0]
    rows, cols = mine0_ref.shape[1] // 4, 2 * panels[0].shape[3]
    slot, core = lax.rem(step, 2), where[count]
    received = [(which, at, chunk) for which, some in enumerate(placed) for at, chunk in enumerate(some)]

    def first_bin(owner, chunk, at):
        return owner * 2 * CHUNK + chunk * CHUNK + at * bins

    def writes(at, held):
        for block, chunk in enumerate(chunks):
            if own:
                spot = out_ref.at[:, pl.ds(first_bin(core, chunk, at), bins), :, spot_of(where, block, cols)]
                source = slots.at[held, block, core if other else 0]
                yield pltpu.make_async_copy(source, spot, sems.at[held, block, 0])
            if other:
                spot = send_ref.at[block, :, pl.ds(at * bins, bins)]
                source = slots.at[held, block, 1 - core if own else 0]
                yield pltpu.make_async_copy(source, spot, sems.at[held, block, 1])

    def places(at, held):
        for k, (_, _, chunk) in enumerate(received):
            spot = spot_of(where, count + 1 + k, cols)
            spot = out_ref.at[:, pl.ds(first_bin(1 - core, chunk, at), bins), :, spot]
            yield pltpu.make_async_copy(place_slots.at[held, k], spot, place_sems.at[held, k])

    @pl.when(step >= 2)
    def _():
        for copy in (*writes(step - 2, slot), *places(step - 2, slot)):
            copy.wait()

    for k, (which, at, _) in enumerate(received):
        place_slots[slot, k] = sent[which][at]
    for copy in places(step, slot):
        copy.start()
    for block, chunk in enumerate(chunks):
        mine_ref = mine1_ref if chunk else mine0_ref
        for f in range(bins):
            if own and other:
                mine = mine_ref[f]
            else:
                target = core if own else 1 - core
                mine = mine_ref[f, pl.ds(pl.multiple_of(target * 2 * rows, 2 * rows), 2 * rows), :]
            panel = panels[block][:, f].reshape(-1, 2, *panels[block].shape[2:])
            panel = jnp.concatenate([panel[:, side].reshape(-1, rows) for side in range(2)], axis=1)
            gram = jnp.dot(mine, panel, preferred_element_type=jnp.float32) * scale
            gram = gram.astype(jnp.bfloat16)
            for target in range(own + other):
                for part in range(2):
                    base = (2 * target + part) * rows
                    slots[slot, block, target, part, f] = gram[base : base + rows]
    for copy in writes(step, slot):
        copy.start()

    @pl.when(step == steps - 1)
    def _():
        for copy in (*writes(step - 1, 1 - slot), *places(step - 1, 1 - slot)):
            copy.wait()
        for copy in (*writes(step, slot), *places(step, slot)):
            copy.wait()


def far(value):
    return pltpu.with_memory_space_constraint(value, pltpu.HBM)


def sent_spec(results, step):
    block = (results.shape[0], 2, step, *results.shape[3:])
    return pl.BlockSpec(block, lambda f, w: (0, 0, f, 0, 0))


def gram(core, mine, blocks, shape, out, *sent, own=True, other=True):
    sources, bins, part, rows = blocks[0][3].shape
    depth, cols, step = sources // 2 * part, 2 * rows, 2
    count = len(blocks)
    chunks = [block[0] for block in blocks]
    received = [block for some, _ in sent for block in some]
    where = [block[1] for block in blocks] + [core] + [block[2] for block in received]
    held = [] if out is None else [out]
    used = [
        pl.BlockSpec((step, 4 * rows, depth), (lambda f, w: (f, 0, 0)) if chunk in chunks else (lambda f, w: (0, 0, 0)))
        for chunk in range(2)
    ]
    send = jax.ShapeDtypeStruct((count, 2, bins, rows, cols), jnp.bfloat16)
    spots = max(len(received), 1)
    return pl.pallas_call(
        functools.partial(
            gram_kernel, 2.0 / depth, chunks, [[block[0] for block in some] for some, _ in sent], own, other
        ),
        grid_spec=pltpu.PrefetchScalarGridSpec(
            num_scalar_prefetch=1,
            grid=(bins // step,),
            in_specs=used
            + [pl.BlockSpec((sources, step, part, rows), lambda f, w: (0, f, 0, 0))] * count
            + [sent_spec(results, step) for _, results in sent]
            + [pl.BlockSpec(memory_space=pl.ANY)] * len(held),
            out_specs=[pl.BlockSpec(memory_space=pl.ANY)] * (own + other),
            scratch_shapes=[
                pltpu.VMEM((2, count, own + other, 2, step, rows, cols), jnp.bfloat16),
                pltpu.VMEM((2, spots, 2, step, rows, cols), jnp.bfloat16),
                pltpu.SemaphoreType.DMA((2, count, 2)),
                pltpu.SemaphoreType.DMA((2, spots)),
            ],
        ),
        out_shape=[jax.ShapeDtypeStruct(shape, jnp.bfloat16)] * own + [send] * other,
        input_output_aliases={3 + count + len(sent): 0} if held else {},
        cost_estimate=pl.CostEstimate(
            flops=8 * count * bins * rows * depth * cols,
            bytes_accessed=2 * bins * (8 * rows * depth + count * (depth * cols + 4 * rows * cols)),
            transcendentals=0,
        ),
        compiler_params=pltpu.CompilerParams(vmem_limit_bytes=24 * MIB),
        name="gram",
    )(jnp.stack(where).astype(jnp.int32), *map(far, mine), *[block[3] for block in blocks], *[r for _, r in sent], *held)


def place_kernel(placed, where, *refs):
    sent, (out_ref, sems) = refs[: len(placed)], refs[-2:]
    step, count = pl.program_id(0), sum(map(len, placed))
    core, copies = where[count], []
    for which, chunks in enumerate(placed):
        bins, cols = sent[which].shape[2], sent[which].shape[4]
        for at, chunk in enumerate(chunks):
            first = (1 - core) * 2 * CHUNK + chunk * CHUNK + step * bins
            spot = out_ref.at[:, pl.ds(first, bins), :, spot_of(where, len(copies), cols)]
            copies.append(pltpu.make_async_copy(sent[which].at[at], spot, sems.at[len(copies)]))
    for copy in copies:
        copy.start()
    for copy in copies:
        copy.wait()


def place(core, out, *sent):
    received = [block for blocks, _ in sent for block in blocks]
    return pl.pallas_call(
        functools.partial(place_kernel, [[block[0] for block in blocks] for blocks, _ in sent]),
        grid_spec=pltpu.PrefetchScalarGridSpec(
            num_scalar_prefetch=1,
            grid=(CHUNK // 2,),
            in_specs=[sent_spec(results, 2) for _, results in sent] + [pl.BlockSpec(memory_space=pl.ANY)],
            out_specs=pl.BlockSpec(memory_space=pl.ANY),
            scratch_shapes=[pltpu.SemaphoreType.DMA((len(received),))],
        ),
        out_shape=jax.ShapeDtypeStruct(out.shape, out.dtype),
        input_output_aliases={1 + len(sent): 0},
        compiler_params=pltpu.CompilerParams(vmem_limit_bytes=24 * MIB),
        name="place",
    )(jnp.stack([block[2] for block in received] + [core]).astype(jnp.int32), *[r for _, r in sent], out)


def mirrored(step):
    return [
        (2 * x + core, (x + (1 - 2 * core) * step) % 4 * 2 + core) for x in range(4) for core in range(2)
    ]


def shards(records, available):
    stations = records.shape[0]
    x, yh, core = lax.axis_index("x"), lax.axis_index("yh"), lax.axis_index("core")
    fwd = lambda v: lax.ppermute(v, ("x", "core"), mirrored(1))
    bwd = lambda v: lax.ppermute(v, ("x", "core"), mirrored(-1))
    over = lambda v: lax.ppermute(v, "yh", [(0, 1), (1, 0)])
    swap = lambda v: lax.ppermute(v, "core", [(0, 1), (1, 0)])
    after = lambda value, *others: lax.optimization_barrier((value, *others))[0]

    def owned(chunk):
        got = lax.all_to_all(chunk, ("yl", "z", "core"), split_axis=0, concat_axis=0, tiled=True)
        return got.reshape(2 * OWNERS, CHUNK, -1, stations)

    def entry(chunk, dx, dy, panel):
        sign = 1 - 2 * core
        chips = [(x - way * dx) % 4 * 2 + (yh + dy) % 2 for way in (sign, -sign)]
        return chunk, *chips, panel

    shape = (2, 4 * CHUNK, stations, 16 * stations)
    first, second = whiten(records, available)
    pa = owned(first)
    na, ba = fwd(pa), bwd(pa)
    pb = owned(after(second, pa))
    ma = rows_of(pa)

    fa, nb, oa = fwd(after(na, pb)), fwd(after(pb, na)), over(after(pa, pb))
    blocks1 = [entry(0, 0, 0, pa), entry(0, 1, 0, na), entry(0, -1, 0, ba)]
    out, sent = gram(core, (ma, ma), blocks1, shape, None)
    mine = ma, rows_of(pb)

    bb, fb, ob = bwd(after(pb, fa, out)), fwd(after(nb, out)), over(after(pb, oa, fa))
    sent1 = blocks1, swap(sent)
    blocks2 = [entry(1, 0, 0, pb), entry(0, 2, 0, fa), entry(1, 1, 0, nb), entry(0, 0, 1, oa)]
    out, sent = gram(core, mine, blocks2, shape, out)

    boa, bob, noa = bwd(after(oa, bb, out)), bwd(after(ob, fb)), over(after(na, ob, bb))
    sent2 = blocks2, swap(sent)
    blocks3 = [entry(1, -1, 0, bb), entry(1, 2, 0, fb), entry(1, 0, 1, ob)]
    out, sent = gram(core, mine, blocks3, shape, out, sent1)

    nob, foa, fob = fwd(after(ob, boa, out)), fwd(after(noa, bob)), over(after(fb, noa, boa))
    sent3 = blocks3, swap(sent)
    blocks4 = [entry(0, -1, 1, boa), entry(1, -1, 1, bob), entry(0, 1, 1, noa)]
    out, sent = gram(core, mine, blocks4, shape, out, sent2)

    sent4 = blocks4, swap(sent)
    blocks5 = [entry(1, 1, 1, nob)]
    out, sent = gram(core, mine, blocks5, shape, out, sent3)

    sent5 = blocks5, swap(sent)
    blocks6 = [entry(0, 2, 1, after(foa, out)), entry(1, 2, 1, fob)]
    (sent,) = gram(core, mine, blocks6, shape, None, own=False)
    (out,) = gram(core, mine, blocks6, shape, out, sent4, other=False)
    return place(core, out, sent5, (blocks6, swap(sent)))


def solution(mesh):
    fine = Mesh(mesh.devices.reshape(4, 2, 2, 2, 4), ("x", "yh", "core", "yl", "z"))
    sta, freq = ("x", "yh", "core"), ("yl", "z")
    return jax.shard_map(
        shards,
        mesh=fine,
        in_specs=(P(sta, freq, None), P(sta, freq)),
        out_specs=P(None, freq, sta, None),
        check_vma=False,
    )
```

```python
import functools

import jax
import jax.numpy as jnp
import numpy as np
from jax import lax
from jax.experimental import pallas as pl
from jax.experimental.pallas import tpu as pltpu
from jax.sharding import Mesh, PartitionSpec as P

FFT_LEN = 512
BINS = 128
BAND_LO = 16
OWNERS = 8
CHUNK = 4
SEG_STEP = 8
MIB = 1024 * 1024


def spectra_table():
    sample = np.arange(FFT_LEN)
    bins = (BAND_LO + np.arange(BINS)).reshape(OWNERS, 2, 2, CHUNK).transpose(2, 0, 1, 3).reshape(-1)
    phase = (sample[:, None] * bins[None, :] % FFT_LEN) * (2.0 * np.pi / FFT_LEN)
    taper = 0.5 - 0.5 * np.cos(2.0 * np.pi * sample / FFT_LEN)
    table = np.stack([np.cos(phase), -np.sin(phase)], axis=2).reshape(FFT_LEN, 2 * BINS) * taper[:, None]
    high = table.astype(jnp.bfloat16)
    low = (table - high.astype(np.float64)).astype(jnp.bfloat16)
    return high, low


def whiten_kernel(records_ref, available_ref, high_ref, low_ref, first_ref, second_ref, rows_ref, turned_ref):
    stations, segs, samples = records_ref.shape
    flat = records_ref[...].reshape(stations * segs, samples)
    spectra = jnp.dot(flat, high_ref[...], preferred_element_type=jnp.float32)
    spectra += jnp.dot(flat, low_ref[...], preferred_element_type=jnp.float32)
    wide = spectra.shape[1]
    for part in range(2):
        rows_ref[part] = spectra[:, part * BINS : (part + 1) * BINS]
    for seg in range(segs):
        turned = jnp.concatenate(
            [rows_ref[part, pl.ds(seg, stations, stride=segs), :].T for part in range(2)], axis=0
        )
        power = jnp.sum(turned * turned, axis=0, keepdims=True) / BINS
        weight = available_ref[seg : seg + 1, :].astype(jnp.float32) / jnp.sqrt(power + 1e-05)
        turned_ref[pl.ds(seg, wide, stride=segs), :] = turned * weight
    whitened = turned_ref[...].reshape(2, 2 * OWNERS, CHUNK, 2, segs, stations).astype(jnp.bfloat16)
    first_ref[...] = whitened[0]
    second_ref[...] = whitened[1]


def whiten(records, available):
    stations, segments, samples = records.shape
    high, low = spectra_table()
    half = jax.ShapeDtypeStruct((2 * OWNERS, CHUNK, 2, segments, stations), jnp.bfloat16)
    half_spec = pl.BlockSpec((2 * OWNERS, CHUNK, 2, SEG_STEP, stations), lambda i: (0, 0, 0, i, 0))
    return pl.pallas_call(
        whiten_kernel,
        grid=(segments // SEG_STEP,),
        in_specs=[
            pl.BlockSpec((stations, SEG_STEP, samples), lambda i: (0, i, 0)),
            pl.BlockSpec((SEG_STEP, stations), lambda i: (i, 0)),
            pl.BlockSpec((samples, 2 * BINS), lambda i: (0, 0)),
            pl.BlockSpec((samples, 2 * BINS), lambda i: (0, 0)),
        ],
        out_specs=[half_spec, half_spec],
        out_shape=[half, half],
        scratch_shapes=[
            pltpu.VMEM((2, stations * SEG_STEP, BINS), jnp.float32),
            pltpu.VMEM((2 * BINS * SEG_STEP, stations), jnp.float32),
        ],
        compiler_params=pltpu.CompilerParams(vmem_limit_bytes=60 * MIB),
        name="whiten",
    )(records, available.T, jnp.asarray(high), jnp.asarray(low))


def rows_kernel(panel_ref, mine_ref):
    sources, _, depth, rows = panel_ref.shape
    panel = panel_ref[:, 0].reshape(sources // 2, 2, 2, depth // 2, rows)
    for core in range(2):
        part = panel[:, core]
        turned = jnp.stack([part[:, 1], -part[:, 0]], axis=1)
        base = 2 * rows * core
        mine_ref[0, base : base + rows] = part.reshape(-1, rows).T
        mine_ref[0, base + rows : base + 2 * rows] = turned.reshape(-1, rows).T


def rows_of(panel):
    sources, bins, depth, rows = panel.shape
    block = (1, 4 * rows, sources // 2 * depth)
    return pl.pallas_call(
        rows_kernel,
        grid=(bins,),
        in_specs=[pl.BlockSpec((sources, 1, depth, rows), lambda f: (0, f, 0, 0))],
        out_specs=pl.BlockSpec(block, lambda f: (f, 0, 0)),
        out_shape=pltpu.HBM((bins, *block[1:]), panel.dtype),
        compiler_params=pltpu.CompilerParams(vmem_limit_bytes=24 * MIB),
        name="rows",
    )(panel)


def spot_of(where, at, cols):
    return pl.ds(pl.multiple_of(where[at] * cols, cols), cols)


def gram_kernel(scale, chunks, placed, own, other, where, mine0_ref, mine1_ref, *refs):
    count, sets = len(chunks), len(placed)
    panels, sent, rest = refs[:count], refs[count : count + sets], refs[count + sets :]
    slots, place_slots, sems, place_sems = rest[-4:]
    out_ref, send_ref = rest[-5 - (own and other)], rest[-5]
    step, steps = pl.program_id(0), pl.num_programs(0)
    bins = mine0_ref.shape[0]
    rows, cols = mine0_ref.shape[1] // 4, 2 * panels[0].shape[3]
    slot, core = lax.rem(step, 2), where[count]
    received = [(which, at, chunk) for which, some in enumerate(placed) for at, chunk in enumerate(some)]

    def first_bin(owner, chunk, at):
        return owner * 2 * CHUNK + chunk * CHUNK + at * bins

    def writes(at, held):
        for block, chunk in enumerate(chunks):
            if own:
                spot = out_ref.at[:, pl.ds(first_bin(core, chunk, at), bins), :, spot_of(where, block, cols)]
                source = slots.at[held, block, core if other else 0]
                yield pltpu.make_async_copy(source, spot, sems.at[held, block, 0])
            if other:
                spot = send_ref.at[block, :, pl.ds(at * bins, bins)]
                source = slots.at[held, block, 1 - core if own else 0]
                yield pltpu.make_async_copy(source, spot, sems.at[held, block, 1])

    def places(at, held):
        for k, (_, _, chunk) in enumerate(received):
            spot = spot_of(where, count + 1 + k, cols)
            spot = out_ref.at[:, pl.ds(first_bin(1 - core, chunk, at), bins), :, spot]
            yield pltpu.make_async_copy(place_slots.at[held, k], spot, place_sems.at[held, k])

    @pl.when(step >= 2)
    def _():
        for copy in (*writes(step - 2, slot), *places(step - 2, slot)):
            copy.wait()

    for k, (which, at, _) in enumerate(received):
        place_slots[slot, k] = sent[which][at]
    for copy in places(step, slot):
        copy.start()
    for block, chunk in enumerate(chunks):
        mine_ref = mine1_ref if chunk else mine0_ref
        for f in range(bins):
            if own and other:
                mine = mine_ref[f]
            else:
                target = core if own else 1 - core
                mine = mine_ref[f, pl.ds(pl.multiple_of(target * 2 * rows, 2 * rows), 2 * rows), :]
            panel = panels[block][:, f].reshape(-1, 2, *panels[block].shape[2:])
            panel = jnp.concatenate([panel[:, side].reshape(-1, rows) for side in range(2)], axis=1)
            gram = jnp.dot(mine, panel, preferred_element_type=jnp.float32) * scale
            gram = gram.astype(jnp.bfloat16)
            for target in range(own + other):
                for part in range(2):
                    base = (2 * target + part) * rows
                    slots[slot, block, target, part, f] = gram[base : base + rows]
    for copy in writes(step, slot):
        copy.start()

    @pl.when(step == steps - 1)
    def _():
        for copy in (*writes(step - 1, 1 - slot), *places(step - 1, 1 - slot)):
            copy.wait()
        for copy in (*writes(step, slot), *places(step, slot)):
            copy.wait()


def far(value):
    return pltpu.with_memory_space_constraint(value, pltpu.HBM)


def sent_spec(results, step):
    block = (results.shape[0], 2, step, *results.shape[3:])
    return pl.BlockSpec(block, lambda f, w: (0, 0, f, 0, 0))


def gram(core, mine, blocks, shape, out, *sent, own=True, other=True):
    sources, bins, part, rows = blocks[0][3].shape
    depth, cols, step = sources // 2 * part, 2 * rows, 2
    count = len(blocks)
    chunks = [block[0] for block in blocks]
    received = [block for some, _ in sent for block in some]
    where = [block[1] for block in blocks] + [core] + [block[2] for block in received]
    held = [] if out is None else [out]
    used = [
        pl.BlockSpec((step, 4 * rows, depth), (lambda f, w: (f, 0, 0)) if chunk in chunks else (lambda f, w: (0, 0, 0)))
        for chunk in range(2)
    ]
    send = jax.ShapeDtypeStruct((count, 2, bins, rows, cols), jnp.bfloat16)
    spots = max(len(received), 1)
    return pl.pallas_call(
        functools.partial(
            gram_kernel, 2.0 / depth, chunks, [[block[0] for block in some] for some, _ in sent], own, other
        ),
        grid_spec=pltpu.PrefetchScalarGridSpec(
            num_scalar_prefetch=1,
            grid=(bins // step,),
            in_specs=used
            + [pl.BlockSpec((sources, step, part, rows), lambda f, w: (0, f, 0, 0))] * count
            + [sent_spec(results, step) for _, results in sent]
            + [pl.BlockSpec(memory_space=pl.ANY)] * len(held),
            out_specs=[pl.BlockSpec(memory_space=pl.ANY)] * (own + other),
            scratch_shapes=[
                pltpu.VMEM((2, count, own + other, 2, step, rows, cols), jnp.bfloat16),
                pltpu.VMEM((2, spots, 2, step, rows, cols), jnp.bfloat16),
                pltpu.SemaphoreType.DMA((2, count, 2)),
                pltpu.SemaphoreType.DMA((2, spots)),
            ],
        ),
        out_shape=[jax.ShapeDtypeStruct(shape, jnp.bfloat16)] * own + [send] * other,
        input_output_aliases={3 + count + len(sent): 0} if held else {},
        cost_estimate=pl.CostEstimate(
            flops=8 * count * bins * rows * depth * cols,
            bytes_accessed=2 * bins * (8 * rows * depth + count * (depth * cols + 4 * rows * cols)),
            transcendentals=0,
        ),
        compiler_params=pltpu.CompilerParams(vmem_limit_bytes=24 * MIB),
        name="gram",
    )(jnp.stack(where).astype(jnp.int32), *map(far, mine), *[block[3] for block in blocks], *[r for _, r in sent], *held)


def place_kernel(placed, where, *refs):
    sent, (out_ref, sems) = refs[: len(placed)], refs[-2:]
    step, count = pl.program_id(0), sum(map(len, placed))
    core, copies = where[count], []
    for which, chunks in enumerate(placed):
        bins, cols = sent[which].shape[2], sent[which].shape[4]
        for at, chunk in enumerate(chunks):
            first = (1 - core) * 2 * CHUNK + chunk * CHUNK + step * bins
            spot = out_ref.at[:, pl.ds(first, bins), :, spot_of(where, len(copies), cols)]
            copies.append(pltpu.make_async_copy(sent[which].at[at], spot, sems.at[len(copies)]))
    for copy in copies:
        copy.start()
    for copy in copies:
        copy.wait()


def place(core, out, *sent):
    received = [block for blocks, _ in sent for block in blocks]
    return pl.pallas_call(
        functools.partial(place_kernel, [[block[0] for block in blocks] for blocks, _ in sent]),
        grid_spec=pltpu.PrefetchScalarGridSpec(
            num_scalar_prefetch=1,
            grid=(CHUNK // 2,),
            in_specs=[sent_spec(results, 2) for _, results in sent] + [pl.BlockSpec(memory_space=pl.ANY)],
            out_specs=pl.BlockSpec(memory_space=pl.ANY),
            scratch_shapes=[pltpu.SemaphoreType.DMA((len(received),))],
        ),
        out_shape=jax.ShapeDtypeStruct(out.shape, out.dtype),
        input_output_aliases={1 + len(sent): 0},
        compiler_params=pltpu.CompilerParams(vmem_limit_bytes=24 * MIB),
        name="place",
    )(jnp.stack([block[2] for block in received] + [core]).astype(jnp.int32), *[r for _, r in sent], out)


def mirrored(step):
    return [
        (2 * x + core, (x + (1 - 2 * core) * step) % 4 * 2 + core) for x in range(4) for core in range(2)
    ]


def shards(records, available):
    stations = records.shape[0]
    x, yh, core = lax.axis_index("x"), lax.axis_index("yh"), lax.axis_index("core")
    fwd = lambda v: lax.ppermute(v, ("x", "core"), mirrored(1))
    bwd = lambda v: lax.ppermute(v, ("x", "core"), mirrored(-1))
    over = lambda v: lax.ppermute(v, "yh", [(0, 1), (1, 0)])
    swap = lambda v: lax.ppermute(v, "core", [(0, 1), (1, 0)])
    after = lambda value, *others: lax.optimization_barrier((value, *others))[0]

    def owned(chunk):
        got = lax.all_to_all(chunk, ("yl", "z", "core"), split_axis=0, concat_axis=0, tiled=True)
        return got.reshape(2 * OWNERS, CHUNK, -1, stations)

    def entry(chunk, dx, dy, panel):
        sign = 1 - 2 * core
        chips = [(x - way * dx) % 4 * 2 + (yh + dy) % 2 for way in (sign, -sign)]
        return chunk, *chips, panel

    shape = (2, 4 * CHUNK, stations, 16 * stations)
    first, second = whiten(records, available)
    pa = owned(first)
    na, ba = fwd(pa), bwd(pa)
    pb = owned(after(second, pa))
    ma = rows_of(pa)

    fa, nb, oa = fwd(after(na, pb)), fwd(after(pb, na)), over(after(pa, pb))
    blocks1 = [entry(0, 0, 0, pa), entry(0, 1, 0, na), entry(0, -1, 0, ba)]
    out, sent = gram(core, (ma, ma), blocks1, shape, None)
    mine = ma, rows_of(pb)

    bb, fb, ob = bwd(after(pb, fa, out)), fwd(after(nb, oa, out)), over(after(pb, oa))
    sent1 = blocks1, swap(sent)
    blocks2 = [entry(1, 0, 0, after(pb, bb)), entry(0, 2, 0, fa), entry(1, 1, 0, nb), entry(0, 0, 1, oa)]
    out, sent = gram(core, mine, blocks2, shape, out)

    boa, bob, noa = bwd(after(oa, bb)), bwd(after(ob, fb)), over(after(na, ob, bb))
    sent2 = blocks2, swap(sent)
    blocks3 = [entry(1, -1, 0, bb), entry(1, 2, 0, fb), entry(1, 0, 1, ob)]
    out, sent = gram(core, mine, blocks3, shape, out, sent1)

    nob, foa, fob = fwd(after(ob, boa, out)), fwd(after(noa, bob)), over(after(fb, noa))
    sent3 = blocks3, swap(sent)
    blocks4 = [entry(0, -1, 1, boa), entry(1, -1, 1, bob), entry(0, 1, 1, noa)]
    out, sent = gram(core, mine, blocks4, shape, out)

    sent4 = blocks4, swap(sent)
    blocks5 = [entry(1, 1, 1, nob)]
    out, sent = gram(core, mine, blocks5, shape, out, sent2)

    sent5 = blocks5, swap(sent)
    blocks6 = [entry(0, 2, 1, after(foa, out)), entry(1, 2, 1, fob)]
    (sent,) = gram(core, mine, blocks6, shape, None, own=False)
    (out,) = gram(core, mine, blocks6, shape, out, sent3, sent4, other=False)
    return place(core, out, sent5, (blocks6, swap(sent)))


def solution(mesh):
    fine = Mesh(mesh.devices.reshape(4, 2, 2, 2, 4), ("x", "yh", "core", "yl", "z"))
    sta, freq = ("x", "yh", "core"), ("yl", "z")
    return jax.shard_map(
        shards,
        mesh=fine,
        in_specs=(P(sta, freq, None), P(sta, freq)),
        out_specs=P(None, freq, sta, None),
        check_vma=False,
    )
```

```python
import functools

import jax
import jax.numpy as jnp
import numpy as np
from jax import lax
from jax.experimental import pallas as pl
from jax.experimental.pallas import tpu as pltpu
from jax.sharding import Mesh, PartitionSpec as P

FFT_LEN = 512
BINS = 128
BAND_LO = 16
OWNERS = 8
CHUNK = 4
SEG_STEP = 8
MIB = 1024 * 1024


def spectra_table():
    sample = np.arange(FFT_LEN)
    bins = (BAND_LO + np.arange(BINS)).reshape(OWNERS, 2, 2, CHUNK).transpose(2, 0, 1, 3).reshape(-1)
    phase = (sample[:, None] * bins[None, :] % FFT_LEN) * (2.0 * np.pi / FFT_LEN)
    taper = 0.5 - 0.5 * np.cos(2.0 * np.pi * sample / FFT_LEN)
    table = np.stack([np.cos(phase), -np.sin(phase)], axis=2).reshape(FFT_LEN, 2 * BINS) * taper[:, None]
    high = table.astype(jnp.bfloat16)
    low = (table - high.astype(np.float64)).astype(jnp.bfloat16)
    return high, low


def whiten_kernel(records_ref, available_ref, high_ref, low_ref, first_ref, second_ref, rows_ref, turned_ref):
    stations, segs, samples = records_ref.shape
    flat = records_ref[...].reshape(stations * segs, samples)
    spectra = jnp.dot(flat, high_ref[...], preferred_element_type=jnp.float32)
    spectra += jnp.dot(flat, low_ref[...], preferred_element_type=jnp.float32)
    wide = spectra.shape[1]
    for part in range(2):
        rows_ref[part] = spectra[:, part * BINS : (part + 1) * BINS]
    for seg in range(segs):
        turned = jnp.concatenate(
            [rows_ref[part, pl.ds(seg, stations, stride=segs), :].T for part in range(2)], axis=0
        )
        power = jnp.sum(turned * turned, axis=0, keepdims=True) / BINS
        weight = available_ref[seg : seg + 1, :].astype(jnp.float32) / jnp.sqrt(power + 1e-05)
        turned_ref[pl.ds(seg, wide, stride=segs), :] = turned * weight
    whitened = turned_ref[...].reshape(2, 2 * OWNERS, CHUNK, 2, segs, stations).astype(jnp.bfloat16)
    first_ref[...] = whitened[0]
    second_ref[...] = whitened[1]


def whiten(records, available):
    stations, segments, samples = records.shape
    high, low = spectra_table()
    half = jax.ShapeDtypeStruct((2 * OWNERS, CHUNK, 2, segments, stations), jnp.bfloat16)
    half_spec = pl.BlockSpec((2 * OWNERS, CHUNK, 2, SEG_STEP, stations), lambda i: (0, 0, 0, i, 0))
    return pl.pallas_call(
        whiten_kernel,
        grid=(segments // SEG_STEP,),
        in_specs=[
            pl.BlockSpec((stations, SEG_STEP, samples), lambda i: (0, i, 0)),
            pl.BlockSpec((SEG_STEP, stations), lambda i: (i, 0)),
            pl.BlockSpec((samples, 2 * BINS), lambda i: (0, 0)),
            pl.BlockSpec((samples, 2 * BINS), lambda i: (0, 0)),
        ],
        out_specs=[half_spec, half_spec],
        out_shape=[half, half],
        scratch_shapes=[
            pltpu.VMEM((2, stations * SEG_STEP, BINS), jnp.float32),
            pltpu.VMEM((2 * BINS * SEG_STEP, stations), jnp.float32),
        ],
        compiler_params=pltpu.CompilerParams(vmem_limit_bytes=60 * MIB),
        name="whiten",
    )(records, available.T, jnp.asarray(high), jnp.asarray(low))


def rows_kernel(panel_ref, mine_ref):
    sources, _, depth, rows = panel_ref.shape
    panel = panel_ref[:, 0].reshape(sources // 2, 2, 2, depth // 2, rows)
    for core in range(2):
        part = panel[:, core]
        turned = jnp.stack([part[:, 1], -part[:, 0]], axis=1)
        base = 2 * rows * core
        mine_ref[0, base : base + rows] = part.reshape(-1, rows).T
        mine_ref[0, base + rows : base + 2 * rows] = turned.reshape(-1, rows).T


def rows_of(panel):
    sources, bins, depth, rows = panel.shape
    block = (1, 4 * rows, sources // 2 * depth)
    return pl.pallas_call(
        rows_kernel,
        grid=(bins,),
        in_specs=[pl.BlockSpec((sources, 1, depth, rows), lambda f: (0, f, 0, 0))],
        out_specs=pl.BlockSpec(block, lambda f: (f, 0, 0)),
        out_shape=pltpu.HBM((bins, *block[1:]), panel.dtype),
        compiler_params=pltpu.CompilerParams(vmem_limit_bytes=24 * MIB),
        name="rows",
    )(panel)


def spot_of(where, at, cols):
    return pl.ds(pl.multiple_of(where[at] * cols, cols), cols)


def gram_kernel(scale, chunks, placed, own, other, where, mine0_ref, mine1_ref, *refs):
    count, sets = len(chunks), len(placed)
    panels, sent, rest = refs[:count], refs[count : count + sets], refs[count + sets :]
    slots, place_slots, sems, place_sems = rest[-4:]
    out_ref, send_ref = rest[-5 - (own and other)], rest[-5]
    step, steps = pl.program_id(0), pl.num_programs(0)
    bins = mine0_ref.shape[0]
    rows, cols = mine0_ref.shape[1] // 4, 2 * panels[0].shape[3]
    slot, core = lax.rem(step, 2), where[count]
    received = [(which, at, chunk) for which, some in enumerate(placed) for at, chunk in enumerate(some)]

    def first_bin(owner, chunk, at):
        return owner * 2 * CHUNK + chunk * CHUNK + at * bins

    def writes(at, held):
        for block, chunk in enumerate(chunks):
            if own:
                spot = out_ref.at[:, pl.ds(first_bin(core, chunk, at), bins), :, spot_of(where, block, cols)]
                source = slots.at[held, block, core if other else 0]
                yield pltpu.make_async_copy(source, spot, sems.at[held, block, 0])
            if other:
                spot = send_ref.at[block, :, pl.ds(at * bins, bins)]
                source = slots.at[held, block, 1 - core if own else 0]
                yield pltpu.make_async_copy(source, spot, sems.at[held, block, 1])

    def places(at, held):
        for k, (_, _, chunk) in enumerate(received):
            spot = spot_of(where, count + 1 + k, cols)
            spot = out_ref.at[:, pl.ds(first_bin(1 - core, chunk, at), bins), :, spot]
            yield pltpu.make_async_copy(place_slots.at[held, k], spot, place_sems.at[held, k])

    @pl.when(step >= 2)
    def _():
        for copy in (*writes(step - 2, slot), *places(step - 2, slot)):
            copy.wait()

    for k, (which, at, _) in enumerate(received):
        place_slots[slot, k] = sent[which][at]
    for copy in places(step, slot):
        copy.start()
    for block, chunk in enumerate(chunks):
        mine_ref = mine1_ref if chunk else mine0_ref
        for f in range(bins):
            if own and other:
                mine = mine_ref[f]
            else:
                target = core if own else 1 - core
                mine = mine_ref[f, pl.ds(pl.multiple_of(target * 2 * rows, 2 * rows), 2 * rows), :]
            panel = panels[block][:, f].reshape(-1, 2, *panels[block].shape[2:])
            panel = jnp.concatenate([panel[:, side].reshape(-1, rows) for side in range(2)], axis=1)
            gram = jnp.dot(mine, panel, preferred_element_type=jnp.float32) * scale
            gram = gram.astype(jnp.bfloat16)
            for target in range(own + other):
                for part in range(2):
                    base = (2 * target + part) * rows
                    slots[slot, block, target, part, f] = gram[base : base + rows]
    for copy in writes(step, slot):
        copy.start()

    @pl.when(step == steps - 1)
    def _():
        for copy in (*writes(step - 1, 1 - slot), *places(step - 1, 1 - slot)):
            copy.wait()
        for copy in (*writes(step, slot), *places(step, slot)):
            copy.wait()


def far(value):
    return pltpu.with_memory_space_constraint(value, pltpu.HBM)


def sent_spec(results, step):
    block = (results.shape[0], 2, step, *results.shape[3:])
    return pl.BlockSpec(block, lambda f, w: (0, 0, f, 0, 0))


def gram(core, mine, blocks, shape, out, *sent, own=True, other=True):
    sources, bins, part, rows = blocks[0][3].shape
    depth, cols, step = sources // 2 * part, 2 * rows, 2
    count = len(blocks)
    chunks = [block[0] for block in blocks]
    received = [block for some, _ in sent for block in some]
    where = [block[1] for block in blocks] + [core] + [block[2] for block in received]
    held = [] if out is None else [out]
    used = [
        pl.BlockSpec((step, 4 * rows, depth), (lambda f, w: (f, 0, 0)) if chunk in chunks else (lambda f, w: (0, 0, 0)))
        for chunk in range(2)
    ]
    send = jax.ShapeDtypeStruct((count, 2, bins, rows, cols), jnp.bfloat16)
    spots = max(len(received), 1)
    return pl.pallas_call(
        functools.partial(
            gram_kernel, 2.0 / depth, chunks, [[block[0] for block in some] for some, _ in sent], own, other
        ),
        grid_spec=pltpu.PrefetchScalarGridSpec(
            num_scalar_prefetch=1,
            grid=(bins // step,),
            in_specs=used
            + [pl.BlockSpec((sources, step, part, rows), lambda f, w: (0, f, 0, 0))] * count
            + [sent_spec(results, step) for _, results in sent]
            + [pl.BlockSpec(memory_space=pl.ANY)] * len(held),
            out_specs=[pl.BlockSpec(memory_space=pl.ANY)] * (own + other),
            scratch_shapes=[
                pltpu.VMEM((2, count, own + other, 2, step, rows, cols), jnp.bfloat16),
                pltpu.VMEM((2, spots, 2, step, rows, cols), jnp.bfloat16),
                pltpu.SemaphoreType.DMA((2, count, 2)),
                pltpu.SemaphoreType.DMA((2, spots)),
            ],
        ),
        out_shape=[jax.ShapeDtypeStruct(shape, jnp.bfloat16)] * own + [send] * other,
        input_output_aliases={3 + count + len(sent): 0} if held else {},
        cost_estimate=pl.CostEstimate(
            flops=8 * count * bins * rows * depth * cols,
            bytes_accessed=2 * bins * (8 * rows * depth + count * (depth * cols + 4 * rows * cols)),
            transcendentals=0,
        ),
        compiler_params=pltpu.CompilerParams(vmem_limit_bytes=24 * MIB),
        name="gram",
    )(jnp.stack(where).astype(jnp.int32), *map(far, mine), *[block[3] for block in blocks], *[r for _, r in sent], *held)


def place_kernel(placed, where, *refs):
    sent, (out_ref, sems) = refs[: len(placed)], refs[-2:]
    step, count = pl.program_id(0), sum(map(len, placed))
    core, copies = where[count], []
    for which, chunks in enumerate(placed):
        bins, cols = sent[which].shape[2], sent[which].shape[4]
        for at, chunk in enumerate(chunks):
            first = (1 - core) * 2 * CHUNK + chunk * CHUNK + step * bins
            spot = out_ref.at[:, pl.ds(first, bins), :, spot_of(where, len(copies), cols)]
            copies.append(pltpu.make_async_copy(sent[which].at[at], spot, sems.at[len(copies)]))
    for copy in copies:
        copy.start()
    for copy in copies:
        copy.wait()


def place(core, out, *sent):
    received = [block for blocks, _ in sent for block in blocks]
    return pl.pallas_call(
        functools.partial(place_kernel, [[block[0] for block in blocks] for blocks, _ in sent]),
        grid_spec=pltpu.PrefetchScalarGridSpec(
            num_scalar_prefetch=1,
            grid=(CHUNK // 2,),
            in_specs=[sent_spec(results, 2) for _, results in sent] + [pl.BlockSpec(memory_space=pl.ANY)],
            out_specs=pl.BlockSpec(memory_space=pl.ANY),
            scratch_shapes=[pltpu.SemaphoreType.DMA((len(received),))],
        ),
        out_shape=jax.ShapeDtypeStruct(out.shape, out.dtype),
        input_output_aliases={1 + len(sent): 0},
        compiler_params=pltpu.CompilerParams(vmem_limit_bytes=24 * MIB),
        name="place",
    )(jnp.stack([block[2] for block in received] + [core]).astype(jnp.int32), *[r for _, r in sent], out)


def mirrored(step):
    return [
        (2 * x + core, (x + (1 - 2 * core) * step) % 4 * 2 + core) for x in range(4) for core in range(2)
    ]


def shards(records, available):
    stations = records.shape[0]
    x, yh, core = lax.axis_index("x"), lax.axis_index("yh"), lax.axis_index("core")
    fwd = lambda v: lax.ppermute(v, ("x", "core"), mirrored(1))
    bwd = lambda v: lax.ppermute(v, ("x", "core"), mirrored(-1))
    over = lambda v: lax.ppermute(v, "yh", [(0, 1), (1, 0)])
    swap = lambda v: lax.ppermute(v, "core", [(0, 1), (1, 0)])
    after = lambda value, *others: lax.optimization_barrier((value, *others))[0]

    def owned(chunk):
        got = lax.all_to_all(chunk, ("yl", "z", "core"), split_axis=0, concat_axis=0, tiled=True)
        return got.reshape(2 * OWNERS, CHUNK, -1, stations)

    def entry(chunk, dx, dy, panel):
        sign = 1 - 2 * core
        chips = [(x - way * dx) % 4 * 2 + (yh + dy) % 2 for way in (sign, -sign)]
        return chunk, *chips, panel

    shape = (2, 4 * CHUNK, stations, 16 * stations)
    first, second = whiten(records, available)
    pa = owned(first)
    na, ba = fwd(pa), bwd(pa)
    pb = owned(after(second, pa))
    ma = rows_of(pa)

    fa, nb, oa = fwd(after(na, pb)), fwd(after(pb, na)), over(after(pa, pb))
    blocks1 = [entry(0, 0, 0, pa), entry(0, 1, 0, na), entry(0, -1, 0, ba)]
    out, sent = gram(core, (ma, ma), blocks1, shape, None)
    mine = ma, rows_of(pb)

    bb, fb, ob = bwd(after(pb, fa, out)), fwd(after(nb, oa, out)), over(after(pb, oa))
    sent1 = blocks1, swap(sent)
    blocks2 = [entry(1, 0, 0, after(pb, bb)), entry(0, 2, 0, fa), entry(1, 1, 0, nb), entry(0, 0, 1, oa)]
    out, sent = gram(core, mine, blocks2, shape, out)

    boa, bob, noa = bwd(after(oa, bb)), bwd(after(ob, fb)), over(after(na, ob, bb))
    sent2 = blocks2, swap(sent)
    blocks3 = [entry(1, -1, 0, bb), entry(1, 2, 0, fb), entry(1, 0, 1, ob)]
    out, sent = gram(core, mine, blocks3, shape, out, sent1)

    nob, foa, fob = fwd(after(ob, boa, out)), fwd(after(noa, bob)), over(after(fb, noa))
    sent3 = blocks3, swap(sent)
    blocks4 = [entry(0, -1, 1, boa), entry(1, -1, 1, bob), entry(0, 1, 1, noa)]
    out, sent = gram(core, mine, blocks4, shape, out)

    sent4 = blocks4, swap(sent)
    blocks5 = [entry(1, 1, 1, nob)]
    out, sent = gram(core, mine, blocks5, shape, out, sent2, sent3)

    sent5 = blocks5, swap(sent)
    blocks6 = [entry(0, 2, 1, after(foa, out)), entry(1, 2, 1, fob)]
    (sent,) = gram(core, mine, blocks6, shape, None, own=False)
    (out,) = gram(core, mine, blocks6, shape, out, sent4, other=False)
    return place(core, out, sent5, (blocks6, swap(sent)))


def solution(mesh):
    fine = Mesh(mesh.devices.reshape(4, 2, 2, 2, 4), ("x", "yh", "core", "yl", "z"))
    sta, freq = ("x", "yh", "core"), ("yl", "z")
    return jax.shard_map(
        shards,
        mesh=fine,
        in_specs=(P(sta, freq, None), P(sta, freq)),
        out_specs=P(None, freq, sta, None),
        check_vma=False,
    )
```
